32 devices in a mesh: dp: 16 (over z, y, core), tensor: 2 (over x).
Axes of the slice: x: 2, y: 2, z: 4, core: 2. Of those that a mesh axis runs over, the one named last changes fastest.
Arguments:
- block_input: bfloat16 [2048, 1024], P('dp'), may hold values from -6 to 6
- output_grad: bfloat16 [2048, 1024], P('dp'), may hold values from -6 to 6
- attn_gain: float32 [1024], replicated, may hold values from 0.5 to 1.5
- w_query: bfloat16 [1024, 1024], P(None, 'tensor'), may hold values from -0.1875 to 0.1875
- w_key: bfloat16 [1024, 1024], P(None, 'tensor'), may hold values from -0.1875 to 0.1875
- w_value: bfloat16 [1024, 2048], P(None, 'tensor'), may hold values from -0.1875 to 0.1875
- conv_query: float32 [4, 1024], P(None, 'tensor'), may hold values from -3 to 3
- conv_key: float32 [4, 1024], P(None, 'tensor'), may hold values from -3 to 3
- conv_value: float32 [4, 2048], P(None, 'tensor'), may hold values from -3 to 3
- w_beta: bfloat16 [1024, 8], P(None, 'tensor'), may hold values from -0.1875 to 0.1875
- w_alpha: bfloat16 [1024, 8], P(None, 'tensor'), may hold values from -0.1875 to 0.1875
- a_log: float32 [8], P('tensor'), may hold values from -3 to 1.5
- dt_bias: float32 [8], P('tensor'), may hold values from -4 to 0
- w_gate_out: bfloat16 [1024, 2048], P(None, 'tensor'), may hold values from -0.1875 to 0.1875
- out_gain: float32 [256], replicated, may hold values from 0.5 to 1.5
- w_out: bfloat16 [2048, 1024], P('tensor'), may hold values from -0.25 to 0.25
- ffn_gain: float32 [1024], replicated, may hold values from 0.5 to 1.5
- w_gate: bfloat16 [1024, 2816], P(None, 'tensor'), may hold values from -0.1875 to 0.1875
- w_up: bfloat16 [1024, 2816], P(None, 'tensor'), may hold values from -0.1875 to 0.1875
- w_down: bfloat16 [2816, 1024], P('tensor'), may hold values from -0.109375 to 0.109375
Outputs:
- block_output: float32 [2048, 1024], P('dp')
- input_grad: float32 [2048, 1024], P('dp')
- grad_attn_gain: float32 [1024], P('dp')
- grad_w_query: float32 [1024, 1024], P('dp', 'tensor')
- grad_w_key: float32 [1024, 1024], P('dp', 'tensor')
- grad_w_value: float32 [1024, 2048], P('dp', 'tensor')
- grad_conv_query: float32 [4, 1024], P(None, 'tensor')
- grad_conv_key: float32 [4, 1024], P(None, 'tensor')
- grad_conv_value: float32 [4, 2048], P(None, 'tensor')
- grad_w_beta: float32 [1024, 8], P('dp', 'tensor')
- grad_w_alpha: float32 [1024, 8], P('dp', 'tensor')
- grad_a_log: float32 [8], P('tensor')
- grad_dt_bias: float32 [8], P('tensor')
- grad_w_gate_out: float32 [1024, 2048], P('dp', 'tensor')
- grad_out_gain: float32 [256], replicated
- grad_w_out: float32 [2048, 1024], P('tensor', 'dp')
- grad_ffn_gain: float32 [1024], P('dp')
- grad_w_gate: float32 [1024, 2816], P('dp', 'tensor')
- grad_w_up: float32 [1024, 2816], P('dp', 'tensor')
- grad_w_down: float32 [2816, 1024], P('tensor', 'dp')
The draws below stay inside these ranges and needn't reach their ends.
All inputs are finite; a program needn't handle non-finite values.
Results may differ from the reference program's by a relative error of at most 0.029.
Values may be sent and summed in bfloat16 or wider, within the bound.
No kernel may reach another device: no remote copies, remote signals or barrier semaphores. Data moves between devices by JAX's collectives and lax.ppermute only.
A program may use at most 192 MiB of HBM per device.

```python
import jax
import jax.numpy as jnp
from jax import lax

D = 1024
HEADS = 8
DK = 128
DV = 256
FF = 2816
KW = 4
GROUP = 64
TOKENS = 2048


def spiked(values, rng, source, target, parts, factor):
    owner, partner = [(jnp.arange(values.shape[dim]) // (values.shape[dim] // parts)).reshape([-1 if axis == dim else 1 for axis in range(values.ndim)]) for dim in (source, target)]
    chosen = jax.random.permutation(rng, parts)[partner]
    strong = (owner == chosen) | (owner == (partner + parts // 2) % parts)
    return jnp.where(strong, factor * values, values)


def level_of(own_key, extent, cuts, smallest, high):
    def one(axis_at, shards_of):
        draws = jax.random.uniform(jax.random.fold_in(jax.random.fold_in(own_key, 6), axis_at), (shards_of,), jnp.float32, smallest / len(cuts), high / len(cuts))
        return jnp.repeat(jnp.exp(draws), extent[axis_at] // shards_of).reshape((-1,) + (1,) * (len(extent) - axis_at - 1))

    loudness = one(*cuts[0])
    for cut in cuts[1:]:
        loudness = loudness * one(*cut)
    return loudness


def noise(stream_key, extent, scale, bound, cuts=(), held_as=jnp.bfloat16):
    loudness = level_of(stream_key, extent, cuts, -0.22, 0.18) if cuts else 1.0
    array = jax.random.normal(stream_key, extent, jnp.float32) * scale * loudness
    return jnp.minimum(jnp.maximum(array, -bound), bound).astype(held_as)


def bell_draw_with(rng, dims, scale, bound, shards, heavy, held_as=jnp.bfloat16):
    array = scale * jax.random.normal(rng, dims, jnp.float32)
    if shards:
        array = array * level_of(rng, dims, shards, -0.22, 0.18)
    return jnp.clip(spiked(array, jax.random.fold_in(rng, 3), *heavy), -bound, bound).astype(held_as)


def setup_inputs(seed: int = 0) -> dict:
    seeds = jax.random.split(jax.random.key(seed), 21)
    block_input = bell_draw_with(seeds[0], (TOKENS, D), 1.0, 6.0, ((0, 16),), (0, 1, 16, 2.0))
    output_grad = bell_draw_with(seeds[1], (TOKENS, D), 1.0, 6.0, ((0, 16),), (0, 1, 16, 2.0))
    attn_gain = jnp.clip(1.0 + 0.1 * jax.random.normal(seeds[2], (D,), jnp.float32), 0.5, 1.5)
    w_query = noise(seeds[3], (D, HEADS * DK), D ** -0.5, 0.1875, ((1, 2),))
    w_key = noise(seeds[4], (D, HEADS * DK), D ** -0.5, 0.1875, ((1, 2),))
    w_value = noise(seeds[5], (D, HEADS * DV), D ** -0.5, 0.1875, ((1, 2),))
    conv_query = noise(seeds[6], (KW, HEADS * DK), KW ** -0.5, 3.0, ((1, 2),), jnp.float32)
    conv_key = noise(seeds[7], (KW, HEADS * DK), KW ** -0.5, 3.0, ((1, 2),), jnp.float32)
    conv_value = noise(seeds[8], (KW, HEADS * DV), KW ** -0.5, 3.0, ((1, 2),), jnp.float32)
    w_beta = noise(seeds[9], (D, HEADS), D ** -0.5, 0.1875, ((1, 2),))
    w_alpha = noise(seeds[10], (D, HEADS), D ** -0.5, 0.1875, ((1, 2),))
    a_log = jnp.clip(-3.0 + 4.5 * jax.random.uniform(seeds[11], (HEADS,), jnp.float32) ** level_of(seeds[11], (HEADS,), ((0, 2),), -0.2, 0.2), -3.0, 1.5)
    dt_bias = jnp.clip(-4.0 + 4.0 * jax.random.uniform(seeds[12], (HEADS,), jnp.float32) ** level_of(seeds[12], (HEADS,), ((0, 2),), -0.2, 0.2), -4.0, 0.0)
    w_gate_out = noise(seeds[13], (D, HEADS * DV), D ** -0.5, 0.1875, ((1, 2),))
    out_gain = jnp.clip(1.0 + 0.1 * jax.random.normal(seeds[14], (DV,), jnp.float32), 0.5, 1.5)
    w_out = noise(seeds[15], (HEADS * DV, D), (HEADS * DV // 4) ** -0.5, 0.25, ((0, 2),))
    ffn_gain = jnp.clip(1.0 + 0.1 * jax.random.normal(seeds[16], (D,), jnp.float32), 0.5, 1.5)
    w_gate = noise(seeds[17], (D, FF), D ** -0.5, 0.1875, ((1, 2),))
    w_up = noise(seeds[18], (D, FF), D ** -0.5, 0.1875, ((1, 2),))
    w_down = noise(seeds[19], (FF, D), FF ** -0.5, 0.109375, ((0, 2),))
    return {"block_input": block_input, "output_grad": output_grad, "attn_gain": attn_gain, "w_query": w_query, "w_key": w_key, "w_value": w_value, "conv_query": conv_query, "conv_key": conv_key, "conv_value": conv_value, "w_beta": w_beta, "w_alpha": w_alpha, "a_log": a_log, "dt_bias": dt_bias, "w_gate_out": w_gate_out, "out_gain": out_gain, "w_out": w_out, "ffn_gain": ffn_gain, "w_gate": w_gate, "w_up": w_up, "w_down": w_down}


epsilon = 1e-06
highest_precision = lax.Precision.HIGHEST

def rms_scale(values, gain):
    return values * lax.rsqrt(lax.optimization_barrier(jnp.mean(values * values, axis=-1, keepdims=True)) + epsilon) * gain

def conv_silu(extended, kernel):
    taps = kernel.shape[0]
    length = extended.shape[0] - taps + 1
    total = kernel[0] * extended[0:length]
    for offset in range(1, taps):
        total = total + kernel[offset] * extended[offset:offset + length]
    return jax.nn.silu(total)

def head_blocks(values, heads, block):
    length = values.shape[0]
    return values.reshape(length // block, block, heads, -1).transpose(2, 0, 1, 3)

def group_terms(keys, values, beta, log_decay):
    size = keys.shape[-2]
    cumulative_decay = jnp.cumsum(log_decay, axis=-1)
    rows = lax.broadcasted_iota(jnp.int32, (size, size), 0)
    cols = lax.broadcasted_iota(jnp.int32, (size, size), 1)
    keep = rows >= cols
    below = rows > cols
    spread = cumulative_decay[..., :, None] - cumulative_decay[..., None, :]
    decay = jnp.where(keep, jnp.exp(jnp.where(keep, spread, 0.0)), 0.0)
    key_dots = jnp.einsum('...tk,...sk->...ts', keys, keys, precision=highest_precision)
    lower_mat = jnp.eye(size, dtype=keys.dtype) + jnp.where(below, beta[..., :, None] * decay * key_dots, 0.0)
    rhs_all = jnp.concatenate([beta[..., None] * values, (beta * jnp.exp(cumulative_decay))[..., None] * keys], axis=-1)
    solved = jax.scipy.linalg.solve_triangular(lower_mat, rhs_all, lower=True, unit_diagonal=True)
    value_dim = values.shape[-1]
    fresh_values = solved[..., :value_dim]
    mixed_keys = solved[..., value_dim:]
    tail = jnp.exp(cumulative_decay[..., -1:] - cumulative_decay)
    tail_keys = keys * tail[..., None]
    key_dim = keys.shape[-1]
    affine_map_matrix = jnp.exp(cumulative_decay[..., -1])[..., None, None] * jnp.eye(key_dim, dtype=keys.dtype) - jnp.einsum('...sk,...sj->...kj', tail_keys, mixed_keys, precision=highest_precision)
    affine_map_offset = jnp.einsum('...sk,...sv->...kv', tail_keys, fresh_values, precision=highest_precision)
    return (cumulative_decay, decay, fresh_values, mixed_keys, affine_map_matrix, affine_map_offset)

def prepare(ext_query, ext_key, ext_value, conv_query, conv_key, conv_value, small_pre, a_log, dt_bias):
    heads = a_log.shape[0]
    query = head_blocks(conv_silu(ext_query, conv_query), heads, GROUP)
    keys = head_blocks(conv_silu(ext_key, conv_key), heads, GROUP)
    values = head_blocks(conv_silu(ext_value, conv_value), heads, GROUP)
    query = query * lax.rsqrt(lax.optimization_barrier(jnp.sum(query * query, axis=-1, keepdims=True)) + epsilon) * query.shape[-1] ** (-0.5)
    keys = keys * lax.rsqrt(lax.optimization_barrier(jnp.sum(keys * keys, axis=-1, keepdims=True)) + epsilon)
    beta = jax.nn.sigmoid(small_pre[:, :heads])
    log_decay = -jnp.exp(a_log) * jax.nn.softplus(small_pre[:, heads:] + dt_bias)
    beta_blocks = beta.reshape(-1, GROUP, heads).transpose(2, 0, 1)
    decay_blocks = log_decay.reshape(-1, GROUP, heads).transpose(2, 0, 1)
    return (query, keys, group_terms(keys, values, beta_blocks, decay_blocks))

def output_pass(query, keys, terms, state):

    def advance(running_state, pieces):
        query_blocks, keys_c, cumulative_decay, decay, fresh_values, mixed_keys, affine_map_matrix, affine_map_offset = pieces
        stored_values = fresh_values - jnp.einsum('wmq,wqf->wmf', mixed_keys, running_state, precision=highest_precision)
        scores = jnp.einsum('htk,hsk->hts', query_blocks, keys_c, precision=highest_precision) * decay
        scan_output = jnp.exp(cumulative_decay)[..., None] * jnp.einsum('zsi,zif->zsf', query_blocks, running_state, precision=highest_precision)
        scan_output = scan_output + jnp.einsum('hts,hsv->htv', scores, stored_values, precision=highest_precision)
        refreshed_state = jnp.einsum('rml,rlp->rmp', affine_map_matrix, running_state, precision=highest_precision) + affine_map_offset
        return (refreshed_state, scan_output)
    ordered = tuple((jnp.moveaxis(item, 1, 0) for item in (query, keys) + tuple(terms)))
    final, results = lax.scan(advance, state, ordered)
    blocks, heads, size, value_dim = results.shape
    return (results.transpose(0, 2, 1, 3).reshape(blocks * size, heads * value_dim), final)

def gate_norm(mixed, gate_pre, out_gain):
    length = mixed.shape[0]
    width = out_gain.shape[0]
    shaped = mixed.reshape(length, -1, width)
    gates = gate_pre.reshape(length, -1, width)
    return (rms_scale(shaped, out_gain) * jax.nn.silu(gates)).reshape(length, -1)

def reference(block_input, output_grad, attn_gain, w_query, w_key, w_value, conv_query, conv_key, conv_value, w_beta, w_alpha, a_log, dt_bias, w_gate_out, out_gain, w_out, ffn_gain, w_gate, w_up, w_down):
    input_wide = block_input.astype(jnp.float32)
    normed_wide, pull_first = jax.vjp(rms_scale, input_wide, attn_gain)
    normed = normed_wide.astype(jnp.bfloat16)
    proj_query = jnp.dot(normed.astype(jnp.float32), w_query.astype(jnp.float32), preferred_element_type=jnp.float32).astype(jnp.bfloat16)
    proj_key = jnp.dot(normed.astype(jnp.float32), w_key.astype(jnp.float32), preferred_element_type=jnp.float32).astype(jnp.bfloat16)
    proj_value = jnp.dot(normed.astype(jnp.float32), w_value.astype(jnp.float32), preferred_element_type=jnp.float32).astype(jnp.bfloat16)
    small_w = jnp.concatenate([w_beta, w_alpha], axis=1)
    small_pre = jnp.dot(normed.astype(jnp.float32), small_w.astype(jnp.float32), preferred_element_type=jnp.float32)
    gate_pre = jnp.dot(normed.astype(jnp.float32), w_gate_out.astype(jnp.float32), preferred_element_type=jnp.float32)
    margin = KW - 1

    def extend(values):
        return jnp.concatenate([jnp.zeros((margin, values.shape[1]), jnp.float32), values.astype(jnp.float32)], axis=0)

    def mixer(ext_query, ext_key, ext_value, kern_query, kern_key, kern_value, small_in, log_rate, rate_bias):
        query, keys, terms = prepare(ext_query, ext_key, ext_value, kern_query, kern_key, kern_value, small_in, log_rate, rate_bias)
        state = jnp.zeros((HEADS, DK, DV), jnp.float32)
        return output_pass(query, keys, terms, state)[0]
    mixed, pull_mixer = jax.vjp(mixer, extend(proj_query), extend(proj_key), extend(proj_value), conv_query, conv_key, conv_value, small_pre, a_log, dt_bias)
    gated_wide, pull_gate = jax.vjp(gate_norm, mixed, gate_pre, out_gain)
    gated = gated_wide.astype(jnp.bfloat16)
    residual = input_wide + jnp.dot(gated.astype(jnp.float32), w_out.astype(jnp.float32), preferred_element_type=jnp.float32)
    ffn_wide, pull_second = jax.vjp(rms_scale, residual, ffn_gain)
    ffn_input = ffn_wide.astype(jnp.bfloat16)
    gate_act = jnp.dot(ffn_input.astype(jnp.float32), w_gate.astype(jnp.float32), preferred_element_type=jnp.float32)
    up_act = jnp.dot(ffn_input.astype(jnp.float32), w_up.astype(jnp.float32), preferred_element_type=jnp.float32)
    hidden = (jax.nn.silu(gate_act) * up_act).astype(jnp.bfloat16)
    block_output = residual + jnp.dot(hidden.astype(jnp.float32), w_down.astype(jnp.float32), preferred_element_type=jnp.float32)
    grad_hidden = jnp.dot(output_grad.astype(jnp.float32), w_down.T.astype(jnp.float32), preferred_element_type=jnp.float32)
    sigma = jax.nn.sigmoid(gate_act)
    grad_gate_act = (grad_hidden * up_act * sigma * (1.0 + gate_act * (1.0 - sigma))).astype(jnp.bfloat16)
    grad_up_act = (grad_hidden * gate_act * sigma).astype(jnp.bfloat16)
    grad_w_down = jnp.dot(hidden.T.astype(jnp.float32), output_grad.astype(jnp.float32), preferred_element_type=jnp.float32)
    grad_w_gate = jnp.dot(ffn_input.T.astype(jnp.float32), grad_gate_act.astype(jnp.float32), preferred_element_type=jnp.float32)
    grad_w_up = jnp.dot(ffn_input.T.astype(jnp.float32), grad_up_act.astype(jnp.float32), preferred_element_type=jnp.float32)
    grad_ffn_in = jnp.dot(grad_gate_act.astype(jnp.float32), w_gate.T.astype(jnp.float32), preferred_element_type=jnp.float32) + jnp.dot(grad_up_act.astype(jnp.float32), w_up.T.astype(jnp.float32), preferred_element_type=jnp.float32)
    grad_resid_norm, grad_ffn_gain = pull_second(grad_ffn_in)
    grad_residual = output_grad.astype(jnp.float32) + grad_resid_norm
    grad_resid_low = grad_residual.astype(jnp.bfloat16)
    grad_w_out = jnp.dot(gated.T.astype(jnp.float32), grad_resid_low.astype(jnp.float32), preferred_element_type=jnp.float32)
    grad_gated = jnp.dot(grad_resid_low.astype(jnp.float32), w_out.T.astype(jnp.float32), preferred_element_type=jnp.float32)
    grad_mixed, grad_gate_pre, grad_out_gain = pull_gate(grad_gated)
    grad_gate_low = grad_gate_pre.astype(jnp.bfloat16)
    grad_ext_query, grad_ext_key, grad_ext_value, grad_conv_query, grad_conv_key, grad_conv_value, grad_small, grad_a_log, grad_dt_bias = pull_mixer(grad_mixed)
    grad_proj_query = grad_ext_query[margin:].astype(jnp.bfloat16)
    grad_proj_key = grad_ext_key[margin:].astype(jnp.bfloat16)
    grad_proj_value = grad_ext_value[margin:].astype(jnp.bfloat16)
    grad_small_low = grad_small.astype(jnp.bfloat16)
    grad_w_query = jnp.dot(normed.T.astype(jnp.float32), grad_proj_query.astype(jnp.float32), preferred_element_type=jnp.float32)
    grad_w_key = jnp.dot(normed.T.astype(jnp.float32), grad_proj_key.astype(jnp.float32), preferred_element_type=jnp.float32)
    grad_w_value = jnp.dot(normed.T.astype(jnp.float32), grad_proj_value.astype(jnp.float32), preferred_element_type=jnp.float32)
    grad_w_gate_out = jnp.dot(normed.T.astype(jnp.float32), grad_gate_low.astype(jnp.float32), preferred_element_type=jnp.float32)
    grad_w_small = jnp.dot(normed.T.astype(jnp.float32), grad_small_low.astype(jnp.float32), preferred_element_type=jnp.float32)
    grad_normed = jnp.dot(grad_proj_query.astype(jnp.float32), w_query.T.astype(jnp.float32), preferred_element_type=jnp.float32)
    grad_normed = grad_normed + jnp.dot(grad_proj_key.astype(jnp.float32), w_key.T.astype(jnp.float32), preferred_element_type=jnp.float32)
    grad_normed = grad_normed + jnp.dot(grad_proj_value.astype(jnp.float32), w_value.T.astype(jnp.float32), preferred_element_type=jnp.float32)
    grad_normed = grad_normed + jnp.dot(grad_gate_low.astype(jnp.float32), w_gate_out.T.astype(jnp.float32), preferred_element_type=jnp.float32)
    grad_normed = grad_normed + jnp.dot(grad_small_low.astype(jnp.float32), small_w.T.astype(jnp.float32), preferred_element_type=jnp.float32)
    grad_input_norm, grad_attn_gain = pull_first(grad_normed)
    input_grad = grad_residual + grad_input_norm
    return (block_output, input_grad, grad_attn_gain, grad_w_query, grad_w_key, grad_w_value, grad_conv_query, grad_conv_key, grad_conv_value, grad_w_small[:, :HEADS], grad_w_small[:, HEADS:], grad_a_log, grad_dt_bias, grad_w_gate_out, grad_out_gain, grad_w_out, grad_ffn_gain, grad_w_gate, grad_w_up, grad_w_down)
```

```python
import functools

import jax
import jax.numpy as jnp
from jax import lax
from jax.experimental import pallas as pl
from jax.experimental.pallas import tpu as pltpu
from jax.sharding import PartitionSpec as P

EPS = 1e-06
LANES = 128
HALO = 8
f32 = jnp.float32
bf16 = jnp.bfloat16


def nn(a, b):
    dims = (((1,), (0,)), ((), ()))
    return lax.dot_general(a.astype(bf16), b.astype(bf16), dims, preferred_element_type=f32)


def nt(a, b):
    dims = (((1,), (1,)), ((), ()))
    return lax.dot_general(a.astype(bf16), b.astype(bf16), dims, preferred_element_type=f32)


def tn(a, b):
    dims = (((0,), (0,)), ((), ()))
    return lax.dot_general(a.astype(bf16), b.astype(bf16), dims, preferred_element_type=f32)


def exact(a, b):
    dims = (((1,), (0,)), ((), ()))
    return lax.dot_general(a, b, dims, preferred_element_type=f32, precision=lax.Precision.HIGHEST)


def row_sum(a):
    return jnp.sum(a, axis=-1, keepdims=True)


def col_sum(a):
    return jnp.sum(a, axis=0, keepdims=True)


def iotas(size):
    return (
        lax.broadcasted_iota(jnp.int32, (size, size), 0),
        lax.broadcasted_iota(jnp.int32, (size, size), 1),
    )


def unit_lower_inverse(low):
    size = low.shape[0]
    rows, cols = iotas(size)

    def same(shift):
        return lax.shift_right_logical(rows, shift) == lax.shift_right_logical(cols, shift)

    eye = jnp.where(rows == cols, 1.0, 0.0).astype(f32)
    shift = 3
    diag = jnp.where(same(shift), low, 0.0)
    inv = eye - diag
    power = exact(diag, diag)
    inv = inv + exact(inv, power)
    power = exact(power, power)
    inv = inv + exact(inv, power)
    while (1 << shift) < size:
        off = jnp.where(same(shift + 1) & jnp.logical_not(same(shift)), low, 0.0)
        inv = inv - exact(inv, exact(off, inv))
        shift += 1
    return inv


def call(body, outs, *args, scratch=()):
    return pl.pallas_call(
        body,
        out_shape=[jax.ShapeDtypeStruct(s, d) for s, d in outs],
        scratch_shapes=list(scratch),
        compiler_params=pltpu.CompilerParams(vmem_limit_bytes=60000 * 1024),
    )(*args)


def softplus(a):
    return jnp.maximum(a, 0.0) + jnp.log1p(jnp.exp(-jnp.abs(a)))


def silu_parts(a):
    s = jax.nn.sigmoid(a)
    return a * s, s * (1.0 + a * (1.0 - s))


def conv_pre(ext, kern, cols, size, margin):
    total = None
    for j in range(margin + 1):
        term = kern[j : j + 1, cols] * ext[pl.ds(HALO - margin + j, size), cols]
        total = term if total is None else total + term
    return total


def decay_terms(small, rate, bias, heads):
    size = small.shape[0]
    rows, cols = iotas(size)
    log_decay = -jnp.exp(rate) * softplus(small + bias)
    tril = jnp.where(rows >= cols, 1.0, 0.0).astype(f32)
    cum = exact(tril, log_decay)
    return log_decay, cum


def head_decay(cum, cum_t, at, rows, cols):
    g = cum[:, at : at + 1]
    spread = g - cum_t[at : at + 1, :]
    keep = rows >= cols
    return g, jnp.where(keep, jnp.exp(jnp.where(keep, spread, 0.0)), 0.0)


def front_body(
    heads, key_dim, value_dim, margin, slices,
    xe, gain, wq, wk, wv, wg, wsm, kern, rate, bias,
    normed_o, ext_o, gate_o, small_o, q_o, k_o, v_o, inv_o, p_o, w_o, u_o, send_o, ext,
):
    size = xe.shape[0] - HALO
    x = xe[...].astype(f32)
    scale = lax.rsqrt(jnp.mean(x * x, axis=-1, keepdims=True) + EPS)
    normed = (x * scale * gain[...]).astype(bf16)
    normed_o[...] = normed
    kc, vc = heads * key_dim, heads * value_dim
    for ref, lo, hi in ((wq, 0, kc), (wk, kc, 2 * kc), (wv, 2 * kc, 2 * kc + vc)):
        part = nn(normed, ref[...]).astype(bf16)
        ext_o[:, lo:hi] = part
        ext[:, lo:hi] = part.astype(f32)
    own = normed[HALO:]
    gate_o[...] = nn(own, wg[...])
    small = nn(own, wsm[...])
    small_o[...] = small
    beta_all = jax.nn.sigmoid(small)
    log_decay, cum = decay_terms(small, rate[...], bias[...], heads)
    cum_t = cum.T
    rows, cols = iotas(size)
    width = value_dim // slices
    for h in range(heads):
        ks = slice(h * key_dim, (h + 1) * key_dim)
        vs = slice(h * value_dim, (h + 1) * value_dim)
        qh = jax.nn.silu(conv_pre(ext, kern, ks, size, margin))
        kh = jax.nn.silu(conv_pre(ext, kern, slice(kc + ks.start, kc + ks.stop), size, margin))
        v = jax.nn.silu(conv_pre(ext, kern, slice(2 * kc + vs.start, 2 * kc + vs.stop), size, margin))
        q = qh * (lax.rsqrt(row_sum(qh * qh) + EPS) * key_dim**-0.5)
        k = kh * lax.rsqrt(row_sum(kh * kh) + EPS)
        beta = beta_all[:, h : h + 1]
        g, decay = head_decay(cum, cum_t, heads + h, rows, cols)
        eg = jnp.exp(g)
        last = cum[size - 1 : size, heads + h : heads + h + 1]
        dots = nt(jnp.concatenate([k, q], axis=0), k)
        low = jnp.where(rows > cols, beta * decay * dots[:size], 0.0)
        inv = unit_lower_inverse(low)
        rhs = jnp.concatenate([beta * v, (beta * eg) * k], axis=1)
        solved = nn(inv, rhs)
        u, w = solved[:, :value_dim], solved[:, value_dim:]
        kt = k * jnp.exp(last - g)
        maps = tn(jnp.concatenate([u, w], axis=1), kt)
        er, ec = iotas(key_dim)
        at = jnp.where(er == ec, jnp.exp(last), 0.0) - maps[value_dim:]
        bt = maps[:value_dim].astype(bf16)
        at = at.astype(bf16)
        for s in range(slices):
            send_o[h * slices + s, :key_dim, :] = at
            send_o[h * slices + s, key_dim:, :] = bt[s * width : (s + 1) * width]
        q_o[:, ks] = q
        k_o[:, ks] = k
        v_o[:, vs] = v
        inv_o[:, h * size : (h + 1) * size] = inv.astype(bf16)
        p_o[:, h * size : (h + 1) * size] = (dots[size:] * decay).astype(bf16)
        w_o[:, ks] = w.astype(bf16)
        u_o[:, vs] = u


def split(a):
    hi = a.astype(bf16)
    return hi, (a - hi.astype(f32)).astype(bf16)


def scan_fwd_body(key_dim, maps, out):
    n, rows, _ = maps.shape
    state = jnp.zeros((rows - key_dim, key_dim), f32)
    for j in range(n):
        out[j] = state.astype(bf16)
        if j < n - 1:
            hi, lo = split(state)
            a = maps[j, :key_dim, :]
            state = nn(hi, a) + nn(lo, a) + maps[j, key_dim:, :].astype(f32)


def scan_bwd_body(key_dim, maps, local, out):
    n = maps.shape[0]
    state = jnp.zeros(local.shape[1:], f32)
    for j in range(n - 1, -1, -1):
        out[j] = state.astype(bf16)
        if j > 0:
            hi, lo = split(state)
            a = maps[j, :key_dim, :]
            state = nt(hi, a) + nt(lo, a) + local[j].astype(f32)


def mix_body(
    heads, key_dim, value_dim,
    st, u, w, p, q, small, rate, bias, gate, gain, wo,
    stored_o, mixed_o, gated_o, part_o,
):
    size = u.shape[0]
    _, cum = decay_terms(small[...], rate[...], bias[...], heads)
    for h in range(heads):
        ks = slice(h * key_dim, (h + 1) * key_dim)
        vs = slice(h * value_dim, (h + 1) * value_dim)
        s = st[h]
        both = nt(jnp.concatenate([w[:, ks], q[:, ks].astype(bf16)], axis=0), s)
        stored = (u[:, vs] - both[:size]).astype(bf16)
        eg = jnp.exp(cum[:, heads + h : heads + h + 1])
        mixed = eg * both[size:] + nn(p[:, h * size : (h + 1) * size], stored)
        stored_o[:, vs] = stored
        mixed_o[:, vs] = mixed
        scale = lax.rsqrt(jnp.mean(mixed * mixed, axis=-1, keepdims=True) + EPS)
        gated_o[:, vs] = (mixed * scale * gain[...] * jax.nn.silu(gate[:, vs])).astype(bf16)
    part_o[...] = nn(gated_o[...], wo[...]).astype(bf16)


def ffn_body(residual, gain, w_gate, w_up, w_down, grad_hidden, input_o, hid_o, gg_o, gu_o, back_o, down_o):
    r = residual[...]
    scale = lax.rsqrt(jnp.mean(r * r, axis=-1, keepdims=True) + EPS)
    ffn_in = (r * scale * gain[...]).astype(bf16)
    input_o[...] = ffn_in
    gate = nn(ffn_in, w_gate[...])
    up = nn(ffn_in, w_up[...])
    sig = jax.nn.sigmoid(gate)
    gh = grad_hidden[...].astype(f32)
    gu_o[...] = (gh * gate * sig).astype(bf16)
    gg_o[...] = (gh * up * sig * (1.0 + gate * (1.0 - sig))).astype(bf16)
    hid_o[...] = (gate * sig * up).astype(bf16)
    back_o[...] = (nt(gg_o[...], w_gate[...]) + nt(gu_o[...], w_up[...])).astype(bf16)
    down_o[...] = nn(hid_o[...], w_down[...]).astype(bf16)


def turn_body(
    heads, key_dim, value_dim, slices,
    residual, back, og, ffn_gain, wo, mixed, gate, out_gain, p, w, q, small, rate, bias,
    gres_o, glow_o, dfg_o, dmix_o, pdo_o, dgate_o, dog_o, send_o,
):
    r = residual[...]
    scale = lax.rsqrt(jnp.mean(r * r, axis=-1, keepdims=True) + EPS)
    b = back[...]
    normal = r * scale
    dfg_o[...] = col_sum(b * normal)
    d = b * ffn_gain[...]
    gres = og[...].astype(f32) + scale * (d - normal * jnp.mean(d * normal, axis=-1, keepdims=True))
    gres_o[...] = gres
    low = gres.astype(bf16)
    glow_o[...] = low
    dgated = nt(low, wo[...])
    size = r.shape[0]
    width = value_dim // slices
    _, cum = decay_terms(small[...], rate[...], bias[...], heads)
    dog = jnp.zeros((1, value_dim), f32)
    for h in range(heads):
        ks = slice(h * key_dim, (h + 1) * key_dim)
        vs = slice(h * value_dim, (h + 1) * value_dim)
        ps = slice(h * size, (h + 1) * size)
        m = mixed[:, vs]
        scale_h = lax.rsqrt(jnp.mean(m * m, axis=-1, keepdims=True) + EPS)
        n = m * scale_h
        act, dact = silu_parts(gate[:, vs])
        dg = dgated[:, vs]
        dgate_o[:, vs] = (dg * (n * out_gain[...]) * dact).astype(bf16)
        dn = dg * act
        dog = dog + col_sum(dn * n)
        dn = dn * out_gain[...]
        dm = scale_h * (dn - n * jnp.mean(dn * n, axis=-1, keepdims=True))
        dm = dm.astype(bf16)
        dmix_o[:, vs] = dm
        pdo = tn(p[:, ps], dm)
        pdo_o[:, vs] = pdo
        eg = jnp.exp(cum[:, heads + h : heads + h + 1])
        left = jnp.concatenate([dm, -pdo.astype(bf16)], axis=0)
        right = jnp.concatenate([(q[:, ks] * eg).astype(bf16), w[:, ks]], axis=0)
        local = tn(left, right).astype(bf16)
        for s in range(slices):
            send_o[h * slices + s] = local[s * width : (s + 1) * width]
    dog_o[...] = dog


def back_body(
    heads, key_dim, value_dim, margin,
    dst, st, ext_i, kern, q_i, k_i, v_i, inv_i, p_i, stored_i, dmix_i, pdo_i, dgate_i, small, rate, bias,
    wq, wk, wv, wg, wsm,
    grads_o, part_o, dconv_o, drate_o, dbias_o, ext, pad,
):
    size = q_i.shape[0]
    total = size + HALO
    kc, vc = heads * key_dim, heads * value_dim
    proj = 2 * kc + vc
    ext[...] = ext_i[...].astype(f32)
    pad[:HALO, :] = jnp.zeros((HALO, proj), f32)
    pad[HALO + size :, :] = jnp.zeros((HALO, proj), f32)
    sm = small[...]
    log_decay, cum = decay_terms(sm, rate[...], bias[...], heads)
    cum_t = cum.T
    beta_all = jax.nn.sigmoid(sm)
    rows, cols = iotas(size)
    lane = lax.broadcasted_iota(jnp.int32, (size, LANES), 1)
    end_row = lax.broadcasted_iota(jnp.int32, (size, 1), 0) == size - 1
    dcum = jnp.zeros((size, LANES), f32)
    dbeta_all = jnp.zeros((size, LANES), f32)

    def conv_back(dy, lo, hi):
        cs = slice(lo, hi)
        pre = conv_pre(ext, kern, cs, size, margin)
        _, dact = silu_parts(pre)
        dpre = dy * dact
        pad[pl.ds(HALO, size), cs] = dpre
        for j in range(margin + 1):
            dconv_o[j : j + 1, cs] = col_sum(dpre * ext[pl.ds(HALO - margin + j, size), cs])

    for h in range(heads):
        ks = slice(h * key_dim, (h + 1) * key_dim)
        vs = slice(h * value_dim, (h + 1) * value_dim)
        ps = slice(h * size, (h + 1) * size)
        q, k, v = q_i[:, ks], k_i[:, ks], v_i[:, vs]
        stored, do = stored_i[:, vs], dmix_i[:, vs]
        s, ds = st[h], dst[h]
        beta = beta_all[:, h : h + 1]
        g, decay = head_decay(cum, cum_t, heads + h, rows, cols)
        eg = jnp.exp(g)
        last = cum[size - 1 : size, heads + h : heads + h + 1]
        kt = k * jnp.exp(last - g)
        kl, ql = k.astype(bf16), q.astype(bf16)
        dstored = pdo_i[:, vs] + nt(kt, ds)
        dr = tn(inv_i[:, ps], dstored)
        drl = dr.astype(bf16)
        states = nt(jnp.concatenate([kl, ql], axis=0), s)
        k_s, q_s = states[:size], states[size:]
        both = jnp.concatenate([drl, do], axis=0)
        inner = nt(both, stored)
        back = nn(both, s)
        dkt = nn(stored, ds)
        dots = nt(kl, kl)
        scaled = decay * dots
        dlow = jnp.where(rows > cols, -inner[:size], 0.0)
        dp = jnp.where(rows >= cols, inner[size:], 0.0)
        dv = beta * dr
        spread = dlow * (beta * scaled) + dp * p_i[:, ps].astype(f32)
        dqk = (dp * decay).astype(bf16)
        dkk = dlow * (beta * decay)
        left = jnp.concatenate([dqk, (dkk + dkk.T).astype(bf16)], axis=0)
        on_k = nn(left, kl)
        dq = on_k[:size] + eg * back[size:]
        tail_part = row_sum(dkt * kt)
        dk = on_k[size:] + tn(dqk, ql) - (beta * eg) * back[:size] + jnp.exp(last - g) * dkt
        dbeta = row_sum(dr * (v - eg * k_s)) + row_sum(dlow * scaled)
        dg = row_sum(spread) - row_sum(spread.T) - tail_part
        dg = dg + eg * row_sum(do.astype(f32) * q_s) - (beta * eg) * row_sum(dr * k_s)
        carry = col_sum(row_sum(s.astype(f32) * ds.astype(f32)))
        at_end = col_sum(tail_part) + jnp.exp(last) * carry
        dg = dg + jnp.where(end_row, at_end, 0.0)
        dcum = dcum + jnp.where(lane == heads + h, dg, 0.0)
        dbeta_all = dbeta_all + jnp.where(lane == h, dbeta, 0.0)
        qh = jax.nn.silu(conv_pre(ext, kern, ks, size, margin))
        rq = lax.rsqrt(row_sum(qh * qh) + EPS)
        unit = qh * rq
        dqn = dq * key_dim**-0.5
        conv_back(rq * (dqn - unit * row_sum(dqn * unit)), ks.start, ks.stop)
        kh = jax.nn.silu(conv_pre(ext, kern, slice(kc + ks.start, kc + ks.stop), size, margin))
        rk = lax.rsqrt(row_sum(kh * kh) + EPS)
        conv_back(rk * (dk - k * row_sum(dk * k)), kc + ks.start, kc + ks.stop)
        conv_back(dv, 2 * kc + vs.start, 2 * kc + vs.stop)

    triu = jnp.where(rows <= cols, 1.0, 0.0).astype(f32)
    dlog = exact(triu, dcum)
    dalpha = dlog * (-jnp.exp(rate[...])) * jax.nn.sigmoid(sm + bias[...])
    drate_o[...] = col_sum(dlog * log_decay)
    dbias_o[...] = col_sum(dalpha)
    dsmall = dalpha + dbeta_all * beta_all * (1.0 - beta_all)
    acc = None
    for ref, lo, hi in ((wq, 0, kc), (wk, kc, 2 * kc), (wv, 2 * kc, proj)):
        dext = None
        for j in range(margin + 1):
            term = kern[j : j + 1, lo:hi] * pad[pl.ds(margin - j, total), lo:hi]
            dext = term if dext is None else dext + term
        dext = dext.astype(bf16)
        grads_o[:, lo:hi] = dext
        part = nt(dext, ref[...])
        acc = part if acc is None else acc + part
    dsl = dsmall.astype(bf16)
    gc = wg.shape[1]
    grads_o[:HALO, proj:] = jnp.zeros((HALO, gc + LANES), bf16)
    grads_o[HALO:, proj : proj + gc] = dgate_i[...]
    grads_o[HALO:, proj + gc :] = dsl
    part_o[:HALO, :] = acc[:HALO].astype(bf16)
    part_o[HALO:, :] = (acc[HALO:] + nt(dgate_i[...], wg[...]) + nt(dsl, wsm[...])).astype(bf16)


def shift_along(block, axis, distance):
    devices = range(lax.axis_size(axis))
    route = [(i - distance, i) for i in devices if i - distance in devices]
    return lax.ppermute(block, axis, route)


def tensor_sum(part):
    if lax.axis_size("tensor") == 2:
        other = lax.ppermute(part, "tensor", [(0, 1), (1, 0)])
        return part.astype(f32) + other.astype(f32)
    return lax.psum(part, "tensor").astype(f32)


def swap(blocks):
    return lax.all_to_all(blocks, "dp", 0, 0, tiled=True)


def on_device(
    block_input, output_grad, attn_gain, w_query, w_key, w_value, conv_query, conv_key, conv_value,
    w_beta, w_alpha, a_log, dt_bias, w_gate_out, out_gain, w_out, ffn_gain, w_gate, w_up, w_down,
):
    size, width = block_input.shape
    heads = a_log.shape[0]
    key_dim = w_query.shape[1] // heads
    value_dim = w_value.shape[1] // heads
    margin = conv_query.shape[0] - 1
    peers = lax.axis_size("dp")
    slices = peers // heads
    kc, vc, gc, ff = w_query.shape[1], w_value.shape[1], w_gate_out.shape[1], w_gate.shape[1]
    proj = 2 * kc + vc
    dims = (heads, key_dim, value_dim)

    halo = shift_along(jnp.pad(block_input[-margin:], ((HALO - margin, 0), (0, 0))), "dp", 1)
    grad_hidden = jnp.dot(output_grad, w_down.T, preferred_element_type=f32).astype(bf16)
    xe = jnp.concatenate([halo, block_input], axis=0)
    kern = jnp.concatenate([conv_query, conv_key, conv_value], axis=1)
    small_w = jnp.pad(jnp.concatenate([w_beta, w_alpha], axis=1), ((0, 0), (0, LANES - 2 * heads)))
    rate = jnp.pad(a_log[None], ((0, 0), (heads, LANES - 2 * heads)))
    bias = jnp.pad(dt_bias[None], ((0, 0), (heads, LANES - 2 * heads)))
    again, fgain, ogain = attn_gain[None], ffn_gain[None], out_gain[None]

    normed, ext, gate_pre, small, q, k, v, inv, p, w, u, send = call(
        functools.partial(front_body, *dims, margin, slices),
        [
            ((size + HALO, width), bf16), ((size + HALO, proj), bf16), ((size, gc), f32),
            ((size, LANES), f32), ((size, kc), f32), ((size, kc), f32), ((size, vc), f32),
            ((size, heads * size), bf16), ((size, heads * size), bf16), ((size, kc), bf16),
            ((size, vc), f32), ((peers, key_dim + value_dim // slices, key_dim), bf16),
        ],
        xe, again, w_query, w_key, w_value, w_gate_out, small_w, kern, rate, bias,
        scratch=[pltpu.VMEM((size + HALO, proj), f32)],
    )
    maps = swap(send)
    piece = (peers, value_dim // slices, key_dim)
    (entry,) = call(functools.partial(scan_fwd_body, key_dim), [(piece, bf16)], maps)
    st = swap(entry).reshape(heads, value_dim, key_dim)
    stored, mixed, gated, mix_part = call(
        functools.partial(mix_body, *dims),
        [((size, vc), bf16), ((size, vc), f32), ((size, vc), bf16), ((size, width), bf16)],
        st, u, w, p, q, small, rate, bias, gate_pre, ogain, w_out,
    )
    residual = block_input.astype(f32) + tensor_sum(mix_part)
    ffn_input, hidden, gga, gua, back_part, down_part = call(
        ffn_body,
        [((size, width), bf16), ((size, ff), bf16), ((size, ff), bf16), ((size, ff), bf16),
         ((size, width), bf16), ((size, width), bf16)],
        residual, fgain, w_gate, w_up, w_down, grad_hidden,
    )
    back = tensor_sum(back_part)
    gres, glow, dfg, dmix, pdo, dgate, dog, send_back = call(
        functools.partial(turn_body, *dims, slices),
        [((size, width), f32), ((size, width), bf16), ((1, width), f32), ((size, vc), bf16),
         ((size, vc), f32), ((size, gc), bf16), ((1, value_dim), f32), (piece, bf16)],
        residual, back, output_grad, fgain, w_out, mixed, gate_pre, ogain, p, w, q, small, rate, bias,
    )
    local = swap(send_back)
    (exits,) = call(functools.partial(scan_bwd_body, key_dim), [(piece, bf16)], maps, local)
    dst = swap(exits).reshape(heads, value_dim, key_dim)

    block_output = residual + tensor_sum(down_part)

    def weight_grad(a, b):
        return lax.dot_general(a, b, (((0,), (0,)), ((), ())), preferred_element_type=f32).astype(bf16)

    def reduce_rows(parts):
        return lax.psum_scatter(
            jnp.concatenate(parts, axis=1), "dp", scatter_dimension=0, tiled=True
        ).astype(f32)

    first = reduce_rows([
        weight_grad(ffn_input, gga), weight_grad(ffn_input, gua),
        weight_grad(output_grad, hidden), weight_grad(glow, gated),
    ])

    grads, part, dconv, drate, dbias = call(
        functools.partial(back_body, *dims, margin),
        [((size + HALO, proj + gc + LANES), bf16), ((size + HALO, width), bf16),
         ((margin + 1, proj), f32), ((1, LANES), f32), ((1, LANES), f32)],
        dst, st, ext, kern, q, k, v, inv, p, stored, dmix, pdo, dgate, small, rate, bias,
        w_query, w_key, w_value, w_gate_out, small_w,
        scratch=[pltpu.VMEM((size + HALO, proj), f32), pltpu.VMEM((size + 2 * HALO, proj), f32)],
    )
    rim = tensor_sum(shift_along(part[:HALO], "dp", -1))
    gnorm = tensor_sum(part[HALO:])
    gnorm = jnp.concatenate([gnorm[: size - HALO], gnorm[size - HALO :] + rim], axis=0)
    x = block_input.astype(f32)
    scale = lax.rsqrt(jnp.mean(x * x, axis=-1, keepdims=True) + EPS)
    normal = x * scale
    dag = jnp.sum(gnorm * normal, axis=0)
    d = gnorm * again
    input_grad = gres + scale * (d - normal * jnp.mean(d * normal, axis=-1, keepdims=True))

    gains = jnp.stack([dag, dfg[0]], axis=1).astype(bf16)
    second = reduce_rows([
        weight_grad(normed, grads),
        jnp.pad(gains, ((0, 0), (0, LANES - 2))),
    ])
    dog_both = tensor_sum(jnp.pad(dog, ((0, 7), (0, 0)))) [:1]
    flat = jnp.concatenate([
        dconv.reshape(-1, LANES), drate, dbias, dog_both.reshape(-1, LANES),
    ], axis=0)
    flat = jnp.sum(lax.all_gather(flat, "dp"), axis=0)
    rows = (margin + 1) * proj // LANES
    gconv = flat[:rows].reshape(margin + 1, proj)
    g_rate = flat[rows, heads : 2 * heads]
    g_bias = flat[rows + 1, heads : 2 * heads]
    g_out_gain = flat[rows + 2 :].reshape(-1)
    sm = proj + gc
    return (
        block_output, input_grad, second[:, sm + LANES],
        second[:, :kc], second[:, kc : 2 * kc], second[:, 2 * kc : proj],
        gconv[:, :kc], gconv[:, kc : 2 * kc], gconv[:, 2 * kc :],
        second[:, sm : sm + heads], second[:, sm + heads : sm + 2 * heads],
        g_rate, g_bias, second[:, proj:sm], g_out_gain,
        first[:, 3 * ff :].T, second[:, sm + LANES + 1],
        first[:, :ff], first[:, ff : 2 * ff], first[:, 2 * ff : 3 * ff].T,
    )


def solution(mesh):
    rows, cols, whole = P("dp", None), P(None, "tensor"), P()
    heads, high = P("tensor"), P("tensor", None)
    in_specs = (
        rows, rows, whole, cols, cols, cols, cols, cols, cols, cols, cols, heads, heads,
        cols, whole, high, whole, cols, cols, high,
    )
    both, crossed, dp = P("dp", "tensor"), P("tensor", "dp"), P("dp")
    out_specs = (
        rows, rows, dp, both, both, both, cols, cols, cols, both, both, heads, heads,
        both, whole, crossed, dp, both, both, crossed,
    )
    return jax.shard_map(
        on_device, mesh=mesh, in_specs=in_specs, out_specs=out_specs, check_vma=False
    )
```

```python
import functools

import jax
import jax.numpy as jnp
from jax import lax
from jax.experimental import pallas as pl
from jax.experimental.pallas import tpu as pltpu
from jax.sharding import PartitionSpec as P

EPS = 1e-06
LANES = 128
HALO = 8
f32 = jnp.float32
bf16 = jnp.bfloat16


def nn(a, b):
    dims = (((1,), (0,)), ((), ()))
    return lax.dot_general(a.astype(bf16), b.astype(bf16), dims, preferred_element_type=f32)


def nt(a, b):
    dims = (((1,), (1,)), ((), ()))
    return lax.dot_general(a.astype(bf16), b.astype(bf16), dims, preferred_element_type=f32)


def tn(a, b):
    dims = (((0,), (0,)), ((), ()))
    return lax.dot_general(a.astype(bf16), b.astype(bf16), dims, preferred_element_type=f32)


def exact(a, b):
    dims = (((1,), (0,)), ((), ()))
    return lax.dot_general(a, b, dims, preferred_element_type=f32, precision=lax.Precision.HIGHEST)


def row_sum(a):
    return jnp.sum(a, axis=-1, keepdims=True)


def col_sum(a):
    return jnp.sum(a, axis=0, keepdims=True)


def iotas(size):
    return (
        lax.broadcasted_iota(jnp.int32, (size, size), 0),
        lax.broadcasted_iota(jnp.int32, (size, size), 1),
    )


def exact3(a, b):
    (ah, al), (bh, bl) = a, b
    return nn(ah, bh) + (nn(ah, bl) + nn(al, bh))


def unit_lower_inverses(lows):
    size = lows[0].shape[0]
    rows, cols = iotas(size)

    def same(shift):
        return lax.shift_right_logical(rows, shift) == lax.shift_right_logical(cols, shift)

    def each(f, *lists):
        return [f(*items) for items in zip(*lists, strict=True)]

    eye = jnp.where(rows == cols, 1.0, 0.0).astype(f32)
    shift = 3
    diags = [jnp.where(same(shift), low, 0.0) for low in lows]
    invs = [eye - diag for diag in diags]
    powers = each(split, diags)
    for _ in range(shift - 1):
        powers = each(split, each(exact3, powers, powers))
        invs = each(lambda x, y: x + y, invs, each(exact3, each(split, invs), powers))
    while (1 << shift) < size:
        keep = same(shift + 1) & jnp.logical_not(same(shift))
        offs = [split(jnp.where(keep, low, 0.0)) for low in lows]
        halves = each(split, invs)
        inner = each(split, each(exact3, offs, halves))
        invs = each(lambda x, y: x - y, invs, each(exact3, halves, inner))
        shift += 1
    return invs


def call(body, outs, *args, scratch=()):
    return pl.pallas_call(
        body,
        out_shape=[jax.ShapeDtypeStruct(s, d) for s, d in outs],
        scratch_shapes=list(scratch),
        compiler_params=pltpu.CompilerParams(vmem_limit_bytes=60000 * 1024),
    )(*args)


def softplus(a):
    return jnp.maximum(a, 0.0) + jnp.log1p(jnp.exp(-jnp.abs(a)))


def place(row, heads):
    lane = lax.broadcasted_iota(jnp.int32, (1, LANES), 1)
    out = jnp.zeros((1, LANES), f32)
    for h in range(heads):
        out = jnp.where(lane == heads + h, row[0:1, h : h + 1], out)
    return out


def silu_parts(a):
    s = jax.nn.sigmoid(a)
    return a * s, s * (1.0 + a * (1.0 - s))


def conv_pre(ext, kern, base, cols, size, margin):
    total = None
    for j in range(margin + 1):
        tap = kern[j : j + 1, cols.start - base : cols.stop - base]
        term = tap * ext[pl.ds(HALO - margin + j, size), cols]
        total = term if total is None else total + term
    return total


def decay_terms(small, rate, bias, heads):
    size = small.shape[0]
    rows, cols = iotas(size)
    log_decay = -jnp.exp(rate) * softplus(small + bias)
    tril = jnp.where(rows >= cols, 1.0, 0.0).astype(f32)
    cum = exact(tril, log_decay)
    return log_decay, cum


def head_decay(cum, cum_t, at, rows, cols):
    g = cum[:, at : at + 1]
    spread = g - cum_t[at : at + 1, :]
    keep = rows >= cols
    return g, jnp.where(keep, jnp.exp(jnp.where(keep, spread, 0.0)), 0.0)


def front_body(
    heads, key_dim, value_dim, margin, slices,
    xs, halo, gain, wq, wk, wv, wg, wb, wa, kq, kk, kv, rate, bias,
    normed_o, ext_o, gate_o, small_o, cum_o, q_o, k_o, v_o, inv_o, p_o, w_o, u_o, wsm_o, send_o, ext,
):
    size = xs.shape[0]
    for ref, lo, hi in ((halo, 0, HALO), (xs, HALO, HALO + size)):
        x = ref[...].astype(f32)
        scale = lax.rsqrt(jnp.mean(x * x, axis=-1, keepdims=True) + EPS)
        normed_o[lo:hi, :] = (x * scale * gain[...]).astype(bf16)
    normed = normed_o[...]
    wsm_o[...] = jnp.zeros(wsm_o.shape, bf16)
    wsm_o[:heads, :] = wb[...]
    wsm_o[heads : 2 * heads, :] = wa[...]
    kc, vc = heads * key_dim, heads * value_dim
    for ref, lo, hi in ((wq, 0, kc), (wk, kc, 2 * kc), (wv, 2 * kc, 2 * kc + vc)):
        part = nn(normed, ref[...]).astype(bf16)
        ext_o[:, lo:hi] = part
        ext[:, lo:hi] = part.astype(f32)
    own = normed[HALO:]
    gate_o[...] = nn(own, wg[...])
    small = nt(own, wsm_o[...])
    small_o[...] = small
    beta_all = jax.nn.sigmoid(small)
    log_decay, cum = decay_terms(small, place(rate, heads), place(bias, heads), heads)
    cum_o[...] = cum
    cum_t = cum.T
    rows, cols = iotas(size)
    width = value_dim // slices
    kept = []
    for h in range(heads):
        ks = slice(h * key_dim, (h + 1) * key_dim)
        vs = slice(h * value_dim, (h + 1) * value_dim)
        qh = jax.nn.silu(conv_pre(ext, kq, 0, ks, size, margin))
        kh = jax.nn.silu(conv_pre(ext, kk, kc, slice(kc + ks.start, kc + ks.stop), size, margin))
        v_o[:, vs] = jax.nn.silu(conv_pre(ext, kv, 2 * kc, slice(2 * kc + vs.start, 2 * kc + vs.stop), size, margin))
        q = qh * (lax.rsqrt(row_sum(qh * qh) + EPS) * key_dim**-0.5)
        k = kh * lax.rsqrt(row_sum(kh * kh) + EPS)
        q_o[:, ks] = q
        k_o[:, ks] = k
        beta = beta_all[:, h : h + 1]
        g, decay = head_decay(cum, cum_t, heads + h, rows, cols)
        dots = nt(jnp.concatenate([k, q], axis=0), k)
        low = jnp.where(rows > cols, beta * decay * dots[:size], 0.0)
        p_o[:, h * size : (h + 1) * size] = (dots[size:] * decay).astype(bf16)
        kept.append((ks, vs, beta, g, low))
    invs = unit_lower_inverses([item[-1] for item in kept])
    solved_all = []
    for (ks, vs, beta, g, _), inv in zip(kept, invs, strict=True):
        rhs = jnp.concatenate([beta * v_o[:, vs], (beta * jnp.exp(g)) * k_o[:, ks]], axis=1)
        solved_all.append(nn(inv, rhs))
    for h, (ks, vs, beta, g, _) in enumerate(kept):
        inv_o[:, h * size : (h + 1) * size] = invs[h].astype(bf16)
        last = cum[size - 1 : size, heads + h : heads + h + 1]
        solved = solved_all[h]
        kt = k_o[:, ks] * jnp.exp(last - g)
        maps = tn(solved, kt)
        er, ec = iotas(key_dim)
        at = jnp.where(er == ec, jnp.exp(last), 0.0) - maps[value_dim:]
        bt = maps[:value_dim].astype(bf16)
        at = at.astype(bf16)
        for s in range(slices):
            send_o[h * slices + s, :key_dim, :] = at
            send_o[h * slices + s, key_dim:, :] = bt[s * width : (s + 1) * width]
        w_o[:, ks] = solved[:, value_dim:].astype(bf16)
        u_o[:, vs] = solved[:, :value_dim]


def split(a):
    hi = a.astype(bf16)
    return hi, (a - hi.astype(f32)).astype(bf16)


def scan_fwd_body(key_dim, maps, out):
    n, rows, _ = maps.shape
    state = jnp.zeros((rows - key_dim, key_dim), f32)
    for j in range(n):
        out[j] = state.astype(bf16)
        if j < n - 1:
            hi, lo = split(state)
            a = maps[j, :key_dim, :]
            state = nn(hi, a) + nn(lo, a) + maps[j, key_dim:, :].astype(f32)


def scan_bwd_body(key_dim, maps, local, out):
    n = maps.shape[0]
    state = jnp.zeros(local.shape[1:], f32)
    for j in range(n - 1, -1, -1):
        out[j] = state.astype(bf16)
        if j > 0:
            hi, lo = split(state)
            a = maps[j, :key_dim, :]
            state = nt(hi, a) + nt(lo, a) + local[j].astype(f32)


def mix_body(
    heads, key_dim, value_dim,
    st, u, w, p, q, cum, gate, gain, wo,
    stored_o, mixed_o, gated_o, part_o,
):
    size = u.shape[0]
    for h in range(heads):
        ks = slice(h * key_dim, (h + 1) * key_dim)
        vs = slice(h * value_dim, (h + 1) * value_dim)
        s = st[h]
        both = nt(jnp.concatenate([w[:, ks], q[:, ks].astype(bf16)], axis=0), s)
        stored = (u[:, vs] - both[:size]).astype(bf16)
        eg = jnp.exp(cum[:, heads + h : heads + h + 1])
        mixed = eg * both[size:] + nn(p[:, h * size : (h + 1) * size], stored)
        stored_o[:, vs] = stored
        mixed_o[:, vs] = mixed
        scale = lax.rsqrt(jnp.mean(mixed * mixed, axis=-1, keepdims=True) + EPS)
        gated_o[:, vs] = (mixed * scale * gain[...] * jax.nn.silu(gate[:, vs])).astype(bf16)
    part_o[...] = nn(gated_o[...], wo[...]).astype(bf16)


def ffn_body(x, mine, other, gain, w_gate, w_up, w_down, grad_hidden, input_o, hid_o, gg_o, gu_o, back_o, down_o):
    r = x[...].astype(f32) + (mine[...].astype(f32) + other[...].astype(f32))
    scale = lax.rsqrt(jnp.mean(r * r, axis=-1, keepdims=True) + EPS)
    ffn_in = (r * scale * gain[...]).astype(bf16)
    input_o[...] = ffn_in
    gate = nn(ffn_in, w_gate[...])
    up = nn(ffn_in, w_up[...])
    sig = jax.nn.sigmoid(gate)
    gh = grad_hidden[...].astype(f32)
    gu_o[...] = (gh * gate * sig).astype(bf16)
    gg_o[...] = (gh * up * sig * (1.0 + gate * (1.0 - sig))).astype(bf16)
    hid_o[...] = (gate * sig * up).astype(bf16)
    back_o[...] = (nt(gg_o[...], w_gate[...]) + nt(gu_o[...], w_up[...])).astype(bf16)
    down_o[...] = nn(hid_o[...], w_down[...]).astype(bf16)


def turn_body(
    heads, key_dim, value_dim, slices,
    x, mine, other, back_mine, back_other, og, ffn_gain, wo, mixed, gate, out_gain, p, w, q, cum,
    gres_o, glow_o, dfg_o, dmix_o, pdo_o, dgate_o, dog_o, send_o,
):
    r = x[...].astype(f32) + (mine[...].astype(f32) + other[...].astype(f32))
    scale = lax.rsqrt(jnp.mean(r * r, axis=-1, keepdims=True) + EPS)
    b = back_mine[...].astype(f32) + back_other[...].astype(f32)
    normal = r * scale
    dfg_o[...] = col_sum(b * normal)
    d = b * ffn_gain[...]
    gres = og[...].astype(f32) + scale * (d - normal * jnp.mean(d * normal, axis=-1, keepdims=True))
    gres_o[...] = gres
    low = gres.astype(bf16)
    glow_o[...] = low
    dgated = nt(low, wo[...])
    size = r.shape[0]
    width = value_dim // slices
    dog = jnp.zeros((1, value_dim), f32)
    for h in range(heads):
        ks = slice(h * key_dim, (h + 1) * key_dim)
        vs = slice(h * value_dim, (h + 1) * value_dim)
        ps = slice(h * size, (h + 1) * size)
        m = mixed[:, vs]
        scale_h = lax.rsqrt(jnp.mean(m * m, axis=-1, keepdims=True) + EPS)
        n = m * scale_h
        act, dact = silu_parts(gate[:, vs])
        dg = dgated[:, vs]
        dgate_o[:, vs] = (dg * (n * out_gain[...]) * dact).astype(bf16)
        dn = dg * act
        dog = dog + col_sum(dn * n)
        dn = dn * out_gain[...]
        dm = scale_h * (dn - n * jnp.mean(dn * n, axis=-1, keepdims=True))
        dm = dm.astype(bf16)
        dmix_o[:, vs] = dm
        pdo = tn(p[:, ps], dm)
        pdo_o[:, vs] = pdo
        eg = jnp.exp(cum[:, heads + h : heads + h + 1])
        left = jnp.concatenate([dm, -pdo.astype(bf16)], axis=0)
        right = jnp.concatenate([(q[:, ks] * eg).astype(bf16), w[:, ks]], axis=0)
        local = tn(left, right).astype(bf16)
        for s in range(slices):
            send_o[h * slices + s] = local[s * width : (s + 1) * width]
    dog_o[...] = dog


def back_body(
    heads, key_dim, value_dim, margin,
    dst, st, xs, halo, normed, ext_i, kq, kk, kv, q_i, k_i, v_i, inv_i, p_i, stored_i, dmix_i, pdo_i, dgate_i,
    small, cum_i, rate_i, bias_i, dog_mine, dog_other, wq, wk, wv, wg, wsm,
    send_o, part_o, wsmall_o, ext, pad, flat,
):
    size = q_i.shape[0]
    total = size + HALO
    kc, vc = heads * key_dim, heads * value_dim
    proj = 2 * kc + vc
    ext[...] = ext_i[...].astype(f32)
    pad[:HALO, :] = jnp.zeros((HALO, proj), f32)
    pad[HALO + size :, :] = jnp.zeros((HALO, proj), f32)
    sm = small[...]
    cum = cum_i[...]
    rate, bias = place(rate_i, heads), place(bias_i, heads)
    log_decay = -jnp.exp(rate) * softplus(sm + bias)
    cum_t = cum.T
    beta_all = jax.nn.sigmoid(sm)
    rows, cols = iotas(size)
    lane = lax.broadcasted_iota(jnp.int32, (size, LANES), 1)
    end_row = lax.broadcasted_iota(jnp.int32, (size, 1), 0) == size - 1
    dcum = jnp.zeros((size, LANES), f32)
    dbeta_all = jnp.zeros((size, LANES), f32)

    blocks = proj // LANES
    flat[...] = jnp.zeros(flat.shape, f32)

    def conv_back(dy, kern, base, lo, hi):
        cs = slice(lo, hi)
        pre = conv_pre(ext, kern, base, cs, size, margin)
        _, dact = silu_parts(pre)
        dpre = dy * dact
        pad[pl.ds(HALO, size), cs] = dpre
        for j in range(margin + 1):
            tap = col_sum(dpre * ext[pl.ds(HALO - margin + j, size), cs])
            for c in range((hi - lo) // LANES):
                at = j * blocks + lo // LANES + c
                flat[at : at + 1, :] = tap[:, c * LANES : (c + 1) * LANES]

    for h in range(heads):
        ks = slice(h * key_dim, (h + 1) * key_dim)
        vs = slice(h * value_dim, (h + 1) * value_dim)
        ps = slice(h * size, (h + 1) * size)
        q, k, v = q_i[:, ks], k_i[:, ks], v_i[:, vs]
        stored, do = stored_i[:, vs], dmix_i[:, vs]
        s, ds = st[h], dst[h]
        beta = beta_all[:, h : h + 1]
        g, decay = head_decay(cum, cum_t, heads + h, rows, cols)
        eg = jnp.exp(g)
        last = cum[size - 1 : size, heads + h : heads + h + 1]
        kt = k * jnp.exp(last - g)
        kl, ql = k.astype(bf16), q.astype(bf16)
        dstored = pdo_i[:, vs] + nt(kt, ds)
        dr = tn(inv_i[:, ps], dstored)
        drl = dr.astype(bf16)
        states = nt(jnp.concatenate([kl, ql], axis=0), s)
        k_s, q_s = states[:size], states[size:]
        both = jnp.concatenate([drl, do], axis=0)
        inner = nt(both, stored)
        back = nn(both, s)
        dkt = nn(stored, ds)
        dots = nt(kl, kl)
        scaled = decay * dots
        dlow = jnp.where(rows > cols, -inner[:size], 0.0)
        dp = jnp.where(rows >= cols, inner[size:], 0.0)
        dv = beta * dr
        spread = dlow * (beta * scaled) + dp * p_i[:, ps].astype(f32)
        dqk = (dp * decay).astype(bf16)
        dkk = dlow * (beta * decay)
        left = jnp.concatenate([dqk, (dkk + dkk.T).astype(bf16)], axis=0)
        on_k = nn(left, kl)
        dq = on_k[:size] + eg * back[size:]
        tail_part = row_sum(dkt * kt)
        dk = on_k[size:] + tn(dqk, ql) - (beta * eg) * back[:size] + jnp.exp(last - g) * dkt
        dbeta = row_sum(dr * (v - eg * k_s)) + row_sum(dlow * scaled)
        dg = row_sum(spread) - row_sum(spread.T) - tail_part
        dg = dg + eg * row_sum(do.astype(f32) * q_s) - (beta * eg) * row_sum(dr * k_s)
        carry = col_sum(row_sum(s.astype(f32) * ds.astype(f32)))
        at_end = col_sum(tail_part) + jnp.exp(last) * carry
        dg = dg + jnp.where(end_row, at_end, 0.0)
        dcum = dcum + jnp.where(lane == heads + h, dg, 0.0)
        dbeta_all = dbeta_all + jnp.where(lane == h, dbeta, 0.0)
        qh = jax.nn.silu(conv_pre(ext, kq, 0, ks, size, margin))
        rq = lax.rsqrt(row_sum(qh * qh) + EPS)
        unit = qh * rq
        dqn = dq * key_dim**-0.5
        conv_back(rq * (dqn - unit * row_sum(dqn * unit)), kq, 0, ks.start, ks.stop)
        kh = jax.nn.silu(conv_pre(ext, kk, kc, slice(kc + ks.start, kc + ks.stop), size, margin))
        rk = lax.rsqrt(row_sum(kh * kh) + EPS)
        conv_back(rk * (dk - k * row_sum(dk * k)), kk, kc, kc + ks.start, kc + ks.stop)
        conv_back(dv, kv, 2 * kc, 2 * kc + vs.start, 2 * kc + vs.stop)

    triu = jnp.where(rows <= cols, 1.0, 0.0).astype(f32)
    dlog = exact(triu, dcum)
    dalpha = dlog * (-jnp.exp(rate)) * jax.nn.sigmoid(sm + bias)
    dsmall = dalpha + dbeta_all * beta_all * (1.0 - beta_all)
    taps = (margin + 1) * blocks
    flat[taps : taps + 1, :] = col_sum(dlog * log_decay)
    flat[taps + 1 : taps + 2, :] = col_sum(dalpha)
    dog = dog_mine[...] + dog_other[...]
    for c in range(value_dim // LANES):
        flat[taps + 2 + c : taps + 3 + c, :] = dog[:, c * LANES : (c + 1) * LANES]
    x = xs[...].astype(f32)
    scale = lax.rsqrt(jnp.mean(x * x, axis=-1, keepdims=True) + EPS)
    hx = halo[...].astype(f32)
    hscale = lax.rsqrt(jnp.mean(hx * hx, axis=-1, keepdims=True) + EPS)
    peers = send_o.shape[0]
    qn, vn = kc // peers, vc // peers
    acc = None
    for ref, kern, lo, hi, n, at in (
        (wq, kq, 0, kc, qn, 0), (wk, kk, kc, 2 * kc, qn, qn), (wv, kv, 2 * kc, proj, vn, 2 * qn),
    ):
        dext = None
        for j in range(margin + 1):
            term = kern[j : j + 1, :] * pad[pl.ds(margin - j, total), lo:hi]
            dext = term if dext is None else dext + term
        part = nt(dext, ref[...])
        acc = part if acc is None else acc + part
        own = (dext[HALO:] * scale).T.astype(bf16)
        rim = (dext[:HALO] * hscale).astype(bf16)
        for e in range(peers):
            send_o[e, at : at + n, :] = own[e * n : (e + 1) * n]
            send_o[e, 2 * (qn + vn) : 2 * (qn + vn) + HALO, at : at + n] = rim[:, e * n : (e + 1) * n]
    dgate = dgate_i[...]
    own = (dgate.astype(f32) * scale).T.astype(bf16)
    fl = flat[...].astype(bf16)
    for e in range(peers):
        send_o[e, 2 * qn + vn : 2 * (qn + vn), :] = own[e * vn : (e + 1) * vn]
        send_o[e, 2 * (qn + vn) + HALO :, :] = fl[e * HALO : (e + 1) * HALO]
    dsl = dsmall.astype(bf16)
    wsmall_o[...] = tn(dsl, normed[HALO:, :])[: wsmall_o.shape[0]]
    part_o[:HALO, :] = acc[:HALO].astype(bf16)
    part_o[HALO:, :] = (acc[HALO:] + nt(dgate, wg[...]) + nn(dsl, wsm[...])).astype(bf16)


def finish_body(heads, xs, gain, part, part_other, rim, rim_other, gres, wsmall, dfg, input_o, tail_o):
    size = xs.shape[0]
    x = xs[...].astype(f32)
    scale = lax.rsqrt(jnp.mean(x * x, axis=-1, keepdims=True) + EPS)
    normal = x * scale
    g = part[HALO:, :].astype(f32) + part_other[HALO:, :].astype(f32)
    edge = rim[...].astype(f32) + rim_other[...].astype(f32)
    g = jnp.concatenate([g[: size - HALO], g[size - HALO :] + edge], axis=0)
    tail_o[...] = jnp.zeros(tail_o.shape, f32)
    tail_o[: 2 * heads, :] = wsmall[: 2 * heads, :]
    tail_o[2 * heads : 2 * heads + 1, :] = col_sum(g * normal)
    tail_o[2 * heads + 1 : 2 * heads + 2, :] = dfg[...]
    d = g * gain[...]
    input_o[...] = gres[...] + scale * (d - normal * jnp.mean(d * normal, axis=-1, keepdims=True))


def gather_body(split_at, recv, xg, gain, tail, send_o, lhs):
    peers, _, size = recv.shape
    n = recv.shape[1] - 2 * HALO
    width = xg.shape[1]
    rows = width // peers
    flat = jnp.zeros((HALO, LANES), f32)
    edge, near = [], []
    for j in range(peers):
        lhs[:, j * size : (j + 1) * size] = recv[j, :n, :]
        edge.append(recv[j, n : n + HALO, :])
        flat = flat + recv[j, n + HALO :, :].astype(f32)
        near.append(xg[j * size - HALO : j * size, :] if j else jnp.zeros((HALO, width), bf16))
    acc = nn(lhs[...], xg[...])
    extra = tn(jnp.concatenate(edge, axis=0), jnp.concatenate(near, axis=0))
    mixed = n - split_at
    top = (acc[:mixed] + extra[:mixed]) * gain[...]
    rest = acc[mixed:] * gain[...]
    half = rows // 2
    wide = mixed == LANES
    if wide:
        top, rest = top.T.astype(bf16), rest.T.astype(bf16)
    else:
        fill = jnp.zeros((LANES - n, width), f32)
        top, half = jnp.concatenate([top, rest, fill], axis=0).T.astype(bf16), 0
    fl = flat.astype(bf16)
    small = tail[...].astype(bf16)
    for e in range(peers):
        lo = e * rows
        block = lo // LANES * LANES
        send_o[e, :rows, :] = top[lo : lo + rows]
        if wide:
            send_o[e, rows : rows + half, :] = jnp.concatenate(
                [rest[lo : lo + half], rest[lo + half : lo + rows]], axis=1
            )
        send_o[e, rows + half : rows + half + 2 * HALO, :] = small[:, block : block + LANES]
        send_o[e, rows + half + 2 * HALO :, :] = fl


def scatter_body(heads, qn, vn, margin, recv, side, q_o, k_o, v_o, g_o, wb_o, wa_o, ag_o, fg_o, cq_o, ck_o, cv_o, rate_o, bias_o, og_o):
    peers = recv.shape[0]
    rows = q_o.shape[0]
    wide = 2 * qn + vn == LANES
    half = rows // 2 if wide else 0
    low = jnp.zeros((2 * HALO, LANES), f32)
    lines = []
    for e in range(peers):
        top = recv[e, :rows, :].astype(f32)
        q_o[:, e * qn : (e + 1) * qn] = top[:, :qn]
        k_o[:, e * qn : (e + 1) * qn] = top[:, qn : 2 * qn]
        v_o[:, e * vn : (e + 1) * vn] = top[:, 2 * qn : 2 * qn + vn]
        if wide:
            rest = recv[e, rows : rows + half, :].astype(f32)
            g_o[:half, e * vn : (e + 1) * vn] = rest[:, :vn]
            g_o[half:, e * vn : (e + 1) * vn] = rest[:, vn:]
        else:
            g_o[:, e * vn : (e + 1) * vn] = top[:, 2 * qn + vn : 2 * (qn + vn)]
        low = low + recv[e, rows + half : rows + half + 2 * HALO, :].astype(f32)
        lines.append(recv[e, rows + half + 2 * HALO :, :].astype(f32))
    picked = low[:, :rows]
    for s in range(1, LANES // rows):
        picked = jnp.where(side[0:1, 0:1] == s, low[:, s * rows : (s + 1) * rows], picked)
    wb_o[...] = picked[:heads]
    wa_o[...] = picked[heads : 2 * heads]
    ag_o[...] = picked[2 * heads : 2 * heads + 1]
    fg_o[...] = picked[2 * heads + 1 : 2 * heads + 2]

    def line(at):
        return lines[at // HALO][at % HALO : at % HALO + 1]

    kb, vb = cq_o.shape[1] // LANES, cv_o.shape[1] // LANES
    blocks = 2 * kb + vb
    for j in range(margin + 1):
        for c in range(blocks):
            at = j * blocks + c
            ref, to = (cq_o, c) if c < kb else (ck_o, c - kb) if c < 2 * kb else (cv_o, c - 2 * kb)
            ref[j : j + 1, to * LANES : (to + 1) * LANES] = line(at)
    at = (margin + 1) * blocks
    rate_o[...] = line(at)[:, heads : 2 * heads]
    bias_o[...] = line(at + 1)[:, heads : 2 * heads]
    for c in range(og_o.shape[1] // LANES):
        og_o[:, c * LANES : (c + 1) * LANES] = line(at + 2 + c)


def ffn_grads_body(inputs, gg, gu, og, hid, out, buf, sems):
    width = inputs.shape[1]
    ff = gg.shape[1]
    step = buf.shape[2] // 3
    copies = []
    for i in range(width // LANES):
        slot = i % 2
        cols = slice(i * LANES, (i + 1) * LANES)
        if i >= 2:
            copies[i - 2].wait()
        lhs = inputs[:, cols]
        buf[slot, :, :ff] = tn(lhs, gg[...]).astype(bf16)
        buf[slot, :, step : step + ff] = tn(lhs, gu[...]).astype(bf16)
        buf[slot, :, 2 * step : 2 * step + ff] = tn(og[:, cols], hid[...]).astype(bf16)
        copy = pltpu.make_async_copy(buf.at[slot], out.at[cols, pl.ds(0, 3 * step)], sems.at[slot])
        copy.start()
        copies.append(copy)
    for copy in copies[-2:]:
        copy.wait()


def out_grads_body(low, gated, before, out, buf, sem):
    buf[...] = tn(low[...], gated[...]).astype(bf16)
    copy = pltpu.make_async_copy(
        buf, out.at[:, pl.ds(out.shape[1] - buf.shape[1], buf.shape[1])], sem.at[0]
    )
    copy.start()
    copy.wait()


def shift_along(block, axis, distance):
    devices = range(lax.axis_size(axis))
    route = [(i - distance, i) for i in devices if i - distance in devices]
    return lax.ppermute(block, axis, route)


def pair(part):
    if lax.axis_size("tensor") == 2:
        return part, lax.ppermute(part, "tensor", [(0, 1), (1, 0)])
    return lax.psum(part, "tensor"), jnp.zeros_like(part)


def swap(blocks):
    return lax.all_to_all(blocks, "dp", 0, 0, tiled=True)


def on_device(
    block_input, output_grad, attn_gain, w_query, w_key, w_value, conv_query, conv_key, conv_value,
    w_beta, w_alpha, a_log, dt_bias, w_gate_out, out_gain, w_out, ffn_gain, w_gate, w_up, w_down,
):
    size, width = block_input.shape
    heads = a_log.shape[0]
    key_dim = w_query.shape[1] // heads
    value_dim = w_value.shape[1] // heads
    margin = conv_query.shape[0] - 1
    peers = lax.axis_size("dp")
    slices = peers // heads
    kc, vc, gc, ff = w_query.shape[1], w_value.shape[1], w_gate_out.shape[1], w_gate.shape[1]
    proj = 2 * kc + vc
    dims = (heads, key_dim, value_dim)
    rows = width // peers

    halo = shift_along(block_input[-HALO:], "dp", 1)
    grad_hidden = jnp.dot(output_grad, w_down.T, preferred_element_type=f32).astype(bf16)
    rate, bias = a_log[None], dt_bias[None]
    again, fgain, ogain = attn_gain[None], ffn_gain[None], out_gain[None]

    normed, ext, gate_pre, small, cum, q, k, v, inv, p, w, u, wsm, send = call(
        functools.partial(front_body, *dims, margin, slices),
        [
            ((size + HALO, width), bf16), ((size + HALO, proj), bf16), ((size, gc), f32),
            ((size, LANES), f32), ((size, LANES), f32), ((size, kc), f32), ((size, kc), f32), ((size, vc), f32),
            ((size, heads * size), bf16), ((size, heads * size), bf16), ((size, kc), bf16),
            ((size, vc), f32), ((LANES, width), bf16),
            ((peers, key_dim + value_dim // slices, key_dim), bf16),
        ],
        block_input, halo, again, w_query, w_key, w_value, w_gate_out, w_beta.T, w_alpha.T,
        conv_query, conv_key, conv_value, rate, bias,
        scratch=[pltpu.VMEM((size + HALO, proj), f32)],
    )
    maps = swap(send)
    maps, late_input = lax.optimization_barrier((maps, block_input))
    everyone = lax.all_gather(late_input, "dp", axis=0, tiled=True)
    piece = (peers, value_dim // slices, key_dim)
    (entry,) = call(functools.partial(scan_fwd_body, key_dim), [(piece, bf16)], maps)
    st = swap(entry).reshape(heads, value_dim, key_dim)
    stored, mixed, gated, mix_part = call(
        functools.partial(mix_body, *dims),
        [((size, vc), bf16), ((size, vc), f32), ((size, vc), bf16), ((size, width), bf16)],
        st, u, w, p, q, cum, gate_pre, ogain, w_out,
    )
    mix_pair = pair(mix_part)
    ffn_input, hidden, gga, gua, back_part, down_part = call(
        ffn_body,
        [((size, width), bf16), ((size, ff), bf16), ((size, ff), bf16), ((size, ff), bf16),
         ((size, width), bf16), ((size, width), bf16)],
        block_input, *mix_pair, fgain, w_gate, w_up, w_down, grad_hidden,
    )
    back_pair = pair(back_part)
    step = -(-ff // LANES) * LANES
    total = 3 * step + gc
    early = pl.pallas_call(
        ffn_grads_body,
        out_shape=jax.ShapeDtypeStruct((width, total), bf16),
        out_specs=pl.BlockSpec(memory_space=pl.ANY),
        scratch_shapes=[pltpu.VMEM((2, LANES, 3 * step), bf16), pltpu.SemaphoreType.DMA((2,))],
        compiler_params=pltpu.CompilerParams(vmem_limit_bytes=60000 * 1024),
    )(ffn_input, gga, gua, output_grad, hidden)
    back_pair, early = lax.optimization_barrier((back_pair, early))
    gres, glow, dfg, dmix, pdo, dgate, dog, send_back = call(
        functools.partial(turn_body, *dims, slices),
        [((size, width), f32), ((size, width), bf16), ((1, width), f32), ((size, vc), bf16),
         ((size, vc), f32), ((size, gc), bf16), ((1, value_dim), f32), (piece, bf16)],
        block_input, *mix_pair, *back_pair, output_grad, fgain, w_out, mixed, gate_pre, ogain, p, w, q, cum,
    )
    early = pl.pallas_call(
        out_grads_body,
        out_shape=jax.ShapeDtypeStruct((width, total), bf16),
        in_specs=[pl.BlockSpec(memory_space=pltpu.VMEM)] * 2 + [pl.BlockSpec(memory_space=pl.ANY)],
        out_specs=pl.BlockSpec(memory_space=pl.ANY),
        input_output_aliases={2: 0},
        scratch_shapes=[pltpu.VMEM((width, gc), bf16), pltpu.SemaphoreType.DMA((1,))],
        compiler_params=pltpu.CompilerParams(vmem_limit_bytes=60000 * 1024),
    )(glow, gated, early)
    send_back, early = lax.optimization_barrier((send_back, early))
    first = lax.psum_scatter(early, "dp", scatter_dimension=0, tiled=True).astype(f32)
    local = swap(send_back)
    (exits,) = call(functools.partial(scan_bwd_body, key_dim), [(piece, bf16)], maps, local)
    dst = swap(exits).reshape(heads, value_dim, key_dim)
    down_pair = pair(down_part)
    dog_pair = pair(dog)

    qn, vn = kc // peers, vc // peers
    share = 2 * (qn + vn)
    send, part, wsmall = call(
        functools.partial(back_body, *dims, margin),
        [((peers, share + 2 * HALO, size), bf16), ((size + HALO, width), bf16), ((2 * HALO, width), f32)],
        dst, st, block_input, halo, normed, ext, conv_query, conv_key, conv_value,
        q, k, v, inv, p, stored, dmix, pdo, dgate,
        small, cum, rate, bias, *dog_pair, w_query, w_key, w_value, w_gate_out, wsm,
        scratch=[
            pltpu.VMEM((size + HALO, proj), f32), pltpu.VMEM((size + 2 * HALO, proj), f32),
            pltpu.VMEM((peers * HALO, LANES), f32),
        ],
    )
    rim_pair = pair(shift_along(part[:HALO], "dp", -1))
    part_pair = pair(part)
    recv = swap(send)
    input_grad, tail = call(
        functools.partial(finish_body, heads),
        [((size, width), f32), ((2 * HALO, width), f32)],
        block_input, again, *part_pair, *rim_pair, gres, wsmall, dfg,
    )
    wide = 2 * qn + vn == LANES
    packed = rows + (rows // 2 if wide else 0) + 3 * HALO
    (send,) = call(
        functools.partial(gather_body, vn), [((peers, packed, LANES), bf16)], recv, everyone, again, tail,
        scratch=[pltpu.VMEM((share, peers * size), bf16)],
    )
    recv = swap(send)
    side = jnp.full((1, 1), lax.axis_index("dp") % (LANES // rows), jnp.int32)
    gq, gk, gv, gg, gwb, gwa, gag, gfg, gcq, gck, gcv, grate, gbias, gog = call(
        functools.partial(scatter_body, heads, qn, vn, margin),
        [((rows, kc), f32), ((rows, kc), f32), ((rows, vc), f32), ((rows, gc), f32),
         ((heads, rows), f32), ((heads, rows), f32), ((1, rows), f32), ((1, rows), f32),
         ((margin + 1, kc), f32), ((margin + 1, kc), f32), ((margin + 1, vc), f32),
         ((1, heads), f32), ((1, heads), f32), ((1, value_dim), f32)],
        recv, side,
    )
    block_output = (
        block_input.astype(f32) + (mix_pair[0].astype(f32) + mix_pair[1].astype(f32))
        + (down_pair[0].astype(f32) + down_pair[1].astype(f32))
    )
    return (
        block_output, input_grad, gag[0], gq, gk, gv, gcq, gck, gcv, gwb.T, gwa.T,
        grate[0], gbias[0], gg, gog[0],
        first[:, 3 * step :].T, gfg[0], first[:, :ff], first[:, step : step + ff], first[:, 2 * step : 2 * step + ff].T,
    )


def solution(mesh):
    rows, cols, whole = P("dp", None), P(None, "tensor"), P()
    heads, high = P("tensor"), P("tensor", None)
    in_specs = (
        rows, rows, whole, cols, cols, cols, cols, cols, cols, cols, cols, heads, heads,
        cols, whole, high, whole, cols, cols, high,
    )
    both, crossed, dp = P("dp", "tensor"), P("tensor", "dp"), P("dp")
    out_specs = (
        rows, rows, dp, both, both, both, cols, cols, cols, both, both, heads, heads,
        both, whole, crossed, dp, both, both, crossed,
    )
    return jax.shard_map(
        on_device, mesh=mesh, in_specs=in_specs, out_specs=out_specs, check_vma=False
    )
```

```python
import functools

import jax
import jax.numpy as jnp
from jax import lax
from jax.experimental import pallas as pl
from jax.experimental.pallas import tpu as pltpu
from jax.sharding import PartitionSpec as P

EPS = 1e-06
LANES = 128
HALO = 8
f32 = jnp.float32
bf16 = jnp.bfloat16


def nn(a, b):
    dims = (((1,), (0,)), ((), ()))
    return lax.dot_general(a.astype(bf16), b.astype(bf16), dims, preferred_element_type=f32)


def nt(a, b):
    dims = (((1,), (1,)), ((), ()))
    return lax.dot_general(a.astype(bf16), b.astype(bf16), dims, preferred_element_type=f32)


def tn(a, b):
    dims = (((0,), (0,)), ((), ()))
    return lax.dot_general(a.astype(bf16), b.astype(bf16), dims, preferred_element_type=f32)


def exact(a, b):
    dims = (((1,), (0,)), ((), ()))
    return lax.dot_general(a, b, dims, preferred_element_type=f32, precision=lax.Precision.HIGHEST)


def row_sum(a):
    return jnp.sum(a, axis=-1, keepdims=True)


def col_sum(a):
    return jnp.sum(a, axis=0, keepdims=True)


def iotas(size):
    return (
        lax.broadcasted_iota(jnp.int32, (size, size), 0),
        lax.broadcasted_iota(jnp.int32, (size, size), 1),
    )


def exact3(a, b):
    (ah, al), (bh, bl) = a, b
    return nn(ah, bh) + (nn(ah, bl) + nn(al, bh))


def unit_lower_inverses(lows):
    size = lows[0].shape[0]
    rows, cols = iotas(size)

    def same(shift):
        return lax.shift_right_logical(rows, shift) == lax.shift_right_logical(cols, shift)

    def each(f, *lists):
        return [f(*items) for items in zip(*lists, strict=True)]

    eye = jnp.where(rows == cols, 1.0, 0.0).astype(f32)
    shift = 3
    diags = [jnp.where(same(shift), low, 0.0) for low in lows]
    invs = [eye - diag for diag in diags]
    powers = each(split, diags)
    for _ in range(shift - 1):
        powers = each(split, each(exact3, powers, powers))
        invs = each(lambda x, y: x + y, invs, each(exact3, each(split, invs), powers))
    while (1 << shift) < size:
        keep = same(shift + 1) & jnp.logical_not(same(shift))
        offs = [split(jnp.where(keep, low, 0.0)) for low in lows]
        halves = each(split, invs)
        inner = each(split, each(exact3, offs, halves))
        invs = each(lambda x, y: x - y, invs, each(exact3, halves, inner))
        shift += 1
    return invs


class Arriving:
    def __init__(self, source, target, sem):
        self.copy = pltpu.make_async_copy(source, target, sem)
        self.target, self.shape, self.waiting = target, target.shape, True
        self.copy.start()

    def ready(self):
        if self.waiting:
            self.copy.wait()
            self.waiting = False
        return self.target

    def __getitem__(self, at):
        return self.ready()[at]


def call(body, outs, *args, scratch=(), raw=(), alias=None):
    anywhere = pl.BlockSpec(memory_space=pl.ANY)
    count = len(args)

    def streams(i):
        shape = args[i].shape
        return i not in raw and len(shape) > 1 and shape[-2] % HALO == 0 and shape[-1] % LANES == 0

    moved = [i for i in range(count) if streams(i)]
    alias = alias or {}
    held = set(alias.values())

    def kernel(*refs):
        own = len(refs) - len(moved) - 1
        sems = refs[-1]
        given = list(refs[:own])
        late = []
        for n, i in enumerate(moved):
            given[i] = Arriving(refs[i], refs[own + n], sems.at[n])
            late.append(given[i])
        body(*given)
        for item in late:
            item.ready()

    return pl.pallas_call(
        kernel,
        name=getattr(body, "func", body).__name__,
        out_shape=[jax.ShapeDtypeStruct(s, d) for s, d in outs],
        in_specs=[
            anywhere if i in raw or i in moved else pl.BlockSpec(memory_space=pltpu.VMEM)
            for i in range(count)
        ],
        out_specs=[
            anywhere if i in held else pl.BlockSpec(memory_space=pltpu.VMEM)
            for i in range(len(outs))
        ],
        input_output_aliases=alias,
        scratch_shapes=[
            *scratch,
            *(pltpu.VMEM(args[i].shape, args[i].dtype) for i in moved),
            pltpu.SemaphoreType.DMA((len(moved),)),
        ],
        compiler_params=pltpu.CompilerParams(vmem_limit_bytes=60000 * 1024),
    )(*args)


def in_step(steps):
    steps = list(steps)
    while steps:
        steps = [step for step in steps if next(step, True) is None]


def softplus(a):
    return jnp.maximum(a, 0.0) + jnp.log1p(jnp.exp(-jnp.abs(a)))


def place(row, heads):
    lane = lax.broadcasted_iota(jnp.int32, (1, LANES), 1)
    out = jnp.zeros((1, LANES), f32)
    for h in range(heads):
        out = jnp.where(lane == heads + h, row[0:1, h : h + 1], out)
    return out


def silu_parts(a):
    s = jax.nn.sigmoid(a)
    return a * s, s * (1.0 + a * (1.0 - s))


def conv_pre(ext, kern, base, cols, size, margin):
    total = None
    for j in range(margin + 1):
        tap = kern[j : j + 1, cols.start - base : cols.stop - base]
        term = tap * ext[pl.ds(HALO - margin + j, size), cols]
        total = term if total is None else total + term
    return total


def decay_terms(small, rate, bias, heads):
    size = small.shape[0]
    rows, cols = iotas(size)
    log_decay = -jnp.exp(rate) * softplus(small + bias)
    tril = jnp.where(rows >= cols, 1.0, 0.0).astype(f32)
    cum = exact(tril, log_decay)
    return log_decay, cum


def head_decay(cum, cum_t, at, rows, cols):
    g = cum[:, at : at + 1]
    spread = g - cum_t[at : at + 1, :]
    keep = rows >= cols
    return g, jnp.where(keep, jnp.exp(jnp.where(keep, spread, 0.0)), 0.0)


def front_body(
    heads, key_dim, value_dim, margin, slices,
    xs, halo, gain, wq, wk, wv, wg, wb, wa, kq, kk, kv, rate, bias,
    normed_o, ext_o, gate_o, small_o, cum_o, q_o, k_o, v_o, inv_o, p_o, w_o, u_o, wsm_o, send_o, ext,
):
    size = xs.shape[0]
    for ref, lo, hi in ((halo, 0, HALO), (xs, HALO, HALO + size)):
        x = ref[...].astype(f32)
        scale = lax.rsqrt(jnp.mean(x * x, axis=-1, keepdims=True) + EPS)
        normed_o[lo:hi, :] = (x * scale * gain[...]).astype(bf16)
    normed = normed_o[...]
    wsm_o[...] = jnp.zeros(wsm_o.shape, bf16)
    wsm_o[:heads, :] = wb[...]
    wsm_o[heads : 2 * heads, :] = wa[...]
    kc, vc = heads * key_dim, heads * value_dim
    for ref, lo, hi in ((wq, 0, kc), (wk, kc, 2 * kc), (wv, 2 * kc, 2 * kc + vc)):
        part = nn(normed, ref[...]).astype(bf16)
        ext_o[:, lo:hi] = part
        ext[:, lo:hi] = part.astype(f32)
    own = normed[HALO:]
    small = nt(own, wsm_o[...])
    small_o[...] = small
    beta_all = jax.nn.sigmoid(small)
    log_decay, cum = decay_terms(small, place(rate, heads), place(bias, heads), heads)
    cum_o[...] = cum
    cum_t = cum.T
    rows, cols = iotas(size)
    width = value_dim // slices
    kept = [None] * heads

    def start(h):
        ks = slice(h * key_dim, (h + 1) * key_dim)
        vs = slice(h * value_dim, (h + 1) * value_dim)
        kh = jax.nn.silu(conv_pre(ext, kk, kc, slice(kc + ks.start, kc + ks.stop), size, margin))
        qh = jax.nn.silu(conv_pre(ext, kq, 0, ks, size, margin))
        yield
        k = kh * lax.rsqrt(row_sum(kh * kh) + EPS)
        q = qh * (lax.rsqrt(row_sum(qh * qh) + EPS) * key_dim**-0.5)
        q_o[:, ks] = q
        k_o[:, ks] = k
        dots = nt(jnp.concatenate([k, q], axis=0), k)
        yield
        beta = beta_all[:, h : h + 1]
        g, decay = head_decay(cum, cum_t, heads + h, rows, cols)
        low = jnp.where(rows > cols, beta * decay * dots[:size], 0.0)
        p_o[:, h * size : (h + 1) * size] = (dots[size:] * decay).astype(bf16)
        kept[h] = (ks, vs, beta, g, low)
        yield
        v_o[:, vs] = jax.nn.silu(conv_pre(ext, kv, 2 * kc, slice(2 * kc + vs.start, 2 * kc + vs.stop), size, margin))

    in_step(start(h) for h in range(heads))
    invs = unit_lower_inverses([item[-1] for item in kept])
    solved_all = []
    for (ks, vs, beta, g, _), inv in zip(kept, invs, strict=True):
        rhs = jnp.concatenate([beta * v_o[:, vs], (beta * jnp.exp(g)) * k_o[:, ks]], axis=1)
        solved_all.append(nn(inv, rhs))
    for h, (ks, vs, beta, g, _) in enumerate(kept):
        inv_o[:, h * size : (h + 1) * size] = invs[h].astype(bf16)
        last = cum[size - 1 : size, heads + h : heads + h + 1]
        solved = solved_all[h]
        kt = k_o[:, ks] * jnp.exp(last - g)
        maps = tn(solved, kt)
        er, ec = iotas(key_dim)
        at = jnp.where(er == ec, jnp.exp(last), 0.0) - maps[value_dim:]
        bt = maps[:value_dim].astype(bf16)
        at = at.astype(bf16)
        for s in range(slices):
            send_o[h * slices + s, :key_dim, :] = at
            send_o[h * slices + s, key_dim:, :] = bt[s * width : (s + 1) * width]
        w_o[:, ks] = solved[:, value_dim:].astype(bf16)
        u_o[:, vs] = solved[:, :value_dim]
    gate_o[...] = nn(own, wg[...])


def split(a):
    hi = a.astype(bf16)
    return hi, (a - hi.astype(f32)).astype(bf16)


def scan_fwd_body(key_dim, maps, out):
    n, rows, _ = maps.shape
    state = jnp.zeros((rows - key_dim, key_dim), f32)
    for j in range(n):
        out[j] = state.astype(bf16)
        if j < n - 1:
            hi, lo = split(state)
            a = maps[j, :key_dim, :]
            state = nn(hi, a) + nn(lo, a) + maps[j, key_dim:, :].astype(f32)


def scan_bwd_body(key_dim, maps, local, out):
    n = maps.shape[0]
    state = jnp.zeros(local.shape[1:], f32)
    for j in range(n - 1, -1, -1):
        out[j] = state.astype(bf16)
        if j > 0:
            hi, lo = split(state)
            a = maps[j, :key_dim, :]
            state = nt(hi, a) + nt(lo, a) + local[j].astype(f32)


def mix_body(
    heads, key_dim, value_dim,
    st, u, w, p, q, cum, gate, gain, wo,
    stored_o, mixed_o, gated_o, part_o,
):
    size = u.shape[0]

    def one(h):
        ks = slice(h * key_dim, (h + 1) * key_dim)
        vs = slice(h * value_dim, (h + 1) * value_dim)
        both = nt(jnp.concatenate([w[:, ks], q[:, ks].astype(bf16)], axis=0), st[h])
        yield
        stored = (u[:, vs] - both[:size]).astype(bf16)
        stored_o[:, vs] = stored
        inner = nn(p[:, h * size : (h + 1) * size], stored)
        yield
        eg = jnp.exp(cum[:, heads + h : heads + h + 1])
        mixed = eg * both[size:] + inner
        mixed_o[:, vs] = mixed
        scale = lax.rsqrt(jnp.mean(mixed * mixed, axis=-1, keepdims=True) + EPS)
        gated_o[:, vs] = (mixed * scale * gain[...] * jax.nn.silu(gate[:, vs])).astype(bf16)

    in_step(one(h) for h in range(heads))
    part_o[...] = nn(gated_o[...], wo[...]).astype(bf16)


def ffn_body(x, mine, other, gain, w_gate, w_up, w_down, grad_hidden, input_o, hid_o, gg_o, gu_o, back_o, down_o):
    r = x[...].astype(f32) + (mine[...].astype(f32) + other[...].astype(f32))
    scale = lax.rsqrt(jnp.mean(r * r, axis=-1, keepdims=True) + EPS)
    ffn_in = (r * scale * gain[...]).astype(bf16)
    input_o[...] = ffn_in
    gate = nn(ffn_in, w_gate[...])
    up = nn(ffn_in, w_up[...])
    sig = jax.nn.sigmoid(gate)
    gh = grad_hidden[...].astype(f32)
    gu_o[...] = (gh * gate * sig).astype(bf16)
    gg_o[...] = (gh * up * sig * (1.0 + gate * (1.0 - sig))).astype(bf16)
    hid_o[...] = (gate * sig * up).astype(bf16)
    back_o[...] = (nt(gg_o[...], w_gate[...]) + nt(gu_o[...], w_up[...])).astype(bf16)
    down_o[...] = nn(hid_o[...], w_down[...]).astype(bf16)


def turn_body(
    heads, key_dim, value_dim, slices,
    x, mine, other, back_mine, back_other, og, ffn_gain, wo, gated, mixed, gate, out_gain, p, w, q, cum, _,
    gres_o, dfg_o, dmix_o, pdo_o, dgate_o, dog_o, send_o, grads_o, buf, sem,
):
    r = x[...].astype(f32) + (mine[...].astype(f32) + other[...].astype(f32))
    scale = lax.rsqrt(jnp.mean(r * r, axis=-1, keepdims=True) + EPS)
    b = back_mine[...].astype(f32) + back_other[...].astype(f32)
    normal = r * scale
    dfg_o[...] = col_sum(b * normal)
    d = b * ffn_gain[...]
    gres = og[...].astype(f32) + scale * (d - normal * jnp.mean(d * normal, axis=-1, keepdims=True))
    gres_o[...] = gres
    low = gres.astype(bf16)
    dgated = nt(low, wo[...])
    buf[...] = tn(low, gated[...]).astype(bf16)
    copy = pltpu.make_async_copy(
        buf, grads_o.at[:, pl.ds(grads_o.shape[1] - buf.shape[1], buf.shape[1])], sem.at[0]
    )
    copy.start()
    size = r.shape[0]
    width = value_dim // slices
    dogs = [None] * heads

    def one(h):
        ks = slice(h * key_dim, (h + 1) * key_dim)
        vs = slice(h * value_dim, (h + 1) * value_dim)
        m = mixed[:, vs]
        scale_h = lax.rsqrt(jnp.mean(m * m, axis=-1, keepdims=True) + EPS)
        n = m * scale_h
        act, dact = silu_parts(gate[:, vs])
        dg = dgated[:, vs]
        dgate_o[:, vs] = (dg * (n * out_gain[...]) * dact).astype(bf16)
        dn = dg * act
        dogs[h] = col_sum(dn * n)
        dn = dn * out_gain[...]
        dm = scale_h * (dn - n * jnp.mean(dn * n, axis=-1, keepdims=True))
        dm = dm.astype(bf16)
        dmix_o[:, vs] = dm
        pdo = tn(p[:, h * size : (h + 1) * size], dm)
        yield
        pdo_o[:, vs] = pdo
        eg = jnp.exp(cum[:, heads + h : heads + h + 1])
        left = jnp.concatenate([dm, -pdo.astype(bf16)], axis=0)
        right = jnp.concatenate([(q[:, ks] * eg).astype(bf16), w[:, ks]], axis=0)
        local = tn(left, right).astype(bf16)
        yield
        for s in range(slices):
            send_o[h * slices + s] = local[s * width : (s + 1) * width]

    in_step(one(h) for h in range(heads))
    dog_o[...] = sum(dogs[1:], dogs[0])
    copy.wait()


def back_body(
    heads, key_dim, value_dim, margin,
    dst, st, xs, halo, normed, ext_i, kq, kk, kv, q_i, k_i, v_i, inv_i, p_i, stored_i, dmix_i, pdo_i, dgate_i,
    small, cum_i, rate_i, bias_i, dog_mine, dog_other, wq, wk, wv, wg, wsm,
    send_o, part_o, wsmall_o, ext, pad, flat,
):
    size = q_i.shape[0]
    total = size + HALO
    kc, vc = heads * key_dim, heads * value_dim
    proj = 2 * kc + vc
    ext[...] = ext_i[...].astype(f32)
    pad[:HALO, :] = jnp.zeros((HALO, proj), f32)
    pad[HALO + size :, :] = jnp.zeros((HALO, proj), f32)
    sm = small[...]
    cum = cum_i[...]
    rate, bias = place(rate_i, heads), place(bias_i, heads)
    log_decay = -jnp.exp(rate) * softplus(sm + bias)
    cum_t = cum.T
    beta_all = jax.nn.sigmoid(sm)
    rows, cols = iotas(size)
    lane = lax.broadcasted_iota(jnp.int32, (size, LANES), 1)
    end_row = lax.broadcasted_iota(jnp.int32, (size, 1), 0) == size - 1
    dcums, dbetas = [None] * heads, [None] * heads

    blocks = proj // LANES
    flat[...] = jnp.zeros(flat.shape, f32)

    def conv_back(dy, kern, base, lo, hi):
        cs = slice(lo, hi)
        pre = conv_pre(ext, kern, base, cs, size, margin)
        _, dact = silu_parts(pre)
        dpre = dy * dact
        pad[pl.ds(HALO, size), cs] = dpre
        for j in range(margin + 1):
            tap = col_sum(dpre * ext[pl.ds(HALO - margin + j, size), cs])
            for c in range((hi - lo) // LANES):
                at = j * blocks + lo // LANES + c
                flat[at : at + 1, :] = tap[:, c * LANES : (c + 1) * LANES]

    def one(h):
        ks = slice(h * key_dim, (h + 1) * key_dim)
        vs = slice(h * value_dim, (h + 1) * value_dim)
        ps = slice(h * size, (h + 1) * size)
        q, k, v = q_i[:, ks], k_i[:, ks], v_i[:, vs]
        stored, do = stored_i[:, vs], dmix_i[:, vs]
        s, ds = st[h], dst[h]
        beta = beta_all[:, h : h + 1]
        g, decay = head_decay(cum, cum_t, heads + h, rows, cols)
        eg = jnp.exp(g)
        last = cum[size - 1 : size, heads + h : heads + h + 1]
        kt = k * jnp.exp(last - g)
        kl, ql = k.astype(bf16), q.astype(bf16)
        states = nt(jnp.concatenate([kl, ql], axis=0), s)
        dstored = pdo_i[:, vs] + nt(kt, ds)
        yield
        dr = tn(inv_i[:, ps], dstored)
        dkt = nn(stored, ds)
        dots = nt(kl, kl)
        yield
        drl = dr.astype(bf16)
        k_s, q_s = states[:size], states[size:]
        both = jnp.concatenate([drl, do], axis=0)
        inner = nt(both, stored)
        back = nn(both, s)
        yield
        scaled = decay * dots
        dlow = jnp.where(rows > cols, -inner[:size], 0.0)
        dp = jnp.where(rows >= cols, inner[size:], 0.0)
        dv = beta * dr
        spread = dlow * (beta * scaled) + dp * p_i[:, ps].astype(f32)
        dqk = (dp * decay).astype(bf16)
        dkk = dlow * (beta * decay)
        left = jnp.concatenate([dqk, (dkk + dkk.T).astype(bf16)], axis=0)
        on_k = nn(left, kl)
        on_q = tn(dqk, ql)
        yield
        dq = on_k[:size] + eg * back[size:]
        tail_part = row_sum(dkt * kt)
        dk = on_k[size:] + on_q - (beta * eg) * back[:size] + jnp.exp(last - g) * dkt
        dbeta = row_sum(dr * (v - eg * k_s)) + row_sum(dlow * scaled)
        dg = row_sum(spread) - row_sum(spread.T) - tail_part
        dg = dg + eg * row_sum(do.astype(f32) * q_s) - (beta * eg) * row_sum(dr * k_s)
        carry = col_sum(row_sum(s.astype(f32) * ds.astype(f32)))
        at_end = col_sum(tail_part) + jnp.exp(last) * carry
        dg = dg + jnp.where(end_row, at_end, 0.0)
        dcums[h] = jnp.where(lane == heads + h, dg, 0.0)
        dbetas[h] = jnp.where(lane == h, dbeta, 0.0)
        yield
        qh = jax.nn.silu(conv_pre(ext, kq, 0, ks, size, margin))
        rq = lax.rsqrt(row_sum(qh * qh) + EPS)
        unit = qh * rq
        dqn = dq * key_dim**-0.5
        conv_back(rq * (dqn - unit * row_sum(dqn * unit)), kq, 0, ks.start, ks.stop)
        kh = jax.nn.silu(conv_pre(ext, kk, kc, slice(kc + ks.start, kc + ks.stop), size, margin))
        rk = lax.rsqrt(row_sum(kh * kh) + EPS)
        conv_back(rk * (dk - k * row_sum(dk * k)), kk, kc, kc + ks.start, kc + ks.stop)
        conv_back(dv, kv, 2 * kc, 2 * kc + vs.start, 2 * kc + vs.stop)

    in_step(one(h) for h in range(heads))
    dcum, dbeta_all = sum(dcums[1:], dcums[0]), sum(dbetas[1:], dbetas[0])
    triu = jnp.where(rows <= cols, 1.0, 0.0).astype(f32)
    dlog = exact(triu, dcum)
    dalpha = dlog * (-jnp.exp(rate)) * jax.nn.sigmoid(sm + bias)
    dsmall = dalpha + dbeta_all * beta_all * (1.0 - beta_all)
    taps = (margin + 1) * blocks
    flat[taps : taps + 1, :] = col_sum(dlog * log_decay)
    flat[taps + 1 : taps + 2, :] = col_sum(dalpha)
    dog = dog_mine[...] + dog_other[...]
    for c in range(value_dim // LANES):
        flat[taps + 2 + c : taps + 3 + c, :] = dog[:, c * LANES : (c + 1) * LANES]
    x = xs[...].astype(f32)
    scale = lax.rsqrt(jnp.mean(x * x, axis=-1, keepdims=True) + EPS)
    hx = halo[...].astype(f32)
    hscale = lax.rsqrt(jnp.mean(hx * hx, axis=-1, keepdims=True) + EPS)
    peers = send_o.shape[0]
    qn, vn = kc // peers, vc // peers
    acc = None
    for ref, kern, lo, hi, n, at in (
        (wq, kq, 0, kc, qn, 0), (wk, kk, kc, 2 * kc, qn, qn), (wv, kv, 2 * kc, proj, vn, 2 * qn),
    ):
        dext = None
        for j in range(margin + 1):
            term = kern[j : j + 1, :] * pad[pl.ds(margin - j, total), lo:hi]
            dext = term if dext is None else dext + term
        part = nt(dext, ref[...])
        acc = part if acc is None else acc + part
        own = (dext[HALO:] * scale).T.astype(bf16)
        rim = (dext[:HALO] * hscale).astype(bf16)
        for e in range(peers):
            send_o[e, at : at + n, :] = own[e * n : (e + 1) * n]
            send_o[e, 2 * (qn + vn) : 2 * (qn + vn) + HALO, at : at + n] = rim[:, e * n : (e + 1) * n]
    dgate = dgate_i[...]
    own = (dgate.astype(f32) * scale).T.astype(bf16)
    fl = flat[...].astype(bf16)
    for e in range(peers):
        send_o[e, 2 * qn + vn : 2 * (qn + vn), :] = own[e * vn : (e + 1) * vn]
        send_o[e, 2 * (qn + vn) + HALO :, :] = fl[e * HALO : (e + 1) * HALO]
    dsl = dsmall.astype(bf16)
    wsmall_o[...] = tn(dsl, normed[HALO:, :])[: wsmall_o.shape[0]]
    part_o[:HALO, :] = acc[:HALO].astype(bf16)
    part_o[HALO:, :] = (acc[HALO:] + nt(dgate, wg[...]) + nn(dsl, wsm[...])).astype(bf16)


def finish_body(heads, xs, gain, part, part_other, rim, rim_other, gres, wsmall, dfg, input_o, tail_o):
    size = xs.shape[0]
    x = xs[...].astype(f32)
    scale = lax.rsqrt(jnp.mean(x * x, axis=-1, keepdims=True) + EPS)
    normal = x * scale
    g = part[HALO:, :].astype(f32) + part_other[HALO:, :].astype(f32)
    edge = rim[...].astype(f32) + rim_other[...].astype(f32)
    g = jnp.concatenate([g[: size - HALO], g[size - HALO :] + edge], axis=0)
    tail_o[...] = jnp.zeros(tail_o.shape, f32)
    tail_o[: 2 * heads, :] = wsmall[: 2 * heads, :]
    tail_o[2 * heads : 2 * heads + 1, :] = col_sum(g * normal)
    tail_o[2 * heads + 1 : 2 * heads + 2, :] = dfg[...]
    d = g * gain[...]
    input_o[...] = gres[...] + scale * (d - normal * jnp.mean(d * normal, axis=-1, keepdims=True))


def gather_body(split_at, recv, xg, gain, tail, send_o, lhs):
    peers, _, size = recv.shape
    n = recv.shape[1] - 2 * HALO
    width = xg.shape[1]
    rows = width // peers
    flat = jnp.zeros((HALO, LANES), f32)
    edge, near = [], []
    for j in range(peers):
        lhs[:, j * size : (j + 1) * size] = recv[j, :n, :]
        edge.append(recv[j, n : n + HALO, :])
        flat = flat + recv[j, n + HALO :, :].astype(f32)
        near.append(xg[j * size - HALO : j * size, :] if j else jnp.zeros((HALO, width), bf16))
    acc = nn(lhs[...], xg[...])
    extra = tn(jnp.concatenate(edge, axis=0), jnp.concatenate(near, axis=0))
    mixed = n - split_at
    top = (acc[:mixed] + extra[:mixed]) * gain[...]
    rest = acc[mixed:] * gain[...]
    half = rows // 2
    wide = mixed == LANES
    if wide:
        top, rest = top.T.astype(bf16), rest.T.astype(bf16)
    else:
        fill = jnp.zeros((LANES - n, width), f32)
        top, half = jnp.concatenate([top, rest, fill], axis=0).T.astype(bf16), 0
    fl = flat.astype(bf16)
    small = tail[...].astype(bf16)
    for e in range(peers):
        lo = e * rows
        block = lo // LANES * LANES
        send_o[e, :rows, :] = top[lo : lo + rows]
        if wide:
            send_o[e, rows : rows + half, :] = jnp.concatenate(
                [rest[lo : lo + half], rest[lo + half : lo + rows]], axis=1
            )
        send_o[e, rows + half : rows + half + 2 * HALO, :] = small[:, block : block + LANES]
        send_o[e, rows + half + 2 * HALO :, :] = fl


def scatter_body(heads, qn, vn, margin, recv, side, q_o, k_o, v_o, g_o, wb_o, wa_o, ag_o, fg_o, cq_o, ck_o, cv_o, rate_o, bias_o, og_o):
    peers = recv.shape[0]
    rows = q_o.shape[0]
    wide = 2 * qn + vn == LANES
    half = rows // 2 if wide else 0
    low = jnp.zeros((2 * HALO, LANES), f32)
    lines = []
    for e in range(peers):
        top = recv[e, :rows, :].astype(f32)
        q_o[:, e * qn : (e + 1) * qn] = top[:, :qn]
        k_o[:, e * qn : (e + 1) * qn] = top[:, qn : 2 * qn]
        v_o[:, e * vn : (e + 1) * vn] = top[:, 2 * qn : 2 * qn + vn]
        if wide:
            rest = recv[e, rows : rows + half, :].astype(f32)
            g_o[:half, e * vn : (e + 1) * vn] = rest[:, :vn]
            g_o[half:, e * vn : (e + 1) * vn] = rest[:, vn:]
        else:
            g_o[:, e * vn : (e + 1) * vn] = top[:, 2 * qn + vn : 2 * (qn + vn)]
        low = low + recv[e, rows + half : rows + half + 2 * HALO, :].astype(f32)
        lines.append(recv[e, rows + half + 2 * HALO :, :].astype(f32))
    picked = low[:, :rows]
    for s in range(1, LANES // rows):
        picked = jnp.where(side[0:1, 0:1] == s, low[:, s * rows : (s + 1) * rows], picked)
    wb_o[...] = picked[:heads]
    wa_o[...] = picked[heads : 2 * heads]
    ag_o[...] = picked[2 * heads : 2 * heads + 1]
    fg_o[...] = picked[2 * heads + 1 : 2 * heads + 2]

    def line(at):
        return lines[at // HALO][at % HALO : at % HALO + 1]

    kb, vb = cq_o.shape[1] // LANES, cv_o.shape[1] // LANES
    blocks = 2 * kb + vb
    for j in range(margin + 1):
        for c in range(blocks):
            at = j * blocks + c
            ref, to = (cq_o, c) if c < kb else (ck_o, c - kb) if c < 2 * kb else (cv_o, c - 2 * kb)
            ref[j : j + 1, to * LANES : (to + 1) * LANES] = line(at)
    at = (margin + 1) * blocks
    rate_o[...] = line(at)[:, heads : 2 * heads]
    bias_o[...] = line(at + 1)[:, heads : 2 * heads]
    for c in range(og_o.shape[1] // LANES):
        og_o[:, c * LANES : (c + 1) * LANES] = line(at + 2 + c)


def ffn_grads_body(inputs, gg, gu, og, hid, out, buf, sems):
    width = inputs.shape[1]
    ff = gg.shape[1]
    step = buf.shape[2] // 3
    copies = []
    for i in range(width // LANES):
        slot = i % 2
        cols = slice(i * LANES, (i + 1) * LANES)
        if i >= 2:
            copies[i - 2].wait()
        lhs = inputs[:, cols]
        buf[slot, :, :ff] = tn(lhs, gg[...]).astype(bf16)
        buf[slot, :, step : step + ff] = tn(lhs, gu[...]).astype(bf16)
        buf[slot, :, 2 * step : 2 * step + ff] = tn(og[:, cols], hid[...]).astype(bf16)
        copy = pltpu.make_async_copy(buf.at[slot], out.at[cols, pl.ds(0, 3 * step)], sems.at[slot])
        copy.start()
        copies.append(copy)
    for copy in copies[-2:]:
        copy.wait()


def shift_along(block, axis, distance):
    devices = range(lax.axis_size(axis))
    route = [(i - distance, i) for i in devices if i - distance in devices]
    return lax.ppermute(block, axis, route)


def pair(part):
    if lax.axis_size("tensor") == 2:
        return part, lax.ppermute(part, "tensor", [(0, 1), (1, 0)])
    return lax.psum(part, "tensor"), jnp.zeros_like(part)


def swap(blocks):
    return lax.all_to_all(blocks, "dp", 0, 0, tiled=True)


def on_device(
    block_input, output_grad, attn_gain, w_query, w_key, w_value, conv_query, conv_key, conv_value,
    w_beta, w_alpha, a_log, dt_bias, w_gate_out, out_gain, w_out, ffn_gain, w_gate, w_up, w_down,
):
    size, width = block_input.shape
    heads = a_log.shape[0]
    key_dim = w_query.shape[1] // heads
    value_dim = w_value.shape[1] // heads
    margin = conv_query.shape[0] - 1
    peers = lax.axis_size("dp")
    slices = peers // heads
    kc, vc, gc, ff = w_query.shape[1], w_value.shape[1], w_gate_out.shape[1], w_gate.shape[1]
    proj = 2 * kc + vc
    dims = (heads, key_dim, value_dim)
    rows = width // peers

    halo = shift_along(block_input[-HALO:], "dp", 1)
    grad_hidden = jnp.dot(output_grad, w_down.T, preferred_element_type=f32).astype(bf16)
    rate, bias = a_log[None], dt_bias[None]
    again, fgain, ogain = attn_gain[None], ffn_gain[None], out_gain[None]

    normed, ext, gate_pre, small, cum, q, k, v, inv, p, w, u, wsm, send = call(
        functools.partial(front_body, *dims, margin, slices),
        [
            ((size + HALO, width), bf16), ((size + HALO, proj), bf16), ((size, gc), f32),
            ((size, LANES), f32), ((size, LANES), f32), ((size, kc), f32), ((size, kc), f32), ((size, vc), f32),
            ((size, heads * size), bf16), ((size, heads * size), bf16), ((size, kc), bf16),
            ((size, vc), f32), ((LANES, width), bf16),
            ((peers, key_dim + value_dim // slices, key_dim), bf16),
        ],
        block_input, halo, again, w_query, w_key, w_value, w_gate_out, w_beta.T, w_alpha.T,
        conv_query, conv_key, conv_value, rate, bias,
        scratch=[pltpu.VMEM((size + HALO, proj), f32)],
    )
    maps = swap(send)
    maps, late_input = lax.optimization_barrier((maps, block_input))
    everyone = lax.all_gather(late_input, "dp", axis=0, tiled=True)
    piece = (peers, value_dim // slices, key_dim)
    (entry,) = call(functools.partial(scan_fwd_body, key_dim), [(piece, bf16)], maps)
    st = swap(entry).reshape(heads, value_dim, key_dim)
    stored, mixed, gated, mix_part = call(
        functools.partial(mix_body, *dims),
        [((size, vc), bf16), ((size, vc), f32), ((size, vc), bf16), ((size, width), bf16)],
        st, u, w, p, q, cum, gate_pre, ogain, w_out,
    )
    mix_pair = pair(mix_part)
    ffn_input, hidden, gga, gua, back_part, down_part = call(
        ffn_body,
        [((size, width), bf16), ((size, ff), bf16), ((size, ff), bf16), ((size, ff), bf16),
         ((size, width), bf16), ((size, width), bf16)],
        block_input, *mix_pair, fgain, w_gate, w_up, w_down, grad_hidden,
    )
    back_pair = pair(back_part)
    step = -(-ff // LANES) * LANES
    total = 3 * step + gc
    early = pl.pallas_call(
        ffn_grads_body,
        out_shape=jax.ShapeDtypeStruct((width, total), bf16),
        out_specs=pl.BlockSpec(memory_space=pl.ANY),
        scratch_shapes=[pltpu.VMEM((2, LANES, 3 * step), bf16), pltpu.SemaphoreType.DMA((2,))],
        compiler_params=pltpu.CompilerParams(vmem_limit_bytes=60000 * 1024),
    )(ffn_input, gga, gua, output_grad, hidden)
    back_pair, early = lax.optimization_barrier((back_pair, early))
    gres, dfg, dmix, pdo, dgate, dog, send_back, early = call(
        functools.partial(turn_body, *dims, slices),
        [((size, width), f32), ((1, width), f32), ((size, vc), bf16), ((size, vc), f32),
         ((size, gc), bf16), ((1, value_dim), f32), (piece, bf16), ((width, total), bf16)],
        block_input, *mix_pair, *back_pair, output_grad, fgain, w_out, gated, mixed, gate_pre, ogain, p, w, q, cum,
        early,
        scratch=[pltpu.VMEM((width, gc), bf16), pltpu.SemaphoreType.DMA((1,))], raw=(16,), alias={16: 7},
    )
    send_back, early = lax.optimization_barrier((send_back, early))
    first = lax.psum_scatter(early, "dp", scatter_dimension=0, tiled=True).astype(f32)
    local = swap(send_back)
    (exits,) = call(functools.partial(scan_bwd_body, key_dim), [(piece, bf16)], maps, local)
    dst = swap(exits).reshape(heads, value_dim, key_dim)
    down_pair = pair(down_part)
    dog_pair = pair(dog)

    qn, vn = kc // peers, vc // peers
    share = 2 * (qn + vn)
    send, part, wsmall = call(
        functools.partial(back_body, *dims, margin),
        [((peers, share + 2 * HALO, size), bf16), ((size + HALO, width), bf16), ((2 * HALO, width), f32)],
        dst, st, block_input, halo, normed, ext, conv_query, conv_key, conv_value,
        q, k, v, inv, p, stored, dmix, pdo, dgate,
        small, cum, rate, bias, *dog_pair, w_query, w_key, w_value, w_gate_out, wsm,
        scratch=[
            pltpu.VMEM((size + HALO, proj), f32), pltpu.VMEM((size + 2 * HALO, proj), f32),
            pltpu.VMEM((peers * HALO, LANES), f32),
        ],
    )
    rim_pair = pair(shift_along(part[:HALO], "dp", -1))
    part_pair = pair(part)
    recv = swap(send)
    input_grad, tail = call(
        functools.partial(finish_body, heads),
        [((size, width), f32), ((2 * HALO, width), f32)],
        block_input, again, *part_pair, *rim_pair, gres, wsmall, dfg,
    )
    wide = 2 * qn + vn == LANES
    packed = rows + (rows // 2 if wide else 0) + 3 * HALO
    (send,) = call(
        functools.partial(gather_body, vn), [((peers, packed, LANES), bf16)], recv, everyone, again, tail,
        scratch=[pltpu.VMEM((share, peers * size), bf16)],
    )
    recv = swap(send)
    side = jnp.full((1, 1), lax.axis_index("dp") % (LANES // rows), jnp.int32)
    gq, gk, gv, gg, gwb, gwa, gag, gfg, gcq, gck, gcv, grate, gbias, gog = call(
        functools.partial(scatter_body, heads, qn, vn, margin),
        [((rows, kc), f32), ((rows, kc), f32), ((rows, vc), f32), ((rows, gc), f32),
         ((heads, rows), f32), ((heads, rows), f32), ((1, rows), f32), ((1, rows), f32),
         ((margin + 1, kc), f32), ((margin + 1, kc), f32), ((margin + 1, vc), f32),
         ((1, heads), f32), ((1, heads), f32), ((1, value_dim), f32)],
        recv, side,
    )
    block_output = (
        block_input.astype(f32) + (mix_pair[0].astype(f32) + mix_pair[1].astype(f32))
        + (down_pair[0].astype(f32) + down_pair[1].astype(f32))
    )
    return (
        block_output, input_grad, gag[0], gq, gk, gv, gcq, gck, gcv, gwb.T, gwa.T,
        grate[0], gbias[0], gg, gog[0],
        first[:, 3 * step :].T, gfg[0], first[:, :ff], first[:, step : step + ff], first[:, 2 * step : 2 * step + ff].T,
    )


def solution(mesh):
    rows, cols, whole = P("dp", None), P(None, "tensor"), P()
    heads, high = P("tensor"), P("tensor", None)
    in_specs = (
        rows, rows, whole, cols, cols, cols, cols, cols, cols, cols, cols, heads, heads,
        cols, whole, high, whole, cols, cols, high,
    )
    both, crossed, dp = P("dp", "tensor"), P("tensor", "dp"), P("dp")
    out_specs = (
        rows, rows, dp, both, both, both, cols, cols, cols, both, both, heads, heads,
        both, whole, crossed, dp, both, both, crossed,
    )
    return jax.shard_map(
        on_device, mesh=mesh, in_specs=in_specs, out_specs=out_specs, check_vma=False
    )
```

```python
import functools

import jax
import jax.numpy as jnp
from jax import lax
from jax.experimental import pallas as pl
from jax.experimental.pallas import tpu as pltpu
from jax.sharding import PartitionSpec as P

EPS = 1e-06
LANES = 128
HALO = 8
f32 = jnp.float32
bf16 = jnp.bfloat16


def nn(a, b):
    dims = (((1,), (0,)), ((), ()))
    return lax.dot_general(a.astype(bf16), b.astype(bf16), dims, preferred_element_type=f32)


def nt(a, b):
    dims = (((1,), (1,)), ((), ()))
    return lax.dot_general(a.astype(bf16), b.astype(bf16), dims, preferred_element_type=f32)


def tn(a, b):
    dims = (((0,), (0,)), ((), ()))
    return lax.dot_general(a.astype(bf16), b.astype(bf16), dims, preferred_element_type=f32)


def exact(a, b):
    dims = (((1,), (0,)), ((), ()))
    return lax.dot_general(a, b, dims, preferred_element_type=f32, precision=lax.Precision.HIGHEST)


def row_sum(a):
    return jnp.sum(a, axis=-1, keepdims=True)


def col_sum(a):
    return jnp.sum(a, axis=0, keepdims=True)


def iotas(size):
    return (
        lax.broadcasted_iota(jnp.int32, (size, size), 0),
        lax.broadcasted_iota(jnp.int32, (size, size), 1),
    )


def exact3(a, b):
    (ah, al), (bh, bl) = a, b
    return nn(ah, bh) + (nn(ah, bl) + nn(al, bh))


def unit_lower_inverses(lows):
    size = lows[0].shape[0]
    rows, cols = iotas(size)

    def same(shift):
        return lax.shift_right_logical(rows, shift) == lax.shift_right_logical(cols, shift)

    def each(f, *lists):
        return [f(*items) for items in zip(*lists, strict=True)]

    eye = jnp.where(rows == cols, 1.0, 0.0).astype(f32)
    shift = 3
    diags = [jnp.where(same(shift), low, 0.0) for low in lows]
    invs = [eye - diag for diag in diags]
    powers = each(split, diags)
    for _ in range(shift - 1):
        powers = each(split, each(exact3, powers, powers))
        invs = each(lambda x, y: x + y, invs, each(exact3, each(split, invs), powers))
    while (1 << shift) < size:
        keep = same(shift + 1) & jnp.logical_not(same(shift))
        offs = [split(jnp.where(keep, low, 0.0)) for low in lows]
        halves = each(split, invs)
        inner = each(split, each(exact3, offs, halves))
        invs = each(lambda x, y: x - y, invs, each(exact3, halves, inner))
        shift += 1
    return invs


WHOLE = 60000 * 1024
NEAR = 20 * 1024 * 1024


def call(body, outs, *args, scratch=(), raw=(), alias=None, near=False, home=()):
    alias = alias or {}
    held = set(alias.values())
    far = pl.BlockSpec(memory_space=pltpu.HBM)
    here = pl.BlockSpec(memory_space=pltpu.VMEM) if near else pl.BlockSpec()
    return pl.pallas_call(
        body,
        name=getattr(body, "func", body).__name__,
        out_shape=[
            (pltpu.HBM if i in home or i in held else jax.ShapeDtypeStruct)(s, d)
            for i, (s, d) in enumerate(outs)
        ],
        in_specs=[far if i in raw else here for i in range(len(args))],
        out_specs=[
            far if i in held or ("out", i) in raw else pl.BlockSpec() if i in home else here
            for i in range(len(outs))
        ],
        input_output_aliases=alias,
        scratch_shapes=list(scratch),
        compiler_params=pltpu.CompilerParams(vmem_limit_bytes=NEAR if near else WHOLE),
    )(*args)


def in_step(steps):
    steps = list(steps)
    while steps:
        steps = [step for step in steps if next(step, True) is None]


def softplus(a):
    return jnp.maximum(a, 0.0) + jnp.log1p(jnp.exp(-jnp.abs(a)))


def place(row, heads):
    lane = lax.broadcasted_iota(jnp.int32, (1, LANES), 1)
    out = jnp.zeros((1, LANES), f32)
    for h in range(heads):
        out = jnp.where(lane == heads + h, row[0:1, h : h + 1], out)
    return out


def silu_parts(a):
    s = jax.nn.sigmoid(a)
    return a * s, s * (1.0 + a * (1.0 - s))


def conv_pre(ext, kern, base, cols, size, margin):
    total = None
    for j in range(margin + 1):
        tap = kern[j : j + 1, cols.start - base : cols.stop - base]
        term = tap * ext[pl.ds(HALO - margin + j, size), cols]
        total = term if total is None else total + term
    return total


def decay_terms(small, rate, bias, heads):
    size = small.shape[0]
    rows, cols = iotas(size)
    log_decay = -jnp.exp(rate) * softplus(small + bias)
    tril = jnp.where(rows >= cols, 1.0, 0.0).astype(f32)
    cum = exact(tril, log_decay)
    return log_decay, cum


def head_decay(cum, cum_t, at, rows, cols):
    g = cum[:, at : at + 1]
    spread = g - cum_t[at : at + 1, :]
    keep = rows >= cols
    return g, jnp.where(keep, jnp.exp(jnp.where(keep, spread, 0.0)), 0.0)


def front_body(
    heads, key_dim, value_dim, margin, slices,
    xs, halo, gain, wq, wk, wv, wg, wb, wa, kq, kk, kv, rate, bias,
    normed_o, ext_o, gate_o, small_o, cum_o, q_o, k_o, v_o, inv_o, p_o, w_o, u_o, wsm_o, send_o, ext,
):
    size = xs.shape[0]
    for ref, lo, hi in ((halo, 0, HALO), (xs, HALO, HALO + size)):
        x = ref[...].astype(f32)
        scale = lax.rsqrt(jnp.mean(x * x, axis=-1, keepdims=True) + EPS)
        normed_o[lo:hi, :] = (x * scale * gain[...]).astype(bf16)
    normed = normed_o[...]
    wsm_o[...] = jnp.zeros(wsm_o.shape, bf16)
    wsm_o[:heads, :] = wb[...]
    wsm_o[heads : 2 * heads, :] = wa[...]
    kc, vc = heads * key_dim, heads * value_dim
    for ref, lo, hi in ((wq, 0, kc), (wk, kc, 2 * kc), (wv, 2 * kc, 2 * kc + vc)):
        part = nn(normed, ref[...]).astype(bf16)
        ext_o[:, lo:hi] = part
        ext[:, lo:hi] = part.astype(f32)
    own = normed[HALO:]
    small = nt(own, wsm_o[...])
    small_o[...] = small
    beta_all = jax.nn.sigmoid(small)
    log_decay, cum = decay_terms(small, place(rate, heads), place(bias, heads), heads)
    cum_o[...] = cum
    cum_t = cum.T
    rows, cols = iotas(size)
    width = value_dim // slices
    kept = [None] * heads

    def start(h):
        ks = slice(h * key_dim, (h + 1) * key_dim)
        vs = slice(h * value_dim, (h + 1) * value_dim)
        kh = jax.nn.silu(conv_pre(ext, kk, kc, slice(kc + ks.start, kc + ks.stop), size, margin))
        qh = jax.nn.silu(conv_pre(ext, kq, 0, ks, size, margin))
        yield
        k = kh * lax.rsqrt(row_sum(kh * kh) + EPS)
        q = qh * (lax.rsqrt(row_sum(qh * qh) + EPS) * key_dim**-0.5)
        q_o[:, ks] = q
        k_o[:, ks] = k
        dots = nt(jnp.concatenate([k, q], axis=0), k)
        yield
        beta = beta_all[:, h : h + 1]
        g, decay = head_decay(cum, cum_t, heads + h, rows, cols)
        low = jnp.where(rows > cols, beta * decay * dots[:size], 0.0)
        p_o[:, h * size : (h + 1) * size] = (dots[size:] * decay).astype(bf16)
        kept[h] = (ks, vs, beta, g, low)
        yield
        v_o[:, vs] = jax.nn.silu(conv_pre(ext, kv, 2 * kc, slice(2 * kc + vs.start, 2 * kc + vs.stop), size, margin))

    in_step(start(h) for h in range(heads))
    invs = unit_lower_inverses([item[-1] for item in kept])
    solved_all = []
    for (ks, vs, beta, g, _), inv in zip(kept, invs, strict=True):
        rhs = jnp.concatenate([beta * v_o[:, vs], (beta * jnp.exp(g)) * k_o[:, ks]], axis=1)
        solved_all.append(nn(inv, rhs))
    for h, (ks, vs, beta, g, _) in enumerate(kept):
        inv_o[:, h * size : (h + 1) * size] = invs[h].astype(bf16)
        last = cum[size - 1 : size, heads + h : heads + h + 1]
        solved = solved_all[h]
        kt = k_o[:, ks] * jnp.exp(last - g)
        maps = tn(solved, kt)
        er, ec = iotas(key_dim)
        at = jnp.where(er == ec, jnp.exp(last), 0.0) - maps[value_dim:]
        bt = maps[:value_dim].astype(bf16)
        at = at.astype(bf16)
        for s in range(slices):
            send_o[h * slices + s, :key_dim, :] = at
            send_o[h * slices + s, key_dim:, :] = bt[s * width : (s + 1) * width]
        w_o[:, ks] = solved[:, value_dim:].astype(bf16)
        u_o[:, vs] = solved[:, :value_dim]
    gate_o[...] = nn(own, wg[...])


def split(a):
    hi = a.astype(bf16)
    return hi, (a - hi.astype(f32)).astype(bf16)


def scan_fwd_body(key_dim, maps, out):
    n, rows, _ = maps.shape
    state = jnp.zeros((rows - key_dim, key_dim), f32)
    for j in range(n):
        out[j] = state.astype(bf16)
        if j < n - 1:
            hi, lo = split(state)
            a = maps[j, :key_dim, :]
            state = nn(hi, a) + nn(lo, a) + maps[j, key_dim:, :].astype(f32)


def scan_bwd_body(key_dim, maps, local, out):
    n = maps.shape[0]
    state = jnp.zeros(local.shape[1:], f32)
    for j in range(n - 1, -1, -1):
        out[j] = state.astype(bf16)
        if j > 0:
            hi, lo = split(state)
            a = maps[j, :key_dim, :]
            state = nt(hi, a) + nt(lo, a) + local[j].astype(f32)


def mix_body(
    heads, key_dim, value_dim,
    st, u, w, p, q, cum, gate, gain, wo,
    stored_o, mixed_o, gated_o, part_o,
):
    size = u.shape[0]

    def one(h):
        ks = slice(h * key_dim, (h + 1) * key_dim)
        vs = slice(h * value_dim, (h + 1) * value_dim)
        both = nt(jnp.concatenate([w[:, ks], q[:, ks].astype(bf16)], axis=0), st[h])
        yield
        stored = (u[:, vs] - both[:size]).astype(bf16)
        stored_o[:, vs] = stored
        inner = nn(p[:, h * size : (h + 1) * size], stored)
        yield
        eg = jnp.exp(cum[:, heads + h : heads + h + 1])
        mixed = eg * both[size:] + inner
        mixed_o[:, vs] = mixed
        scale = lax.rsqrt(jnp.mean(mixed * mixed, axis=-1, keepdims=True) + EPS)
        gated_o[:, vs] = (mixed * scale * gain[...] * jax.nn.silu(gate[:, vs])).astype(bf16)

    in_step(one(h) for h in range(heads))
    part_o[...] = nn(gated_o[...], wo[...]).astype(bf16)


def hidden_body(og, w_down, out):
    out[...] = nt(og[...], w_down[...]).astype(bf16)


def ffn_body(x, mine, other, gain, w_gate, w_up, w_down, grad_hidden, input_o, hid_o, gg_o, gu_o, back_o, down_o):
    r = x[...].astype(f32) + (mine[...].astype(f32) + other[...].astype(f32))
    scale = lax.rsqrt(jnp.mean(r * r, axis=-1, keepdims=True) + EPS)
    ffn_in = (r * scale * gain[...]).astype(bf16)
    input_o[...] = ffn_in
    gate = nn(ffn_in, w_gate[...])
    up = nn(ffn_in, w_up[...])
    sig = jax.nn.sigmoid(gate)
    gh = grad_hidden[...].astype(f32)
    gu_o[...] = (gh * gate * sig).astype(bf16)
    gg_o[...] = (gh * up * sig * (1.0 + gate * (1.0 - sig))).astype(bf16)
    hid_o[...] = (gate * sig * up).astype(bf16)
    back_o[...] = (nt(gg_o[...], w_gate[...]) + nt(gu_o[...], w_up[...])).astype(bf16)
    down_o[...] = nn(hid_o[...], w_down[...]).astype(bf16)


def turn_body(
    heads, key_dim, value_dim, slices,
    x, mine, other, back_mine, back_other, og, ffn_gain, wo, gated, mixed, gate, out_gain, p, w, q, cum, _,
    gres_o, dfg_o, dmix_o, pdo_o, dgate_o, dog_o, send_o, grads_o, buf, sem,
):
    r = x[...].astype(f32) + (mine[...].astype(f32) + other[...].astype(f32))
    scale = lax.rsqrt(jnp.mean(r * r, axis=-1, keepdims=True) + EPS)
    b = back_mine[...].astype(f32) + back_other[...].astype(f32)
    normal = r * scale
    dfg_o[...] = col_sum(b * normal)
    d = b * ffn_gain[...]
    gres = og[...].astype(f32) + scale * (d - normal * jnp.mean(d * normal, axis=-1, keepdims=True))
    gres_o[...] = gres
    low = gres.astype(bf16)
    dgated = nt(low, wo[...])
    buf[...] = tn(low, gated[...]).astype(bf16)
    copy = pltpu.make_async_copy(
        buf, grads_o.at[:, pl.ds(grads_o.shape[1] - buf.shape[1], buf.shape[1])], sem.at[0]
    )
    copy.start()
    size = r.shape[0]
    width = value_dim // slices
    dogs = [None] * heads

    def one(h):
        ks = slice(h * key_dim, (h + 1) * key_dim)
        vs = slice(h * value_dim, (h + 1) * value_dim)
        m = mixed[:, vs]
        scale_h = lax.rsqrt(jnp.mean(m * m, axis=-1, keepdims=True) + EPS)
        n = m * scale_h
        act, dact = silu_parts(gate[:, vs])
        dg = dgated[:, vs]
        dgate_o[:, vs] = (dg * (n * out_gain[...]) * dact).astype(bf16)
        dn = dg * act
        dogs[h] = col_sum(dn * n)
        dn = dn * out_gain[...]
        dm = scale_h * (dn - n * jnp.mean(dn * n, axis=-1, keepdims=True))
        dm = dm.astype(bf16)
        dmix_o[:, vs] = dm
        pdo = tn(p[:, h * size : (h + 1) * size], dm)
        yield
        pdo_o[:, vs] = pdo
        eg = jnp.exp(cum[:, heads + h : heads + h + 1])
        left = jnp.concatenate([dm, -pdo.astype(bf16)], axis=0)
        right = jnp.concatenate([(q[:, ks] * eg).astype(bf16), w[:, ks]], axis=0)
        local = tn(left, right).astype(bf16)
        yield
        for s in range(slices):
            send_o[h * slices + s] = local[s * width : (s + 1) * width]

    in_step(one(h) for h in range(heads))
    dog_o[...] = sum(dogs[1:], dogs[0])
    copy.wait()


def back_body(
    heads, key_dim, value_dim, margin,
    dst, st, xs, halo, normed, ext_i, kq, kk, kv, q_i, k_i, v_i, inv_i, p_i, stored_i, dmix_i, pdo_i, dgate_i,
    small, cum_i, rate_i, bias_i, dog_mine, dog_other, wq, wk, wv, wg, wsm,
    send_o, part_o, wsmall_o, ext, pad, flat,
):
    size = q_i.shape[0]
    total = size + HALO
    kc, vc = heads * key_dim, heads * value_dim
    proj = 2 * kc + vc
    ext[...] = ext_i[...].astype(f32)
    pad[:HALO, :] = jnp.zeros((HALO, proj), f32)
    pad[HALO + size :, :] = jnp.zeros((HALO, proj), f32)
    sm = small[...]
    cum = cum_i[...]
    rate, bias = place(rate_i, heads), place(bias_i, heads)
    log_decay = -jnp.exp(rate) * softplus(sm + bias)
    cum_t = cum.T
    beta_all = jax.nn.sigmoid(sm)
    rows, cols = iotas(size)
    lane = lax.broadcasted_iota(jnp.int32, (size, LANES), 1)
    end_row = lax.broadcasted_iota(jnp.int32, (size, 1), 0) == size - 1
    dcums, dbetas = [None] * heads, [None] * heads

    blocks = proj // LANES
    flat[...] = jnp.zeros(flat.shape, f32)

    def conv_back(dy, kern, base, lo, hi):
        cs = slice(lo, hi)
        pre = conv_pre(ext, kern, base, cs, size, margin)
        _, dact = silu_parts(pre)
        dpre = dy * dact
        pad[pl.ds(HALO, size), cs] = dpre
        for j in range(margin + 1):
            tap = col_sum(dpre * ext[pl.ds(HALO - margin + j, size), cs])
            for c in range((hi - lo) // LANES):
                at = j * blocks + lo // LANES + c
                flat[at : at + 1, :] = tap[:, c * LANES : (c + 1) * LANES]

    def one(h):
        ks = slice(h * key_dim, (h + 1) * key_dim)
        vs = slice(h * value_dim, (h + 1) * value_dim)
        ps = slice(h * size, (h + 1) * size)
        q, k, v = q_i[:, ks], k_i[:, ks], v_i[:, vs]
        stored, do = stored_i[:, vs], dmix_i[:, vs]
        s, ds = st[h], dst[h]
        beta = beta_all[:, h : h + 1]
        g, decay = head_decay(cum, cum_t, heads + h, rows, cols)
        eg = jnp.exp(g)
        last = cum[size - 1 : size, heads + h : heads + h + 1]
        kt = k * jnp.exp(last - g)
        kl, ql = k.astype(bf16), q.astype(bf16)
        states = nt(jnp.concatenate([kl, ql], axis=0), s)
        dstored = pdo_i[:, vs] + nt(kt, ds)
        yield
        dr = tn(inv_i[:, ps], dstored)
        dkt = nn(stored, ds)
        dots = nt(kl, kl)
        yield
        drl = dr.astype(bf16)
        k_s, q_s = states[:size], states[size:]
        both = jnp.concatenate([drl, do], axis=0)
        inner = nt(both, stored)
        back = nn(both, s)
        yield
        scaled = decay * dots
        dlow = jnp.where(rows > cols, -inner[:size], 0.0)
        dp = jnp.where(rows >= cols, inner[size:], 0.0)
        dv = beta * dr
        spread = dlow * (beta * scaled) + dp * p_i[:, ps].astype(f32)
        dqk = (dp * decay).astype(bf16)
        dkk = dlow * (beta * decay)
        left = jnp.concatenate([dqk, (dkk + dkk.T).astype(bf16)], axis=0)
        on_k = nn(left, kl)
        on_q = tn(dqk, ql)
        yield
        dq = on_k[:size] + eg * back[size:]
        tail_part = row_sum(dkt * kt)
        dk = on_k[size:] + on_q - (beta * eg) * back[:size] + jnp.exp(last - g) * dkt
        dbeta = row_sum(dr * (v - eg * k_s)) + row_sum(dlow * scaled)
        dg = row_sum(spread) - row_sum(spread.T) - tail_part
        dg = dg + eg * row_sum(do.astype(f32) * q_s) - (beta * eg) * row_sum(dr * k_s)
        carry = col_sum(row_sum(s.astype(f32) * ds.astype(f32)))
        at_end = col_sum(tail_part) + jnp.exp(last) * carry
        dg = dg + jnp.where(end_row, at_end, 0.0)
        dcums[h] = jnp.where(lane == heads + h, dg, 0.0)
        dbetas[h] = jnp.where(lane == h, dbeta, 0.0)
        yield
        qh = jax.nn.silu(conv_pre(ext, kq, 0, ks, size, margin))
        rq = lax.rsqrt(row_sum(qh * qh) + EPS)
        unit = qh * rq
        dqn = dq * key_dim**-0.5
        conv_back(rq * (dqn - unit * row_sum(dqn * unit)), kq, 0, ks.start, ks.stop)
        kh = jax.nn.silu(conv_pre(ext, kk, kc, slice(kc + ks.start, kc + ks.stop), size, margin))
        rk = lax.rsqrt(row_sum(kh * kh) + EPS)
        conv_back(rk * (dk - k * row_sum(dk * k)), kk, kc, kc + ks.start, kc + ks.stop)
        conv_back(dv, kv, 2 * kc, 2 * kc + vs.start, 2 * kc + vs.stop)

    in_step(one(h) for h in range(heads))
    dcum, dbeta_all = sum(dcums[1:], dcums[0]), sum(dbetas[1:], dbetas[0])
    triu = jnp.where(rows <= cols, 1.0, 0.0).astype(f32)
    dlog = exact(triu, dcum)
    dalpha = dlog * (-jnp.exp(rate)) * jax.nn.sigmoid(sm + bias)
    dsmall = dalpha + dbeta_all * beta_all * (1.0 - beta_all)
    taps = (margin + 1) * blocks
    flat[taps : taps + 1, :] = col_sum(dlog * log_decay)
    flat[taps + 1 : taps + 2, :] = col_sum(dalpha)
    dog = dog_mine[...] + dog_other[...]
    for c in range(value_dim // LANES):
        flat[taps + 2 + c : taps + 3 + c, :] = dog[:, c * LANES : (c + 1) * LANES]
    x = xs[...].astype(f32)
    scale = lax.rsqrt(jnp.mean(x * x, axis=-1, keepdims=True) + EPS)
    hx = halo[...].astype(f32)
    hscale = lax.rsqrt(jnp.mean(hx * hx, axis=-1, keepdims=True) + EPS)
    peers = send_o.shape[0]
    qn, vn = kc // peers, vc // peers
    acc = None
    for ref, kern, lo, hi, n, at in (
        (wq, kq, 0, kc, qn, 0), (wk, kk, kc, 2 * kc, qn, qn), (wv, kv, 2 * kc, proj, vn, 2 * qn),
    ):
        dext = None
        for j in range(margin + 1):
            term = kern[j : j + 1, :] * pad[pl.ds(margin - j, total), lo:hi]
            dext = term if dext is None else dext + term
        part = nt(dext, ref[...])
        acc = part if acc is None else acc + part
        own = (dext[HALO:] * scale).T.astype(bf16)
        rim = (dext[:HALO] * hscale).astype(bf16)
        for e in range(peers):
            send_o[e, at : at + n, :] = own[e * n : (e + 1) * n]
            send_o[e, 2 * (qn + vn) : 2 * (qn + vn) + HALO, at : at + n] = rim[:, e * n : (e + 1) * n]
    dgate = dgate_i[...]
    own = (dgate.astype(f32) * scale).T.astype(bf16)
    fl = flat[...].astype(bf16)
    for e in range(peers):
        send_o[e, 2 * qn + vn : 2 * (qn + vn), :] = own[e * vn : (e + 1) * vn]
        send_o[e, 2 * (qn + vn) + HALO :, :] = fl[e * HALO : (e + 1) * HALO]
    dsl = dsmall.astype(bf16)
    wsmall_o[...] = tn(dsl, normed[HALO:, :])[: wsmall_o.shape[0]]
    part_o[:HALO, :] = acc[:HALO].astype(bf16)
    part_o[HALO:, :] = (acc[HALO:] + nt(dgate, wg[...]) + nn(dsl, wsm[...])).astype(bf16)


def finish_body(heads, xs, gain, part, part_other, rim, rim_other, gres, wsmall, dfg, input_o, tail_o):
    size = xs.shape[0]
    x = xs[...].astype(f32)
    scale = lax.rsqrt(jnp.mean(x * x, axis=-1, keepdims=True) + EPS)
    normal = x * scale
    g = part[HALO:, :].astype(f32) + part_other[HALO:, :].astype(f32)
    edge = rim[...].astype(f32) + rim_other[...].astype(f32)
    g = jnp.concatenate([g[: size - HALO], g[size - HALO :] + edge], axis=0)
    tail_o[...] = jnp.zeros(tail_o.shape, f32)
    tail_o[: 2 * heads, :] = wsmall[: 2 * heads, :]
    tail_o[2 * heads : 2 * heads + 1, :] = col_sum(g * normal)
    tail_o[2 * heads + 1 : 2 * heads + 2, :] = dfg[...]
    d = g * gain[...]
    input_o[...] = gres[...] + scale * (d - normal * jnp.mean(d * normal, axis=-1, keepdims=True))


def gather_body(split_at, recv, xg, gain, tail, send_o, lhs):
    peers, _, size = recv.shape
    n = recv.shape[1] - 2 * HALO
    width = xg.shape[1]
    rows = width // peers
    flat = jnp.zeros((HALO, LANES), f32)
    edge, near = [], []
    for j in range(peers):
        lhs[:, j * size : (j + 1) * size] = recv[j, :n, :]
        edge.append(recv[j, n : n + HALO, :])
        flat = flat + recv[j, n + HALO :, :].astype(f32)
        near.append(xg[j * size - HALO : j * size, :] if j else jnp.zeros((HALO, width), bf16))
    acc = nn(lhs[...], xg[...])
    extra = tn(jnp.concatenate(edge, axis=0), jnp.concatenate(near, axis=0))
    mixed = n - split_at
    top = (acc[:mixed] + extra[:mixed]) * gain[...]
    rest = acc[mixed:] * gain[...]
    half = rows // 2
    wide = mixed == LANES
    if wide:
        top, rest = top.T.astype(bf16), rest.T.astype(bf16)
    else:
        fill = jnp.zeros((LANES - n, width), f32)
        top, half = jnp.concatenate([top, rest, fill], axis=0).T.astype(bf16), 0
    fl = flat.astype(bf16)
    small = tail[...].astype(bf16)
    for e in range(peers):
        lo = e * rows
        block = lo // LANES * LANES
        send_o[e, :rows, :] = top[lo : lo + rows]
        if wide:
            send_o[e, rows : rows + half, :] = jnp.concatenate(
                [rest[lo : lo + half], rest[lo + half : lo + rows]], axis=1
            )
        send_o[e, rows + half : rows + half + 2 * HALO, :] = small[:, block : block + LANES]
        send_o[e, rows + half + 2 * HALO :, :] = fl


def scatter_body(heads, qn, vn, margin, recv, side, q_o, k_o, v_o, g_o, wb_o, wa_o, ag_o, fg_o, cq_o, ck_o, cv_o, rate_o, bias_o, og_o):
    peers = recv.shape[0]
    rows = q_o.shape[0]
    wide = 2 * qn + vn == LANES
    half = rows // 2 if wide else 0
    low = jnp.zeros((2 * HALO, LANES), f32)
    lines = []
    for e in range(peers):
        top = recv[e, :rows, :].astype(f32)
        q_o[:, e * qn : (e + 1) * qn] = top[:, :qn]
        k_o[:, e * qn : (e + 1) * qn] = top[:, qn : 2 * qn]
        v_o[:, e * vn : (e + 1) * vn] = top[:, 2 * qn : 2 * qn + vn]
        if wide:
            rest = recv[e, rows : rows + half, :].astype(f32)
            g_o[:half, e * vn : (e + 1) * vn] = rest[:, :vn]
            g_o[half:, e * vn : (e + 1) * vn] = rest[:, vn:]
        else:
            g_o[:, e * vn : (e + 1) * vn] = top[:, 2 * qn + vn : 2 * (qn + vn)]
        low = low + recv[e, rows + half : rows + half + 2 * HALO, :].astype(f32)
        lines.append(recv[e, rows + half + 2 * HALO :, :].astype(f32))
    picked = low[:, :rows]
    for s in range(1, LANES // rows):
        picked = jnp.where(side[0:1, 0:1] == s, low[:, s * rows : (s + 1) * rows], picked)
    wb_o[...] = picked[:heads]
    wa_o[...] = picked[heads : 2 * heads]
    ag_o[...] = picked[2 * heads : 2 * heads + 1]
    fg_o[...] = picked[2 * heads + 1 : 2 * heads + 2]

    def line(at):
        return lines[at // HALO][at % HALO : at % HALO + 1]

    kb, vb = cq_o.shape[1] // LANES, cv_o.shape[1] // LANES
    blocks = 2 * kb + vb
    for j in range(margin + 1):
        for c in range(blocks):
            at = j * blocks + c
            ref, to = (cq_o, c) if c < kb else (ck_o, c - kb) if c < 2 * kb else (cv_o, c - 2 * kb)
            ref[j : j + 1, to * LANES : (to + 1) * LANES] = line(at)
    at = (margin + 1) * blocks
    rate_o[...] = line(at)[:, heads : 2 * heads]
    bias_o[...] = line(at + 1)[:, heads : 2 * heads]
    for c in range(og_o.shape[1] // LANES):
        og_o[:, c * LANES : (c + 1) * LANES] = line(at + 2 + c)


def ffn_grads_body(inputs, gg, gu, og, hid, out, buf, sems):
    width = inputs.shape[1]
    ff = gg.shape[1]
    step = buf.shape[2] // 3
    copies = []
    for i in range(width // LANES):
        slot = i % 2
        cols = slice(i * LANES, (i + 1) * LANES)
        if i >= 2:
            copies[i - 2].wait()
        lhs = inputs[:, cols]
        buf[slot, :, :ff] = tn(lhs, gg[...]).astype(bf16)
        buf[slot, :, step : step + ff] = tn(lhs, gu[...]).astype(bf16)
        buf[slot, :, 2 * step : 2 * step + ff] = tn(og[:, cols], hid[...]).astype(bf16)
        copy = pltpu.make_async_copy(buf.at[slot], out.at[cols, pl.ds(0, 3 * step)], sems.at[slot])
        copy.start()
        copies.append(copy)
    for copy in copies[-2:]:
        copy.wait()


def shift_along(block, axis, distance):
    devices = range(lax.axis_size(axis))
    route = [(i - distance, i) for i in devices if i - distance in devices]
    return lax.ppermute(block, axis, route)


def pair(part):
    if lax.axis_size("tensor") == 2:
        return part, lax.ppermute(part, "tensor", [(0, 1), (1, 0)])
    return lax.psum(part, "tensor"), jnp.zeros_like(part)


def swap(blocks):
    return lax.all_to_all(blocks, "dp", 0, 0, tiled=True)


def on_device(
    block_input, output_grad, attn_gain, w_query, w_key, w_value, conv_query, conv_key, conv_value,
    w_beta, w_alpha, a_log, dt_bias, w_gate_out, out_gain, w_out, ffn_gain, w_gate, w_up, w_down,
):
    size, width = block_input.shape
    heads = a_log.shape[0]
    key_dim = w_query.shape[1] // heads
    value_dim = w_value.shape[1] // heads
    margin = conv_query.shape[0] - 1
    peers = lax.axis_size("dp")
    slices = peers // heads
    kc, vc, gc, ff = w_query.shape[1], w_value.shape[1], w_gate_out.shape[1], w_gate.shape[1]
    proj = 2 * kc + vc
    dims = (heads, key_dim, value_dim)
    rows = width // peers

    halo = shift_along(block_input[-HALO:], "dp", 1)
    rate, bias = a_log[None], dt_bias[None]
    again, fgain, ogain = attn_gain[None], ffn_gain[None], out_gain[None]

    normed, ext, gate_pre, small, cum, q, k, v, inv, p, w, u, wsm, send = call(
        functools.partial(front_body, *dims, margin, slices),
        [
            ((size + HALO, width), bf16), ((size + HALO, proj), bf16), ((size, gc), f32),
            ((size, LANES), f32), ((size, LANES), f32), ((size, kc), f32), ((size, kc), f32), ((size, vc), f32),
            ((size, heads * size), bf16), ((size, heads * size), bf16), ((size, kc), bf16),
            ((size, vc), f32), ((LANES, width), bf16),
            ((peers, key_dim + value_dim // slices, key_dim), bf16),
        ],
        block_input, halo, again, w_query, w_key, w_value, w_gate_out, w_beta.T, w_alpha.T,
        conv_query, conv_key, conv_value, rate, bias,
        scratch=[pltpu.VMEM((size + HALO, proj), f32)],
    )
    maps = swap(send)
    maps, late_input = lax.optimization_barrier((maps, block_input))
    everyone = lax.all_gather(late_input, "dp", axis=0, tiled=True)
    piece = (peers, value_dim // slices, key_dim)
    (entry,) = call(functools.partial(scan_fwd_body, key_dim), [(piece, bf16)], maps)
    st = swap(entry).reshape(heads, value_dim, key_dim)
    stored, mixed, gated, mix_part = call(
        functools.partial(mix_body, *dims),
        [((size, vc), bf16), ((size, vc), f32), ((size, vc), bf16), ((size, width), bf16)],
        st, u, w, p, q, cum, gate_pre, ogain, w_out,
    )
    mix_part, late_grad = lax.optimization_barrier((mix_part, output_grad))
    mix_pair = pair(mix_part)
    (grad_hidden,) = call(hidden_body, [((size, ff), bf16)], late_grad, w_down, near=True)
    ffn_input, hidden, gga, gua, back_part, down_part = call(
        ffn_body,
        [((size, width), bf16), ((size, ff), bf16), ((size, ff), bf16), ((size, ff), bf16),
         ((size, width), bf16), ((size, width), bf16)],
        block_input, *mix_pair, fgain, w_gate, w_up, w_down, grad_hidden, near=True, home=(4, 5),
    )
    back_pair = pair(back_part)
    step = -(-ff // LANES) * LANES
    total = 3 * step + gc
    (early,) = call(
        ffn_grads_body, [((width, total), bf16)], ffn_input, gga, gua, output_grad, hidden,
        scratch=[pltpu.VMEM((2, LANES, 3 * step), bf16), pltpu.SemaphoreType.DMA((2,))],
        raw=(("out", 0),), home=(0,), near=True,
    )
    back_pair, early = lax.optimization_barrier((back_pair, early))
    gres, dfg, dmix, pdo, dgate, dog, send_back, early = call(
        functools.partial(turn_body, *dims, slices),
        [((size, width), f32), ((1, width), f32), ((size, vc), bf16), ((size, vc), f32),
         ((size, gc), bf16), ((1, value_dim), f32), (piece, bf16), ((width, total), bf16)],
        block_input, *mix_pair, *back_pair, output_grad, fgain, w_out, gated, mixed, gate_pre, ogain, p, w, q, cum,
        early,
        scratch=[pltpu.VMEM((width, gc), bf16), pltpu.SemaphoreType.DMA((1,))], raw=(16,), alias={16: 7}, near=True, home=range(7),
    )
    send_back, early = lax.optimization_barrier((send_back, early))
    first = lax.psum_scatter(early, "dp", scatter_dimension=0, tiled=True).astype(f32)
    local = swap(send_back)
    (exits,) = call(functools.partial(scan_bwd_body, key_dim), [(piece, bf16)], maps, local)
    dst = swap(exits).reshape(heads, value_dim, key_dim)
    down_pair = pair(down_part)
    dog_pair = pair(dog)

    qn, vn = kc // peers, vc // peers
    share = 2 * (qn + vn)
    send, part, wsmall = call(
        functools.partial(back_body, *dims, margin),
        [((peers, share + 2 * HALO, size), bf16), ((size + HALO, width), bf16), ((2 * HALO, width), f32)],
        dst, st, block_input, halo, normed, ext, conv_query, conv_key, conv_value,
        q, k, v, inv, p, stored, dmix, pdo, dgate,
        small, cum, rate, bias, *dog_pair, w_query, w_key, w_value, w_gate_out, wsm,
        scratch=[
            pltpu.VMEM((size + HALO, proj), f32), pltpu.VMEM((size + 2 * HALO, proj), f32),
            pltpu.VMEM((peers * HALO, LANES), f32),
        ],
    )
    rim_pair = pair(shift_along(part[:HALO], "dp", -1))
    part_pair = pair(part)
    recv = swap(send)
    input_grad, tail = call(
        functools.partial(finish_body, heads),
        [((size, width), f32), ((2 * HALO, width), f32)],
        block_input, again, *part_pair, *rim_pair, gres, wsmall, dfg,
    )
    wide = 2 * qn + vn == LANES
    packed = rows + (rows // 2 if wide else 0) + 3 * HALO
    (send,) = call(
        functools.partial(gather_body, vn), [((peers, packed, LANES), bf16)], recv, everyone, again, tail,
        scratch=[pltpu.VMEM((share, peers * size), bf16)],
    )
    recv = swap(send)
    side = jnp.full((1, 1), lax.axis_index("dp") % (LANES // rows), jnp.int32)
    gq, gk, gv, gg, gwb, gwa, gag, gfg, gcq, gck, gcv, grate, gbias, gog = call(
        functools.partial(scatter_body, heads, qn, vn, margin),
        [((rows, kc), f32), ((rows, kc), f32), ((rows, vc), f32), ((rows, gc), f32),
         ((heads, rows), f32), ((heads, rows), f32), ((1, rows), f32), ((1, rows), f32),
         ((margin + 1, kc), f32), ((margin + 1, kc), f32), ((margin + 1, vc), f32),
         ((1, heads), f32), ((1, heads), f32), ((1, value_dim), f32)],
        recv, side,
    )
    block_output = (
        block_input.astype(f32) + (mix_pair[0].astype(f32) + mix_pair[1].astype(f32))
        + (down_pair[0].astype(f32) + down_pair[1].astype(f32))
    )
    return (
        block_output, input_grad, gag[0], gq, gk, gv, gcq, gck, gcv, gwb.T, gwa.T,
        grate[0], gbias[0], gg, gog[0],
        first[:, 3 * step :].T, gfg[0], first[:, :ff], first[:, step : step + ff], first[:, 2 * step : 2 * step + ff].T,
    )


def solution(mesh):
    rows, cols, whole = P("dp", None), P(None, "tensor"), P()
    heads, high = P("tensor"), P("tensor", None)
    in_specs = (
        rows, rows, whole, cols, cols, cols, cols, cols, cols, cols, cols, heads, heads,
        cols, whole, high, whole, cols, cols, high,
    )
    both, crossed, dp = P("dp", "tensor"), P("tensor", "dp"), P("dp")
    out_specs = (
        rows, rows, dp, both, both, both, cols, cols, cols, both, both, heads, heads,
        both, whole, crossed, dp, both, both, crossed,
    )
    return jax.shard_map(
        on_device, mesh=mesh, in_specs=in_specs, out_specs=out_specs, check_vma=False
    )
```

```python
import functools

import jax
import jax.numpy as jnp
from jax import lax
from jax.experimental import pallas as pl
from jax.experimental.pallas import tpu as pltpu
from jax.sharding import PartitionSpec as P

EPS = 1e-06
LANES = 128
HALO = 8
f32 = jnp.float32
bf16 = jnp.bfloat16


def nn(a, b):
    dims = (((1,), (0,)), ((), ()))
    return lax.dot_general(a.astype(bf16), b.astype(bf16), dims, preferred_element_type=f32)


def nt(a, b):
    dims = (((1,), (1,)), ((), ()))
    return lax.dot_general(a.astype(bf16), b.astype(bf16), dims, preferred_element_type=f32)


def tn(a, b):
    dims = (((0,), (0,)), ((), ()))
    return lax.dot_general(a.astype(bf16), b.astype(bf16), dims, preferred_element_type=f32)


def exact(a, b):
    dims = (((1,), (0,)), ((), ()))
    return lax.dot_general(a, b, dims, preferred_element_type=f32, precision=lax.Precision.HIGHEST)


def row_sum(a):
    return jnp.sum(a, axis=-1, keepdims=True)


def col_sum(a):
    return jnp.sum(a, axis=0, keepdims=True)


def iotas(size):
    return (
        lax.broadcasted_iota(jnp.int32, (size, size), 0),
        lax.broadcasted_iota(jnp.int32, (size, size), 1),
    )


def exact3(a, b):
    (ah, al), (bh, bl) = a, b
    return nn(ah, bh) + (nn(ah, bl) + nn(al, bh))


def unit_lower_inverses(lows):
    size = lows[0].shape[0]
    rows, cols = iotas(size)

    def same(shift):
        return lax.shift_right_logical(rows, shift) == lax.shift_right_logical(cols, shift)

    def each(f, *lists):
        return [f(*items) for items in zip(*lists, strict=True)]

    eye = jnp.where(rows == cols, 1.0, 0.0).astype(f32)
    shift = 3
    diags = [jnp.where(same(shift), low, 0.0) for low in lows]
    invs = [eye - diag for diag in diags]
    powers = each(split, diags)
    for _ in range(shift - 1):
        powers = each(split, each(exact3, powers, powers))
        invs = each(lambda x, y: x + y, invs, each(exact3, each(split, invs), powers))
    while (1 << shift) < size:
        keep = same(shift + 1) & jnp.logical_not(same(shift))
        offs = [split(jnp.where(keep, low, 0.0)) for low in lows]
        halves = each(split, invs)
        inner = each(split, each(exact3, offs, halves))
        invs = each(lambda x, y: x - y, invs, each(exact3, halves, inner))
        shift += 1
    return invs


WHOLE = 60000 * 1024
NEAR = 20 * 1024 * 1024


def call(body, outs, *args, scratch=(), raw=(), alias=None, near=False, home=()):
    alias = alias or {}
    held = set(alias.values())
    far = pl.BlockSpec(memory_space=pltpu.HBM)
    here = pl.BlockSpec(memory_space=pltpu.VMEM) if near else pl.BlockSpec()
    return pl.pallas_call(
        body,
        name=getattr(body, "func", body).__name__,
        out_shape=[
            (pltpu.HBM if i in home or i in held else jax.ShapeDtypeStruct)(s, d)
            for i, (s, d) in enumerate(outs)
        ],
        in_specs=[far if i in raw else here for i in range(len(args))],
        out_specs=[
            far if i in held or ("out", i) in raw else pl.BlockSpec() if i in home else here
            for i in range(len(outs))
        ],
        input_output_aliases=alias,
        scratch_shapes=list(scratch),
        compiler_params=pltpu.CompilerParams(vmem_limit_bytes=NEAR if near else WHOLE),
    )(*args)


def in_step(steps):
    steps = list(steps)
    while steps:
        steps = [step for step in steps if next(step, True) is None]


def softplus(a):
    return jnp.maximum(a, 0.0) + jnp.log1p(jnp.exp(-jnp.abs(a)))


def place(row, heads):
    lane = lax.broadcasted_iota(jnp.int32, (1, LANES), 1)
    out = jnp.zeros((1, LANES), f32)
    for h in range(heads):
        out = jnp.where(lane == heads + h, row[0:1, h : h + 1], out)
    return out


def silu_parts(a):
    s = jax.nn.sigmoid(a)
    return a * s, s * (1.0 + a * (1.0 - s))


def conv_pre(ext, kern, base, cols, size, margin):
    total = None
    for j in range(margin + 1):
        tap = kern[j : j + 1, cols.start - base : cols.stop - base]
        term = tap * ext[pl.ds(HALO - margin + j, size), cols]
        total = term if total is None else total + term
    return total


def decay_terms(small, rate, bias, heads):
    size = small.shape[0]
    rows, cols = iotas(size)
    log_decay = -jnp.exp(rate) * softplus(small + bias)
    tril = jnp.where(rows >= cols, 1.0, 0.0).astype(f32)
    cum = exact(tril, log_decay)
    return log_decay, cum


def head_decay(cum, cum_t, at, rows, cols):
    g = cum[:, at : at + 1]
    spread = g - cum_t[at : at + 1, :]
    keep = rows >= cols
    return g, jnp.where(keep, jnp.exp(jnp.where(keep, spread, 0.0)), 0.0)


def front_body(
    heads, key_dim, value_dim, margin, slices,
    xs, halo, gain, wq, wk, wv, wg, wb, wa, kq, kk, kv, rate, bias,
    normed_o, ext_o, gate_o, small_o, cum_o, q_o, k_o, v_o, inv_o, p_o, w_o, u_o, wsm_o, send_o, ext,
):
    size = xs.shape[0]
    for ref, lo, hi in ((halo, 0, HALO), (xs, HALO, HALO + size)):
        x = ref[...].astype(f32)
        scale = lax.rsqrt(jnp.mean(x * x, axis=-1, keepdims=True) + EPS)
        normed_o[lo:hi, :] = (x * scale * gain[...]).astype(bf16)
    normed = normed_o[...]
    wsm_o[...] = jnp.zeros(wsm_o.shape, bf16)
    wsm_o[:heads, :] = wb[...]
    wsm_o[heads : 2 * heads, :] = wa[...]
    kc, vc = heads * key_dim, heads * value_dim
    for ref, lo, hi in ((wq, 0, kc), (wk, kc, 2 * kc), (wv, 2 * kc, 2 * kc + vc)):
        part = nn(normed, ref[...]).astype(bf16)
        ext_o[:, lo:hi] = part
        ext[:, lo:hi] = part.astype(f32)
    own = normed[HALO:]
    small = nt(own, wsm_o[...])
    small_o[...] = small
    beta_all = jax.nn.sigmoid(small)
    log_decay, cum = decay_terms(small, place(rate, heads), place(bias, heads), heads)
    cum_o[...] = cum
    cum_t = cum.T
    rows, cols = iotas(size)
    width = value_dim // slices
    kept = [None] * heads

    def start(h):
        ks = slice(h * key_dim, (h + 1) * key_dim)
        vs = slice(h * value_dim, (h + 1) * value_dim)
        kh = jax.nn.silu(conv_pre(ext, kk, kc, slice(kc + ks.start, kc + ks.stop), size, margin))
        qh = jax.nn.silu(conv_pre(ext, kq, 0, ks, size, margin))
        yield
        k = kh * lax.rsqrt(row_sum(kh * kh) + EPS)
        q = qh * (lax.rsqrt(row_sum(qh * qh) + EPS) * key_dim**-0.5)
        q_o[:, ks] = q
        k_o[:, ks] = k
        dots = nt(jnp.concatenate([k, q], axis=0), k)
        yield
        beta = beta_all[:, h : h + 1]
        g, decay = head_decay(cum, cum_t, heads + h, rows, cols)
        low = jnp.where(rows > cols, beta * decay * dots[:size], 0.0)
        p_o[:, h * size : (h + 1) * size] = (dots[size:] * decay).astype(bf16)
        kept[h] = (ks, vs, beta, g, low)
        yield
        v_o[:, vs] = jax.nn.silu(conv_pre(ext, kv, 2 * kc, slice(2 * kc + vs.start, 2 * kc + vs.stop), size, margin))

    in_step(start(h) for h in range(heads))
    invs = unit_lower_inverses([item[-1] for item in kept])
    solved_all = []
    for (ks, vs, beta, g, _), inv in zip(kept, invs, strict=True):
        rhs = jnp.concatenate([beta * v_o[:, vs], (beta * jnp.exp(g)) * k_o[:, ks]], axis=1)
        solved_all.append(nn(inv, rhs))
    for h, (ks, vs, beta, g, _) in enumerate(kept):
        inv_o[:, h * size : (h + 1) * size] = invs[h].astype(bf16)
        last = cum[size - 1 : size, heads + h : heads + h + 1]
        solved = solved_all[h]
        kt = k_o[:, ks] * jnp.exp(last - g)
        maps = tn(solved, kt)
        er, ec = iotas(key_dim)
        at = jnp.where(er == ec, jnp.exp(last), 0.0) - maps[value_dim:]
        bt = maps[:value_dim].astype(bf16)
        at = at.astype(bf16)
        for s in range(slices):
            send_o[h * slices + s, :key_dim, :] = at
            send_o[h * slices + s, key_dim:, :] = bt[s * width : (s + 1) * width]
        w_o[:, ks] = solved[:, value_dim:].astype(bf16)
        u_o[:, vs] = solved[:, :value_dim]
    gate_o[...] = nn(own, wg[...])


def split(a):
    hi = a.astype(bf16)
    return hi, (a - hi.astype(f32)).astype(bf16)


def scan_fwd_body(key_dim, maps, out):
    n, rows, _ = maps.shape
    state = jnp.zeros((rows - key_dim, key_dim), f32)
    for j in range(n):
        out[j] = state.astype(bf16)
        if j < n - 1:
            hi, lo = split(state)
            a = maps[j, :key_dim, :]
            state = nn(hi, a) + nn(lo, a) + maps[j, key_dim:, :].astype(f32)


def scan_bwd_body(key_dim, maps, local, out):
    n = maps.shape[0]
    rows = out.shape[1]
    state = jnp.zeros(out.shape[1:], f32)
    for j in range(n - 1, -1, -1):
        out[j] = state.astype(bf16)
        if j > 0:
            hi, lo = split(state)
            a = maps[j, :key_dim, :]
            state = nt(hi, a) + nt(lo, a) + local[j, :rows, :].astype(f32)


def mix_body(
    heads, key_dim, value_dim,
    st, u, w, p, q, cum, gate, gain, wo,
    stored_o, mixed_o, gated_o, part_o,
):
    size = u.shape[0]

    def one(h):
        ks = slice(h * key_dim, (h + 1) * key_dim)
        vs = slice(h * value_dim, (h + 1) * value_dim)
        both = nt(jnp.concatenate([w[:, ks], q[:, ks].astype(bf16)], axis=0), st[h])
        yield
        stored = (u[:, vs] - both[:size]).astype(bf16)
        stored_o[:, vs] = stored
        inner = nn(p[:, h * size : (h + 1) * size], stored)
        yield
        eg = jnp.exp(cum[:, heads + h : heads + h + 1])
        mixed = eg * both[size:] + inner
        mixed_o[:, vs] = mixed
        scale = lax.rsqrt(jnp.mean(mixed * mixed, axis=-1, keepdims=True) + EPS)
        gated_o[:, vs] = (mixed * scale * gain[...] * jax.nn.silu(gate[:, vs])).astype(bf16)

    in_step(one(h) for h in range(heads))
    part_o[...] = nn(gated_o[...], wo[...]).astype(bf16)


def hidden_body(og, w_down, out):
    out[...] = nt(og[...], w_down[...]).astype(bf16)


def ffn_body(x, mine, other, gain, w_gate, w_up, w_down, grad_hidden, input_o, hid_o, gg_o, gu_o, back_o, down_o):
    r = x[...].astype(f32) + (mine[...].astype(f32) + other[...].astype(f32))
    scale = lax.rsqrt(jnp.mean(r * r, axis=-1, keepdims=True) + EPS)
    ffn_in = (r * scale * gain[...]).astype(bf16)
    input_o[...] = ffn_in
    gate = nn(ffn_in, w_gate[...])
    up = nn(ffn_in, w_up[...])
    sig = jax.nn.sigmoid(gate)
    gh = grad_hidden[...].astype(f32)
    gu_o[...] = (gh * gate * sig).astype(bf16)
    gg_o[...] = (gh * up * sig * (1.0 + gate * (1.0 - sig))).astype(bf16)
    hid_o[...] = (gate * sig * up).astype(bf16)
    back_o[...] = (nt(gg_o[...], w_gate[...]) + nt(gu_o[...], w_up[...])).astype(bf16)
    down_o[...] = nn(hid_o[...], w_down[...]).astype(bf16)


def turn_body(
    heads, key_dim, value_dim, slices,
    x, mine, other, back_mine, back_other, og, ffn_gain, wo, gated, mixed, gate, out_gain, p, w, q, cum, _,
    gres_o, dfg_o, dmix_o, pdo_o, dgate_o, dog_o, send_o, grads_o, buf, sem,
):
    xf = x[...].astype(f32)
    in_scale = lax.rsqrt(jnp.mean(xf * xf, axis=-1, keepdims=True) + EPS)
    r = xf + (mine[...].astype(f32) + other[...].astype(f32))
    scale = lax.rsqrt(jnp.mean(r * r, axis=-1, keepdims=True) + EPS)
    b = back_mine[...].astype(f32) + back_other[...].astype(f32)
    normal = r * scale
    dfg_o[...] = col_sum(b * normal)
    d = b * ffn_gain[...]
    gres = og[...].astype(f32) + scale * (d - normal * jnp.mean(d * normal, axis=-1, keepdims=True))
    gres_o[...] = gres
    low = gres.astype(bf16)
    dgated = nt(low, wo[...])
    buf[...] = tn(low, gated[...]).astype(bf16)
    copy = pltpu.make_async_copy(
        buf, grads_o.at[:, pl.ds(grads_o.shape[1] - buf.shape[1], buf.shape[1])], sem.at[0]
    )
    copy.start()
    size = r.shape[0]
    width = value_dim // slices
    dogs = [None] * heads

    def one(h):
        ks = slice(h * key_dim, (h + 1) * key_dim)
        vs = slice(h * value_dim, (h + 1) * value_dim)
        m = mixed[:, vs]
        scale_h = lax.rsqrt(jnp.mean(m * m, axis=-1, keepdims=True) + EPS)
        n = m * scale_h
        act, dact = silu_parts(gate[:, vs])
        dg = dgated[:, vs]
        dgate = (dg * (n * out_gain[...]) * dact).astype(bf16)
        dgate_o[:, vs] = dgate
        scaled = (dgate.astype(f32) * in_scale).T.astype(bf16)
        dn = dg * act
        dogs[h] = col_sum(dn * n)
        dn = dn * out_gain[...]
        dm = scale_h * (dn - n * jnp.mean(dn * n, axis=-1, keepdims=True))
        dm = dm.astype(bf16)
        dmix_o[:, vs] = dm
        pdo = tn(p[:, h * size : (h + 1) * size], dm)
        yield
        pdo_o[:, vs] = pdo
        eg = jnp.exp(cum[:, heads + h : heads + h + 1])
        left = jnp.concatenate([dm, -pdo.astype(bf16)], axis=0)
        right = jnp.concatenate([(q[:, ks] * eg).astype(bf16), w[:, ks]], axis=0)
        local = tn(left, right).astype(bf16)
        yield
        for s in range(slices):
            send_o[h * slices + s, :width, :] = local[s * width : (s + 1) * width]
            send_o[h * slices + s, width:, :] = scaled[s * width : (s + 1) * width]

    in_step(one(h) for h in range(heads))
    dog_o[...] = sum(dogs[1:], dogs[0])
    copy.wait()


def back_body(
    heads, key_dim, value_dim, margin,
    dst, st, xs, halo, normed, ext_i, kq, kk, kv, q_i, k_i, v_i, inv_i, p_i, stored_i, dmix_i, pdo_i, dgate_i,
    small, cum_i, rate_i, bias_i, dog_mine, dog_other, wq, wk, wv, wg, wsm,
    send_o, part_o, wsmall_o, ext, pad, flat,
):
    size = q_i.shape[0]
    total = size + HALO
    kc, vc = heads * key_dim, heads * value_dim
    proj = 2 * kc + vc
    ext[...] = ext_i[...].astype(f32)
    pad[:HALO, :] = jnp.zeros((HALO, proj), f32)
    pad[HALO + size :, :] = jnp.zeros((HALO, proj), f32)
    sm = small[...]
    cum = cum_i[...]
    rate, bias = place(rate_i, heads), place(bias_i, heads)
    log_decay = -jnp.exp(rate) * softplus(sm + bias)
    cum_t = cum.T
    beta_all = jax.nn.sigmoid(sm)
    rows, cols = iotas(size)
    lane = lax.broadcasted_iota(jnp.int32, (size, LANES), 1)
    end_row = lax.broadcasted_iota(jnp.int32, (size, 1), 0) == size - 1
    dcums, dbetas = [None] * heads, [None] * heads

    blocks = proj // LANES
    flat[...] = jnp.zeros(flat.shape, f32)

    def conv_back(dy, kern, base, lo, hi):
        cs = slice(lo, hi)
        pre = conv_pre(ext, kern, base, cs, size, margin)
        _, dact = silu_parts(pre)
        dpre = dy * dact
        pad[pl.ds(HALO, size), cs] = dpre
        for j in range(margin + 1):
            tap = col_sum(dpre * ext[pl.ds(HALO - margin + j, size), cs])
            for c in range((hi - lo) // LANES):
                at = j * blocks + lo // LANES + c
                flat[at : at + 1, :] = tap[:, c * LANES : (c + 1) * LANES]

    def one(h):
        ks = slice(h * key_dim, (h + 1) * key_dim)
        vs = slice(h * value_dim, (h + 1) * value_dim)
        ps = slice(h * size, (h + 1) * size)
        q, k, v = q_i[:, ks], k_i[:, ks], v_i[:, vs]
        stored, do = stored_i[:, vs], dmix_i[:, vs]
        s, ds = st[h], dst[h]
        beta = beta_all[:, h : h + 1]
        g, decay = head_decay(cum, cum_t, heads + h, rows, cols)
        eg = jnp.exp(g)
        last = cum[size - 1 : size, heads + h : heads + h + 1]
        kt = k * jnp.exp(last - g)
        kl, ql = k.astype(bf16), q.astype(bf16)
        states = nt(jnp.concatenate([kl, ql], axis=0), s)
        dstored = pdo_i[:, vs] + nt(kt, ds)
        yield
        dr = tn(inv_i[:, ps], dstored)
        dkt = nn(stored, ds)
        dots = nt(kl, kl)
        yield
        drl = dr.astype(bf16)
        k_s, q_s = states[:size], states[size:]
        both = jnp.concatenate([drl, do], axis=0)
        inner = nt(both, stored)
        back = nn(both, s)
        yield
        scaled = decay * dots
        dlow = jnp.where(rows > cols, -inner[:size], 0.0)
        dp = jnp.where(rows >= cols, inner[size:], 0.0)
        dv = beta * dr
        spread = dlow * (beta * scaled) + dp * p_i[:, ps].astype(f32)
        dqk = (dp * decay).astype(bf16)
        dkk = dlow * (beta * decay)
        left = jnp.concatenate([dqk, (dkk + dkk.T).astype(bf16)], axis=0)
        on_k = nn(left, kl)
        on_q = tn(dqk, ql)
        yield
        dq = on_k[:size] + eg * back[size:]
        tail_part = row_sum(dkt * kt)
        dk = on_k[size:] + on_q - (beta * eg) * back[:size] + jnp.exp(last - g) * dkt
        dbeta = row_sum(dr * (v - eg * k_s)) + row_sum(dlow * scaled)
        dg = row_sum(spread) - row_sum(spread.T) - tail_part
        dg = dg + eg * row_sum(do.astype(f32) * q_s) - (beta * eg) * row_sum(dr * k_s)
        carry = col_sum(row_sum(s.astype(f32) * ds.astype(f32)))
        at_end = col_sum(tail_part) + jnp.exp(last) * carry
        dg = dg + jnp.where(end_row, at_end, 0.0)
        dcums[h] = jnp.where(lane == heads + h, dg, 0.0)
        dbetas[h] = jnp.where(lane == h, dbeta, 0.0)
        yield
        qh = jax.nn.silu(conv_pre(ext, kq, 0, ks, size, margin))
        rq = lax.rsqrt(row_sum(qh * qh) + EPS)
        unit = qh * rq
        dqn = dq * key_dim**-0.5
        conv_back(rq * (dqn - unit * row_sum(dqn * unit)), kq, 0, ks.start, ks.stop)
        kh = jax.nn.silu(conv_pre(ext, kk, kc, slice(kc + ks.start, kc + ks.stop), size, margin))
        rk = lax.rsqrt(row_sum(kh * kh) + EPS)
        conv_back(rk * (dk - k * row_sum(dk * k)), kk, kc, kc + ks.start, kc + ks.stop)
        conv_back(dv, kv, 2 * kc, 2 * kc + vs.start, 2 * kc + vs.stop)

    in_step(one(h) for h in range(heads))
    dcum, dbeta_all = sum(dcums[1:], dcums[0]), sum(dbetas[1:], dbetas[0])
    triu = jnp.where(rows <= cols, 1.0, 0.0).astype(f32)
    dlog = exact(triu, dcum)
    dalpha = dlog * (-jnp.exp(rate)) * jax.nn.sigmoid(sm + bias)
    dsmall = dalpha + dbeta_all * beta_all * (1.0 - beta_all)
    taps = (margin + 1) * blocks
    flat[taps : taps + 1, :] = col_sum(dlog * log_decay)
    flat[taps + 1 : taps + 2, :] = col_sum(dalpha)
    dog = dog_mine[...] + dog_other[...]
    for c in range(value_dim // LANES):
        flat[taps + 2 + c : taps + 3 + c, :] = dog[:, c * LANES : (c + 1) * LANES]
    x = xs[...].astype(f32)
    scale = lax.rsqrt(jnp.mean(x * x, axis=-1, keepdims=True) + EPS)
    hx = halo[...].astype(f32)
    hscale = lax.rsqrt(jnp.mean(hx * hx, axis=-1, keepdims=True) + EPS)
    peers = send_o.shape[0]
    qn, vn = kc // peers, vc // peers
    acc = None
    for ref, kern, lo, hi, n, at in (
        (wq, kq, 0, kc, qn, 0), (wk, kk, kc, 2 * kc, qn, qn), (wv, kv, 2 * kc, proj, vn, 2 * qn),
    ):
        dext = None
        for j in range(margin + 1):
            term = kern[j : j + 1, :] * pad[pl.ds(margin - j, total), lo:hi]
            dext = term if dext is None else dext + term
        part = nt(dext, ref[...])
        acc = part if acc is None else acc + part
        own = (dext[HALO:] * scale).T.astype(bf16)
        rim = (dext[:HALO] * hscale).astype(bf16)
        for e in range(peers):
            send_o[e, at : at + n, :] = own[e * n : (e + 1) * n]
            send_o[e, 2 * qn + vn : 2 * qn + vn + HALO, at : at + n] = rim[:, e * n : (e + 1) * n]
    dgate = dgate_i[...]
    fl = flat[...].astype(bf16)
    for e in range(peers):
        send_o[e, 2 * qn + vn + HALO :, :] = fl[e * HALO : (e + 1) * HALO]
    dsl = dsmall.astype(bf16)
    wsmall_o[...] = tn(dsl, normed[HALO:, :])[: wsmall_o.shape[0]]
    part_o[:HALO, :] = acc[:HALO].astype(bf16)
    part_o[HALO:, :] = (acc[HALO:] + nt(dgate, wg[...]) + nn(dsl, wsm[...])).astype(bf16)


def finish_body(heads, xs, gain, part, part_other, rim, rim_other, gres, wsmall, dfg, input_o, tail_o):
    size = xs.shape[0]
    x = xs[...].astype(f32)
    scale = lax.rsqrt(jnp.mean(x * x, axis=-1, keepdims=True) + EPS)
    normal = x * scale
    g = part[HALO:, :].astype(f32) + part_other[HALO:, :].astype(f32)
    edge = rim[...].astype(f32) + rim_other[...].astype(f32)
    g = jnp.concatenate([g[: size - HALO], g[size - HALO :] + edge], axis=0)
    tail_o[...] = jnp.zeros(tail_o.shape, f32)
    tail_o[: 2 * heads, :] = wsmall[: 2 * heads, :]
    tail_o[2 * heads : 2 * heads + 1, :] = col_sum(g * normal)
    tail_o[2 * heads + 1 : 2 * heads + 2, :] = dfg[...]
    d = g * gain[...]
    input_o[...] = gres[...] + scale * (d - normal * jnp.mean(d * normal, axis=-1, keepdims=True))


def gather_body(split_at, pieces, recv, gates, *refs):
    parts = refs[:pieces]
    gain, tail, which, send_o, lhs = refs[pieces:]
    peers, _, size = recv.shape
    mixed = recv.shape[1] - 2 * HALO
    n = mixed + split_at
    width = gain.shape[1]
    rows = width // peers
    flat = jnp.zeros((HALO, LANES), f32)
    edge = []
    for j in range(peers):
        cols = slice(j * size, (j + 1) * size)
        lhs[:mixed, cols] = recv[j, :mixed, :]
        lhs[mixed:, cols] = gates[j, split_at:, :]
        edge.append(recv[j, mixed : mixed + HALO, :])
        flat = flat + recv[j, mixed + HALO :, :].astype(f32)
    edge = jnp.concatenate(edge, axis=0)
    products, extras = [], []
    for xg in parts:
        none = jnp.zeros((HALO, xg.shape[1]), bf16)
        near = [xg[j * size - HALO : j * size, :] if j else none for j in range(peers)]
        products.append(nn(lhs[...], xg[...]))
        extras.append(tn(edge, jnp.concatenate(near, axis=0)))
    if pieces == 2:
        first = which[0:1, 0:1] == 0
        products = [jnp.where(first, *products), jnp.where(first, *products[::-1])]
        extras = [jnp.where(first, *extras), jnp.where(first, *extras[::-1])]
    acc = jnp.concatenate(products, axis=1)
    extra = jnp.concatenate(extras, axis=1)
    top = (acc[:mixed] + extra[:mixed]) * gain[...]
    rest = acc[mixed:] * gain[...]
    half = rows // 2
    wide = mixed == LANES
    if wide:
        top, rest = top.T.astype(bf16), rest.T.astype(bf16)
    else:
        fill = jnp.zeros((LANES - n, width), f32)
        top, half = jnp.concatenate([top, rest, fill], axis=0).T.astype(bf16), 0
    fl = flat.astype(bf16)
    small = tail[...].astype(bf16)
    for e in range(peers):
        lo = e * rows
        block = lo // LANES * LANES
        send_o[e, :rows, :] = top[lo : lo + rows]
        if wide:
            send_o[e, rows : rows + half, :] = jnp.concatenate(
                [rest[lo : lo + half], rest[lo + half : lo + rows]], axis=1
            )
        send_o[e, rows + half : rows + half + 2 * HALO, :] = small[:, block : block + LANES]
        send_o[e, rows + half + 2 * HALO :, :] = fl


def scatter_body(heads, qn, vn, margin, recv, side, q_o, k_o, v_o, g_o, wb_o, wa_o, ag_o, fg_o, cq_o, ck_o, cv_o, rate_o, bias_o, og_o):
    peers = recv.shape[0]
    rows = q_o.shape[0]
    wide = 2 * qn + vn == LANES
    half = rows // 2 if wide else 0
    low = jnp.zeros((2 * HALO, LANES), f32)
    lines = []
    for e in range(peers):
        top = recv[e, :rows, :].astype(f32)
        q_o[:, e * qn : (e + 1) * qn] = top[:, :qn]
        k_o[:, e * qn : (e + 1) * qn] = top[:, qn : 2 * qn]
        v_o[:, e * vn : (e + 1) * vn] = top[:, 2 * qn : 2 * qn + vn]
        if wide:
            rest = recv[e, rows : rows + half, :].astype(f32)
            g_o[:half, e * vn : (e + 1) * vn] = rest[:, :vn]
            g_o[half:, e * vn : (e + 1) * vn] = rest[:, vn:]
        else:
            g_o[:, e * vn : (e + 1) * vn] = top[:, 2 * qn + vn : 2 * (qn + vn)]
        low = low + recv[e, rows + half : rows + half + 2 * HALO, :].astype(f32)
        lines.append(recv[e, rows + half + 2 * HALO :, :].astype(f32))
    picked = low[:, :rows]
    for s in range(1, LANES // rows):
        picked = jnp.where(side[0:1, 0:1] == s, low[:, s * rows : (s + 1) * rows], picked)
    wb_o[...] = picked[:heads]
    wa_o[...] = picked[heads : 2 * heads]
    ag_o[...] = picked[2 * heads : 2 * heads + 1]
    fg_o[...] = picked[2 * heads + 1 : 2 * heads + 2]

    def line(at):
        return lines[at // HALO][at % HALO : at % HALO + 1]

    kb, vb = cq_o.shape[1] // LANES, cv_o.shape[1] // LANES
    blocks = 2 * kb + vb
    for j in range(margin + 1):
        for c in range(blocks):
            at = j * blocks + c
            ref, to = (cq_o, c) if c < kb else (ck_o, c - kb) if c < 2 * kb else (cv_o, c - 2 * kb)
            ref[j : j + 1, to * LANES : (to + 1) * LANES] = line(at)
    at = (margin + 1) * blocks
    rate_o[...] = line(at)[:, heads : 2 * heads]
    bias_o[...] = line(at + 1)[:, heads : 2 * heads]
    for c in range(og_o.shape[1] // LANES):
        og_o[:, c * LANES : (c + 1) * LANES] = line(at + 2 + c)


def ffn_grads_body(inputs, gg, gu, og, hid, out, buf, sems):
    width = inputs.shape[1]
    ff = gg.shape[1]
    step = buf.shape[2] // 3
    copies = []
    for i in range(width // LANES):
        slot = i % 2
        cols = slice(i * LANES, (i + 1) * LANES)
        if i >= 2:
            copies[i - 2].wait()
        lhs = inputs[:, cols]
        buf[slot, :, :ff] = tn(lhs, gg[...]).astype(bf16)
        buf[slot, :, step : step + ff] = tn(lhs, gu[...]).astype(bf16)
        buf[slot, :, 2 * step : 2 * step + ff] = tn(og[:, cols], hid[...]).astype(bf16)
        copy = pltpu.make_async_copy(buf.at[slot], out.at[cols, pl.ds(0, 3 * step)], sems.at[slot])
        copy.start()
        copies.append(copy)
    for copy in copies[-2:]:
        copy.wait()


def shift_along(block, axis, distance):
    devices = range(lax.axis_size(axis))
    route = [(i - distance, i) for i in devices if i - distance in devices]
    return lax.ppermute(block, axis, route)


def pair(part):
    if lax.axis_size("tensor") == 2:
        return part, lax.ppermute(part, "tensor", [(0, 1), (1, 0)])
    return lax.psum(part, "tensor"), jnp.zeros_like(part)


def swap(blocks):
    return lax.all_to_all(blocks, "dp", 0, 0, tiled=True)


def on_device(
    block_input, output_grad, attn_gain, w_query, w_key, w_value, conv_query, conv_key, conv_value,
    w_beta, w_alpha, a_log, dt_bias, w_gate_out, out_gain, w_out, ffn_gain, w_gate, w_up, w_down,
):
    size, width = block_input.shape
    heads = a_log.shape[0]
    key_dim = w_query.shape[1] // heads
    value_dim = w_value.shape[1] // heads
    margin = conv_query.shape[0] - 1
    peers = lax.axis_size("dp")
    slices = peers // heads
    kc, vc, gc, ff = w_query.shape[1], w_value.shape[1], w_gate_out.shape[1], w_gate.shape[1]
    proj = 2 * kc + vc
    dims = (heads, key_dim, value_dim)
    rows = width // peers

    halo = shift_along(block_input[-HALO:], "dp", 1)
    rate, bias = a_log[None], dt_bias[None]
    again, fgain, ogain = attn_gain[None], ffn_gain[None], out_gain[None]

    normed, ext, gate_pre, small, cum, q, k, v, inv, p, w, u, wsm, send = call(
        functools.partial(front_body, *dims, margin, slices),
        [
            ((size + HALO, width), bf16), ((size + HALO, proj), bf16), ((size, gc), f32),
            ((size, LANES), f32), ((size, LANES), f32), ((size, kc), f32), ((size, kc), f32), ((size, vc), f32),
            ((size, heads * size), bf16), ((size, heads * size), bf16), ((size, kc), bf16),
            ((size, vc), f32), ((LANES, width), bf16),
            ((peers, key_dim + value_dim // slices, key_dim), bf16),
        ],
        block_input, halo, again, w_query, w_key, w_value, w_gate_out, w_beta.T, w_alpha.T,
        conv_query, conv_key, conv_value, rate, bias,
        scratch=[pltpu.VMEM((size + HALO, proj), f32)],
    )
    maps = swap(send)
    maps, late_input = lax.optimization_barrier((maps, block_input))
    paired = lax.axis_size("tensor") == 2
    if paired:
        half = width // 2
        late_input = lax.dynamic_slice_in_dim(late_input, lax.axis_index("tensor") * half, half, 1)
    everyone = lax.all_gather(late_input, "dp", axis=0, tiled=True)
    piece = (peers, value_dim // slices, key_dim)
    (entry,) = call(functools.partial(scan_fwd_body, key_dim), [(piece, bf16)], maps)
    st = swap(entry).reshape(heads, value_dim, key_dim)
    stored, mixed, gated, mix_part = call(
        functools.partial(mix_body, *dims),
        [((size, vc), bf16), ((size, vc), f32), ((size, vc), bf16), ((size, width), bf16)],
        st, u, w, p, q, cum, gate_pre, ogain, w_out,
    )
    mix_part, late_grad = lax.optimization_barrier((mix_part, output_grad))
    mix_pair = pair(mix_part)
    (grad_hidden,) = call(hidden_body, [((size, ff), bf16)], late_grad, w_down, near=True)
    ffn_input, hidden, gga, gua, back_part, down_part = call(
        ffn_body,
        [((size, width), bf16), ((size, ff), bf16), ((size, ff), bf16), ((size, ff), bf16),
         ((size, width), bf16), ((size, width), bf16)],
        block_input, *mix_pair, fgain, w_gate, w_up, w_down, grad_hidden, near=True, home=(4, 5),
    )
    back_pair = pair(back_part)
    step = -(-ff // LANES) * LANES
    total = 3 * step + gc
    (early,) = call(
        ffn_grads_body, [((width, total), bf16)], ffn_input, gga, gua, output_grad, hidden,
        scratch=[pltpu.VMEM((2, LANES, 3 * step), bf16), pltpu.SemaphoreType.DMA((2,))],
        raw=(("out", 0),), home=(0,), near=True,
    )
    back_pair, early = lax.optimization_barrier((back_pair, early))
    gres, dfg, dmix, pdo, dgate, dog, send_back, early = call(
        functools.partial(turn_body, *dims, slices),
        [((size, width), f32), ((1, width), f32), ((size, vc), bf16), ((size, vc), f32),
         ((size, gc), bf16), ((1, value_dim), f32),
         ((peers, 2 * piece[1], key_dim), bf16), ((width, total), bf16)],
        block_input, *mix_pair, *back_pair, output_grad, fgain, w_out, gated, mixed, gate_pre, ogain, p, w, q, cum,
        early,
        scratch=[pltpu.VMEM((width, gc), bf16), pltpu.SemaphoreType.DMA((1,))], raw=(16,), alias={16: 7}, near=True, home=range(7),
    )
    send_back, early, everyone = lax.optimization_barrier((send_back, early, everyone))
    pieces = pair(everyone) if paired else (everyone,)
    first = lax.psum_scatter(early, "dp", scatter_dimension=0, tiled=True).astype(f32)
    local = swap(send_back)
    (exits,) = call(functools.partial(scan_bwd_body, key_dim), [(piece, bf16)], maps, local)
    dst = swap(exits).reshape(heads, value_dim, key_dim)
    down_pair = pair(down_part)
    dog_pair = pair(dog)

    qn, vn = kc // peers, vc // peers
    share = 2 * (qn + vn)
    send, part, wsmall = call(
        functools.partial(back_body, *dims, margin),
        [((peers, share - vn + 2 * HALO, size), bf16), ((size + HALO, width), bf16), ((2 * HALO, width), f32)],
        dst, st, block_input, halo, normed, ext, conv_query, conv_key, conv_value,
        q, k, v, inv, p, stored, dmix, pdo, dgate,
        small, cum, rate, bias, *dog_pair, w_query, w_key, w_value, w_gate_out, wsm,
        scratch=[
            pltpu.VMEM((size + HALO, proj), f32), pltpu.VMEM((size + 2 * HALO, proj), f32),
            pltpu.VMEM((peers * HALO, LANES), f32),
        ],
    )
    rim_pair = pair(shift_along(part[:HALO], "dp", -1))
    part_pair = pair(part)
    recv = swap(send)
    input_grad, tail = call(
        functools.partial(finish_body, heads),
        [((size, width), f32), ((2 * HALO, width), f32)],
        block_input, again, *part_pair, *rim_pair, gres, wsmall, dfg,
    )
    wide = 2 * qn + vn == LANES
    packed = rows + (rows // 2 if wide else 0) + 3 * HALO
    (send,) = call(
        functools.partial(gather_body, vn, len(pieces)), [((peers, packed, LANES), bf16)],
        recv, local, *pieces, again, tail, jnp.full((1, 1), lax.axis_index("tensor"), jnp.int32),
        scratch=[pltpu.VMEM((share, peers * size), bf16)],
    )
    recv = swap(send)
    side = jnp.full((1, 1), lax.axis_index("dp") % (LANES // rows), jnp.int32)
    gq, gk, gv, gg, gwb, gwa, gag, gfg, gcq, gck, gcv, grate, gbias, gog = call(
        functools.partial(scatter_body, heads, qn, vn, margin),
        [((rows, kc), f32), ((rows, kc), f32), ((rows, vc), f32), ((rows, gc), f32),
         ((heads, rows), f32), ((heads, rows), f32), ((1, rows), f32), ((1, rows), f32),
         ((margin + 1, kc), f32), ((margin + 1, kc), f32), ((margin + 1, vc), f32),
         ((1, heads), f32), ((1, heads), f32), ((1, value_dim), f32)],
        recv, side,
    )
    block_output = (
        block_input.astype(f32) + (mix_pair[0].astype(f32) + mix_pair[1].astype(f32))
        + (down_pair[0].astype(f32) + down_pair[1].astype(f32))
    )
    return (
        block_output, input_grad, gag[0], gq, gk, gv, gcq, gck, gcv, gwb.T, gwa.T,
        grate[0], gbias[0], gg, gog[0],
        first[:, 3 * step :].T, gfg[0], first[:, :ff], first[:, step : step + ff], first[:, 2 * step : 2 * step + ff].T,
    )


def solution(mesh):
    rows, cols, whole = P("dp", None), P(None, "tensor"), P()
    heads, high = P("tensor"), P("tensor", None)
    in_specs = (
        rows, rows, whole, cols, cols, cols, cols, cols, cols, cols, cols, heads, heads,
        cols, whole, high, whole, cols, cols, high,
    )
    both, crossed, dp = P("dp", "tensor"), P("tensor", "dp"), P("dp")
    out_specs = (
        rows, rows, dp, both, both, both, cols, cols, cols, both, both, heads, heads,
        both, whole, crossed, dp, both, both, crossed,
    )
    return jax.shard_map(
        on_device, mesh=mesh, in_specs=in_specs, out_specs=out_specs, check_vma=False
    )
```

```python
import functools

import jax
import jax.numpy as jnp
from jax import lax
from jax.experimental import pallas as pl
from jax.experimental.pallas import tpu as pltpu
from jax.sharding import PartitionSpec as P

EPS = 1e-06
LANES = 128
HALO = 8
f32 = jnp.float32
bf16 = jnp.bfloat16


def nn(a, b):
    dims = (((1,), (0,)), ((), ()))
    return lax.dot_general(a.astype(bf16), b.astype(bf16), dims, preferred_element_type=f32)


def nt(a, b):
    dims = (((1,), (1,)), ((), ()))
    return lax.dot_general(a.astype(bf16), b.astype(bf16), dims, preferred_element_type=f32)


def tn(a, b):
    dims = (((0,), (0,)), ((), ()))
    return lax.dot_general(a.astype(bf16), b.astype(bf16), dims, preferred_element_type=f32)


def exact(a, b):
    dims = (((1,), (0,)), ((), ()))
    return lax.dot_general(a, b, dims, preferred_element_type=f32, precision=lax.Precision.HIGHEST)


def row_sum(a):
    return jnp.sum(a, axis=-1, keepdims=True)


def col_sum(a):
    return jnp.sum(a, axis=0, keepdims=True)


def iotas(size):
    return (
        lax.broadcasted_iota(jnp.int32, (size, size), 0),
        lax.broadcasted_iota(jnp.int32, (size, size), 1),
    )


def exact3(a, b):
    (ah, al), (bh, bl) = a, b
    return nn(ah, bh) + (nn(ah, bl) + nn(al, bh))


def unit_lower_inverses(lows):
    size = lows[0].shape[0]
    rows, cols = iotas(size)

    def same(shift):
        return lax.shift_right_logical(rows, shift) == lax.shift_right_logical(cols, shift)

    def each(f, *lists):
        return [f(*items) for items in zip(*lists, strict=True)]

    eye = jnp.where(rows == cols, 1.0, 0.0).astype(f32)
    shift = 3
    diags = [jnp.where(same(shift), low, 0.0) for low in lows]
    invs = [eye - diag for diag in diags]
    powers = each(split, diags)
    for _ in range(shift - 1):
        powers = each(split, each(exact3, powers, powers))
        invs = each(lambda x, y: x + y, invs, each(exact3, each(split, invs), powers))
    while (1 << shift) < size:
        keep = same(shift + 1) & jnp.logical_not(same(shift))
        offs = [split(jnp.where(keep, low, 0.0)) for low in lows]
        halves = each(split, invs)
        inner = each(split, each(exact3, offs, halves))
        invs = each(lambda x, y: x - y, invs, each(exact3, halves, inner))
        shift += 1
    return invs


WHOLE = 60000 * 1024
NEAR = 20 * 1024 * 1024


def call(body, outs, *args, scratch=(), raw=(), alias=None, near=False, home=()):
    alias = alias or {}
    held = set(alias.values())
    far = pl.BlockSpec(memory_space=pltpu.HBM)
    here = pl.BlockSpec(memory_space=pltpu.VMEM) if near else pl.BlockSpec()
    return pl.pallas_call(
        body,
        name=getattr(body, "func", body).__name__,
        out_shape=[
            (pltpu.HBM if i in home or i in held else jax.ShapeDtypeStruct)(s, d)
            for i, (s, d) in enumerate(outs)
        ],
        in_specs=[far if i in raw else here for i in range(len(args))],
        out_specs=[
            far if i in held or ("out", i) in raw else pl.BlockSpec() if i in home else here
            for i in range(len(outs))
        ],
        input_output_aliases=alias,
        scratch_shapes=list(scratch),
        compiler_params=pltpu.CompilerParams(vmem_limit_bytes=NEAR if near else WHOLE),
    )(*args)


def in_step(steps):
    steps = list(steps)
    while steps:
        steps = [step for step in steps if next(step, True) is None]


def softplus(a):
    return jnp.maximum(a, 0.0) + jnp.log1p(jnp.exp(-jnp.abs(a)))


def place(row, heads):
    lane = lax.broadcasted_iota(jnp.int32, (1, LANES), 1)
    out = jnp.zeros((1, LANES), f32)
    for h in range(heads):
        out = jnp.where(lane == heads + h, row[0:1, h : h + 1], out)
    return out


def silu_parts(a):
    s = jax.nn.sigmoid(a)
    return a * s, s * (1.0 + a * (1.0 - s))


def conv_pre(ext, kern, base, cols, size, margin):
    total = None
    for j in range(margin + 1):
        tap = kern[j : j + 1, cols.start - base : cols.stop - base]
        term = tap * ext[pl.ds(HALO - margin + j, size), cols]
        total = term if total is None else total + term
    return total


def decay_terms(small, rate, bias, heads):
    size = small.shape[0]
    rows, cols = iotas(size)
    log_decay = -jnp.exp(rate) * softplus(small + bias)
    tril = jnp.where(rows >= cols, 1.0, 0.0).astype(f32)
    cum = exact(tril, log_decay)
    return log_decay, cum


def head_decay(cum, cum_t, at, rows, cols):
    g = cum[:, at : at + 1]
    spread = g - cum_t[at : at + 1, :]
    keep = rows >= cols
    return g, jnp.where(keep, jnp.exp(jnp.where(keep, spread, 0.0)), 0.0)


def front_body(
    heads, key_dim, value_dim, margin, slices,
    xs, halo, gain, wq, wk, wv, wg, wb, wa, kq, kk, kv, rate, bias,
    normed_o, ext_o, gate_o, small_o, cum_o, q_o, k_o, v_o, inv_o, p_o, w_o, u_o, wsm_o, send_o, ext,
):
    size = xs.shape[0]
    for ref, lo, hi in ((halo, 0, HALO), (xs, HALO, HALO + size)):
        x = ref[...].astype(f32)
        scale = lax.rsqrt(jnp.mean(x * x, axis=-1, keepdims=True) + EPS)
        normed_o[lo:hi, :] = (x * scale * gain[...]).astype(bf16)
    normed = normed_o[...]
    wsm_o[...] = jnp.zeros(wsm_o.shape, bf16)
    wsm_o[:heads, :] = wb[...]
    wsm_o[heads : 2 * heads, :] = wa[...]
    kc, vc = heads * key_dim, heads * value_dim
    for ref, lo, hi in ((wq, 0, kc), (wk, kc, 2 * kc), (wv, 2 * kc, 2 * kc + vc)):
        part = nn(normed, ref[...]).astype(bf16)
        ext_o[:, lo:hi] = part
        ext[:, lo:hi] = part.astype(f32)
    own = normed[HALO:]
    small = nt(own, wsm_o[...])
    small_o[...] = small
    beta_all = jax.nn.sigmoid(small)
    log_decay, cum = decay_terms(small, place(rate, heads), place(bias, heads), heads)
    cum_o[...] = cum
    cum_t = cum.T
    rows, cols = iotas(size)
    width = value_dim // slices
    kept = [None] * heads

    def start(h):
        ks = slice(h * key_dim, (h + 1) * key_dim)
        vs = slice(h * value_dim, (h + 1) * value_dim)
        kh = jax.nn.silu(conv_pre(ext, kk, kc, slice(kc + ks.start, kc + ks.stop), size, margin))
        qh = jax.nn.silu(conv_pre(ext, kq, 0, ks, size, margin))
        yield
        k = kh * lax.rsqrt(row_sum(kh * kh) + EPS)
        q = qh * (lax.rsqrt(row_sum(qh * qh) + EPS) * key_dim**-0.5)
        q_o[:, ks] = q
        k_o[:, ks] = k
        dots = nt(jnp.concatenate([k, q], axis=0), k)
        yield
        beta = beta_all[:, h : h + 1]
        g, decay = head_decay(cum, cum_t, heads + h, rows, cols)
        low = jnp.where(rows > cols, beta * decay * dots[:size], 0.0)
        p_o[:, h * size : (h + 1) * size] = (dots[size:] * decay).astype(bf16)
        kept[h] = (ks, vs, beta, g, low)
        yield
        v_o[:, vs] = jax.nn.silu(conv_pre(ext, kv, 2 * kc, slice(2 * kc + vs.start, 2 * kc + vs.stop), size, margin))

    in_step(start(h) for h in range(heads))
    invs = unit_lower_inverses([item[-1] for item in kept])
    solved_all = []
    for (ks, vs, beta, g, _), inv in zip(kept, invs, strict=True):
        rhs = jnp.concatenate([beta * v_o[:, vs], (beta * jnp.exp(g)) * k_o[:, ks]], axis=1)
        solved_all.append(nn(inv, rhs))
    for h, (ks, vs, beta, g, _) in enumerate(kept):
        inv_o[:, h * size : (h + 1) * size] = invs[h].astype(bf16)
        last = cum[size - 1 : size, heads + h : heads + h + 1]
        solved = solved_all[h]
        kt = k_o[:, ks] * jnp.exp(last - g)
        maps = tn(solved, kt)
        er, ec = iotas(key_dim)
        at = jnp.where(er == ec, jnp.exp(last), 0.0) - maps[value_dim:]
        bt = maps[:value_dim].astype(bf16)
        at = at.astype(bf16)
        for s in range(slices):
            send_o[h * slices + s, :key_dim, :] = at
            send_o[h * slices + s, key_dim:, :] = bt[s * width : (s + 1) * width]
        w_o[:, ks] = solved[:, value_dim:].astype(bf16)
        u_o[:, vs] = solved[:, :value_dim]
    gate_o[...] = nn(own, wg[...])


def split(a):
    hi = a.astype(bf16)
    return hi, (a - hi.astype(f32)).astype(bf16)


def scan_fwd_body(key_dim, maps, out):
    n, rows, _ = maps.shape
    state = jnp.zeros((rows - key_dim, key_dim), f32)
    for j in range(n):
        out[j] = state.astype(bf16)
        if j < n - 1:
            hi, lo = split(state)
            a = maps[j, :key_dim, :]
            state = nn(hi, a) + nn(lo, a) + maps[j, key_dim:, :].astype(f32)


def scan_bwd_body(key_dim, maps, local, out):
    n = maps.shape[0]
    rows = out.shape[1]
    state = jnp.zeros(out.shape[1:], f32)
    for j in range(n - 1, -1, -1):
        out[j] = state.astype(bf16)
        if j > 0:
            hi, lo = split(state)
            a = maps[j, :key_dim, :]
            state = nt(hi, a) + nt(lo, a) + local[j, :rows, :].astype(f32)


def mix_body(
    heads, key_dim, value_dim,
    st, u, w, p, q, cum, gate, gain, wo,
    stored_o, mixed_o, gated_o, part_o,
):
    size = u.shape[0]

    def one(h):
        ks = slice(h * key_dim, (h + 1) * key_dim)
        vs = slice(h * value_dim, (h + 1) * value_dim)
        both = nt(jnp.concatenate([w[:, ks], q[:, ks].astype(bf16)], axis=0), st[h])
        yield
        stored = (u[:, vs] - both[:size]).astype(bf16)
        stored_o[:, vs] = stored
        inner = nn(p[:, h * size : (h + 1) * size], stored)
        yield
        eg = jnp.exp(cum[:, heads + h : heads + h + 1])
        mixed = eg * both[size:] + inner
        mixed_o[:, vs] = mixed
        scale = lax.rsqrt(jnp.mean(mixed * mixed, axis=-1, keepdims=True) + EPS)
        gated_o[:, vs] = (mixed * scale * gain[...] * jax.nn.silu(gate[:, vs])).astype(bf16)

    in_step(one(h) for h in range(heads))
    part_o[...] = nn(gated_o[...], wo[...]).astype(bf16)


def hidden_body(og, w_down, out):
    out[...] = nt(og[...], w_down[...]).astype(bf16)


def ffn_body(x, mine, other, gain, w_gate, w_up, w_down, grad_hidden, input_o, hid_o, gg_o, gu_o, back_o, down_o):
    r = x[...].astype(f32) + (mine[...].astype(f32) + other[...].astype(f32))
    scale = lax.rsqrt(jnp.mean(r * r, axis=-1, keepdims=True) + EPS)
    ffn_in = (r * scale * gain[...]).astype(bf16)
    input_o[...] = ffn_in
    gate = nn(ffn_in, w_gate[...])
    up = nn(ffn_in, w_up[...])
    sig = jax.nn.sigmoid(gate)
    gh = grad_hidden[...].astype(f32)
    gu_o[...] = (gh * gate * sig).astype(bf16)
    gg_o[...] = (gh * up * sig * (1.0 + gate * (1.0 - sig))).astype(bf16)
    hid_o[...] = (gate * sig * up).astype(bf16)
    back_o[...] = (nt(gg_o[...], w_gate[...]) + nt(gu_o[...], w_up[...])).astype(bf16)
    down_o[...] = nn(hid_o[...], w_down[...]).astype(bf16)


def turn_body(
    heads, key_dim, value_dim, slices,
    x, mine, other, back_mine, back_other, og, ffn_gain, wo, gated, mixed, gate, out_gain, p, w, q, cum, _,
    gres_o, dfg_o, dmix_o, pdo_o, dgate_o, dog_o, send_o, grads_o, buf, sem,
):
    xf = x[...].astype(f32)
    in_scale = lax.rsqrt(jnp.mean(xf * xf, axis=-1, keepdims=True) + EPS)
    r = xf + (mine[...].astype(f32) + other[...].astype(f32))
    scale = lax.rsqrt(jnp.mean(r * r, axis=-1, keepdims=True) + EPS)
    b = back_mine[...].astype(f32) + back_other[...].astype(f32)
    normal = r * scale
    dfg_o[...] = col_sum(b * normal)
    d = b * ffn_gain[...]
    gres = og[...].astype(f32) + scale * (d - normal * jnp.mean(d * normal, axis=-1, keepdims=True))
    gres_o[...] = gres
    low = gres.astype(bf16)
    dgated = nt(low, wo[...])
    buf[...] = tn(low, gated[...]).astype(bf16)
    copy = pltpu.make_async_copy(
        buf, grads_o.at[:, pl.ds(grads_o.shape[1] - buf.shape[1], buf.shape[1])], sem.at[0]
    )
    copy.start()
    size = r.shape[0]
    width = value_dim // slices
    dogs = [None] * heads

    def one(h):
        ks = slice(h * key_dim, (h + 1) * key_dim)
        vs = slice(h * value_dim, (h + 1) * value_dim)
        m = mixed[:, vs]
        scale_h = lax.rsqrt(jnp.mean(m * m, axis=-1, keepdims=True) + EPS)
        n = m * scale_h
        act, dact = silu_parts(gate[:, vs])
        dg = dgated[:, vs]
        dgate = (dg * (n * out_gain[...]) * dact).astype(bf16)
        dgate_o[:, vs] = dgate
        scaled = (dgate.astype(f32) * in_scale).T.astype(bf16)
        dn = dg * act
        dogs[h] = col_sum(dn * n)
        dn = dn * out_gain[...]
        dm = scale_h * (dn - n * jnp.mean(dn * n, axis=-1, keepdims=True))
        dm = dm.astype(bf16)
        dmix_o[:, vs] = dm
        pdo = tn(p[:, h * size : (h + 1) * size], dm)
        yield
        pdo_o[:, vs] = pdo
        eg = jnp.exp(cum[:, heads + h : heads + h + 1])
        left = jnp.concatenate([dm, -pdo.astype(bf16)], axis=0)
        right = jnp.concatenate([(q[:, ks] * eg).astype(bf16), w[:, ks]], axis=0)
        local = tn(left, right).astype(bf16)
        yield
        for s in range(slices):
            send_o[h * slices + s, :width, :] = local[s * width : (s + 1) * width]
            send_o[h * slices + s, width:, :] = scaled[s * width : (s + 1) * width]

    in_step(one(h) for h in range(heads))
    dog_o[...] = sum(dogs[1:], dogs[0])
    copy.wait()


def back_body(
    heads, key_dim, value_dim, margin,
    dst, st, xs, halo, normed, ext_i, kq, kk, kv, q_i, k_i, v_i, inv_i, p_i, stored_i, dmix_i, pdo_i, dgate_i,
    small, cum_i, rate_i, bias_i, dog_mine, dog_other, wq, wk, wv, wg, wsm,
    send_o, part_o, wsmall_o, ext, pad, flat,
):
    size = q_i.shape[0]
    total = size + HALO
    kc, vc = heads * key_dim, heads * value_dim
    proj = 2 * kc + vc
    ext[...] = ext_i[...].astype(f32)
    pad[:HALO, :] = jnp.zeros((HALO, proj), f32)
    pad[HALO + size :, :] = jnp.zeros((HALO, proj), f32)
    sm = small[...]
    cum = cum_i[...]
    rate, bias = place(rate_i, heads), place(bias_i, heads)
    log_decay = -jnp.exp(rate) * softplus(sm + bias)
    cum_t = cum.T
    beta_all = jax.nn.sigmoid(sm)
    rows, cols = iotas(size)
    lane = lax.broadcasted_iota(jnp.int32, (size, LANES), 1)
    end_row = lax.broadcasted_iota(jnp.int32, (size, 1), 0) == size - 1
    dcums, dbetas = [None] * heads, [None] * heads

    blocks = proj // LANES
    flat[...] = jnp.zeros(flat.shape, f32)

    def conv_back(dy, kern, base, lo, hi):
        cs = slice(lo, hi)
        pre = conv_pre(ext, kern, base, cs, size, margin)
        _, dact = silu_parts(pre)
        dpre = dy * dact
        pad[pl.ds(HALO, size), cs] = dpre
        for j in range(margin + 1):
            tap = col_sum(dpre * ext[pl.ds(HALO - margin + j, size), cs])
            for c in range((hi - lo) // LANES):
                at = j * blocks + lo // LANES + c
                flat[at : at + 1, :] = tap[:, c * LANES : (c + 1) * LANES]

    def one(h):
        ks = slice(h * key_dim, (h + 1) * key_dim)
        vs = slice(h * value_dim, (h + 1) * value_dim)
        ps = slice(h * size, (h + 1) * size)
        q, k, v = q_i[:, ks], k_i[:, ks], v_i[:, vs]
        stored, do = stored_i[:, vs], dmix_i[:, vs]
        s, ds = st[h], dst[h]
        beta = beta_all[:, h : h + 1]
        g, decay = head_decay(cum, cum_t, heads + h, rows, cols)
        eg = jnp.exp(g)
        last = cum[size - 1 : size, heads + h : heads + h + 1]
        kt = k * jnp.exp(last - g)
        kl, ql = k.astype(bf16), q.astype(bf16)
        states = nt(jnp.concatenate([kl, ql], axis=0), s)
        dstored = pdo_i[:, vs] + nt(kt, ds)
        yield
        dr = tn(inv_i[:, ps], dstored)
        dkt = nn(stored, ds)
        dots = nt(kl, kl)
        yield
        drl = dr.astype(bf16)
        k_s, q_s = states[:size], states[size:]
        both = jnp.concatenate([drl, do], axis=0)
        inner = nt(both, stored)
        back = nn(both, s)
        yield
        scaled = decay * dots
        dlow = jnp.where(rows > cols, -inner[:size], 0.0)
        dp = jnp.where(rows >= cols, inner[size:], 0.0)
        dv = beta * dr
        spread = dlow * (beta * scaled) + dp * p_i[:, ps].astype(f32)
        dqk = (dp * decay).astype(bf16)
        dkk = dlow * (beta * decay)
        left = jnp.concatenate([dqk, (dkk + dkk.T).astype(bf16)], axis=0)
        on_k = nn(left, kl)
        on_q = tn(dqk, ql)
        yield
        dq = on_k[:size] + eg * back[size:]
        tail_part = row_sum(dkt * kt)
        dk = on_k[size:] + on_q - (beta * eg) * back[:size] + jnp.exp(last - g) * dkt
        dbeta = row_sum(dr * (v - eg * k_s)) + row_sum(dlow * scaled)
        dg = row_sum(spread) - row_sum(spread.T) - tail_part
        dg = dg + eg * row_sum(do.astype(f32) * q_s) - (beta * eg) * row_sum(dr * k_s)
        carry = col_sum(row_sum(s.astype(f32) * ds.astype(f32)))
        at_end = col_sum(tail_part) + jnp.exp(last) * carry
        dg = dg + jnp.where(end_row, at_end, 0.0)
        dcums[h] = jnp.where(lane == heads + h, dg, 0.0)
        dbetas[h] = jnp.where(lane == h, dbeta, 0.0)
        yield
        qh = jax.nn.silu(conv_pre(ext, kq, 0, ks, size, margin))
        rq = lax.rsqrt(row_sum(qh * qh) + EPS)
        unit = qh * rq
        dqn = dq * key_dim**-0.5
        conv_back(rq * (dqn - unit * row_sum(dqn * unit)), kq, 0, ks.start, ks.stop)
        kh = jax.nn.silu(conv_pre(ext, kk, kc, slice(kc + ks.start, kc + ks.stop), size, margin))
        rk = lax.rsqrt(row_sum(kh * kh) + EPS)
        conv_back(rk * (dk - k * row_sum(dk * k)), kk, kc, kc + ks.start, kc + ks.stop)
        conv_back(dv, kv, 2 * kc, 2 * kc + vs.start, 2 * kc + vs.stop)

    in_step(one(h) for h in range(heads))
    dcum, dbeta_all = sum(dcums[1:], dcums[0]), sum(dbetas[1:], dbetas[0])
    triu = jnp.where(rows <= cols, 1.0, 0.0).astype(f32)
    dlog = exact(triu, dcum)
    dalpha = dlog * (-jnp.exp(rate)) * jax.nn.sigmoid(sm + bias)
    dsmall = dalpha + dbeta_all * beta_all * (1.0 - beta_all)
    taps = (margin + 1) * blocks
    flat[taps : taps + 1, :] = col_sum(dlog * log_decay)
    flat[taps + 1 : taps + 2, :] = col_sum(dalpha)
    dog = dog_mine[...] + dog_other[...]
    for c in range(value_dim // LANES):
        flat[taps + 2 + c : taps + 3 + c, :] = dog[:, c * LANES : (c + 1) * LANES]
    x = xs[...].astype(f32)
    scale = lax.rsqrt(jnp.mean(x * x, axis=-1, keepdims=True) + EPS)
    hx = halo[...].astype(f32)
    hscale = lax.rsqrt(jnp.mean(hx * hx, axis=-1, keepdims=True) + EPS)
    peers = send_o.shape[0]
    qn, vn = kc // peers, vc // peers
    acc = None
    for ref, kern, lo, hi, n, at in (
        (wq, kq, 0, kc, qn, 0), (wk, kk, kc, 2 * kc, qn, qn), (wv, kv, 2 * kc, proj, vn, 2 * qn),
    ):
        dext = None
        for j in range(margin + 1):
            term = kern[j : j + 1, :] * pad[pl.ds(margin - j, total), lo:hi]
            dext = term if dext is None else dext + term
        part = nt(dext, ref[...])
        acc = part if acc is None else acc + part
        own = (dext[HALO:] * scale).T.astype(bf16)
        rim = (dext[:HALO] * hscale).astype(bf16)
        for e in range(peers):
            send_o[e, at : at + n, :] = own[e * n : (e + 1) * n]
            send_o[e, 2 * qn + vn : 2 * qn + vn + HALO, at : at + n] = rim[:, e * n : (e + 1) * n]
    dgate = dgate_i[...]
    fl = flat[...].astype(bf16)
    for e in range(peers):
        send_o[e, 2 * qn + vn + HALO :, :] = fl[e * HALO : (e + 1) * HALO]
    dsl = dsmall.astype(bf16)
    wsmall_o[...] = tn(dsl, normed[HALO:, :])[: wsmall_o.shape[0]]
    part_o[:HALO, :] = acc[:HALO].astype(bf16)
    part_o[HALO:, :] = (acc[HALO:] + nt(dgate, wg[...]) + nn(dsl, wsm[...])).astype(bf16)


def finish_body(heads, xs, gain, part, part_other, rim, rim_other, gres, wsmall, dfg, input_o, tail_o):
    size = xs.shape[0]
    x = xs[...].astype(f32)
    scale = lax.rsqrt(jnp.mean(x * x, axis=-1, keepdims=True) + EPS)
    normal = x * scale
    g = part[HALO:, :].astype(f32) + part_other[HALO:, :].astype(f32)
    edge = rim[...].astype(f32) + rim_other[...].astype(f32)
    g = jnp.concatenate([g[: size - HALO], g[size - HALO :] + edge], axis=0)
    tail_o[...] = jnp.zeros(tail_o.shape, f32)
    tail_o[: 2 * heads, :] = wsmall[: 2 * heads, :]
    tail_o[2 * heads : 2 * heads + 1, :] = col_sum(g * normal)
    tail_o[2 * heads + 1 : 2 * heads + 2, :] = dfg[...]
    d = g * gain[...]
    input_o[...] = gres[...] + scale * (d - normal * jnp.mean(d * normal, axis=-1, keepdims=True))


def gather_body(split_at, pieces, recv, gates, *refs):
    parts = refs[:pieces]
    gain, tail, which, send_o, lhs = refs[pieces:]
    peers, _, size = recv.shape
    mixed = recv.shape[1] - 2 * HALO
    n = mixed + split_at
    width = gain.shape[1]
    rows = width // peers
    flat = jnp.zeros((HALO, LANES), f32)
    edge = []
    for j in range(peers):
        cols = slice(j * size, (j + 1) * size)
        lhs[:mixed, cols] = recv[j, :mixed, :]
        lhs[mixed:, cols] = gates[j, split_at:, :]
        edge.append(recv[j, mixed : mixed + HALO, :])
        flat = flat + recv[j, mixed + HALO :, :].astype(f32)
    edge = jnp.concatenate(edge, axis=0)
    products, extras = [], []
    for xg in parts:
        none = jnp.zeros((HALO, xg.shape[1]), bf16)
        near = [xg[j * size - HALO : j * size, :] if j else none for j in range(peers)]
        products.append(nn(lhs[...], xg[...]))
        extras.append(tn(edge, jnp.concatenate(near, axis=0)))
    if pieces == 2:
        first = which[0:1, 0:1] == 0
        products = [jnp.where(first, *products), jnp.where(first, *products[::-1])]
        extras = [jnp.where(first, *extras), jnp.where(first, *extras[::-1])]
    acc = jnp.concatenate(products, axis=1)
    extra = jnp.concatenate(extras, axis=1)
    top = (acc[:mixed] + extra[:mixed]) * gain[...]
    rest = acc[mixed:] * gain[...]
    half = rows // 2
    wide = mixed == LANES
    if wide:
        top, rest = top.T.astype(bf16), rest.T.astype(bf16)
    else:
        fill = jnp.zeros((LANES - n, width), f32)
        top, half = jnp.concatenate([top, rest, fill], axis=0).T.astype(bf16), 0
    fl = flat.astype(bf16)
    small = tail[...].astype(bf16)
    for e in range(peers):
        lo = e * rows
        block = lo // LANES * LANES
        send_o[e, :rows, :] = top[lo : lo + rows]
        if wide:
            send_o[e, rows : rows + half, :] = jnp.concatenate(
                [rest[lo : lo + half], rest[lo + half : lo + rows]], axis=1
            )
        send_o[e, rows + half : rows + half + 2 * HALO, :] = small[:, block : block + LANES]
        send_o[e, rows + half + 2 * HALO :, :] = fl


def scatter_body(heads, qn, vn, margin, recv, side, q_o, k_o, v_o, g_o, wb_o, wa_o, ag_o, fg_o, cq_o, ck_o, cv_o, rate_o, bias_o, og_o):
    peers = recv.shape[0]
    rows = q_o.shape[0]
    wide = 2 * qn + vn == LANES
    half = rows // 2 if wide else 0
    low = jnp.zeros((2 * HALO, LANES), f32)
    lines = []
    for e in range(peers):
        top = recv[e, :rows, :].astype(f32)
        q_o[:, e * qn : (e + 1) * qn] = top[:, :qn]
        k_o[:, e * qn : (e + 1) * qn] = top[:, qn : 2 * qn]
        v_o[:, e * vn : (e + 1) * vn] = top[:, 2 * qn : 2 * qn + vn]
        if wide:
            rest = recv[e, rows : rows + half, :].astype(f32)
            g_o[:half, e * vn : (e + 1) * vn] = rest[:, :vn]
            g_o[half:, e * vn : (e + 1) * vn] = rest[:, vn:]
        else:
            g_o[:, e * vn : (e + 1) * vn] = top[:, 2 * qn + vn : 2 * (qn + vn)]
        low = low + recv[e, rows + half : rows + half + 2 * HALO, :].astype(f32)
        lines.append(recv[e, rows + half + 2 * HALO :, :].astype(f32))
    picked = low[:, :rows]
    for s in range(1, LANES // rows):
        picked = jnp.where(side[0:1, 0:1] == s, low[:, s * rows : (s + 1) * rows], picked)
    wb_o[...] = picked[:heads]
    wa_o[...] = picked[heads : 2 * heads]
    ag_o[...] = picked[2 * heads : 2 * heads + 1]
    fg_o[...] = picked[2 * heads + 1 : 2 * heads + 2]

    def line(at):
        return lines[at // HALO][at % HALO : at % HALO + 1]

    kb, vb = cq_o.shape[1] // LANES, cv_o.shape[1] // LANES
    blocks = 2 * kb + vb
    for j in range(margin + 1):
        for c in range(blocks):
            at = j * blocks + c
            ref, to = (cq_o, c) if c < kb else (ck_o, c - kb) if c < 2 * kb else (cv_o, c - 2 * kb)
            ref[j : j + 1, to * LANES : (to + 1) * LANES] = line(at)
    at = (margin + 1) * blocks
    rate_o[...] = line(at)[:, heads : 2 * heads]
    bias_o[...] = line(at + 1)[:, heads : 2 * heads]
    for c in range(og_o.shape[1] // LANES):
        og_o[:, c * LANES : (c + 1) * LANES] = line(at + 2 + c)


def ffn_grads_body(inputs, gg, gu, og, hid, out, buf, sems):
    width = inputs.shape[1]
    ff = gg.shape[1]
    step = buf.shape[2] // 3
    copies = []
    for i in range(width // LANES):
        slot = i % 2
        cols = slice(i * LANES, (i + 1) * LANES)
        if i >= 2:
            copies[i - 2].wait()
        lhs = inputs[:, cols]
        buf[slot, :, :ff] = tn(lhs, gg[...]).astype(bf16)
        buf[slot, :, step : step + ff] = tn(lhs, gu[...]).astype(bf16)
        buf[slot, :, 2 * step : 2 * step + ff] = tn(og[:, cols], hid[...]).astype(bf16)
        copy = pltpu.make_async_copy(buf.at[slot], out.at[cols, pl.ds(0, 3 * step)], sems.at[slot])
        copy.start()
        copies.append(copy)
    for copy in copies[-2:]:
        copy.wait()


def shift_along(block, axis, distance):
    devices = range(lax.axis_size(axis))
    route = [(i - distance, i) for i in devices if i - distance in devices]
    return lax.ppermute(block, axis, route)


def pair(part):
    if lax.axis_size("tensor") == 2:
        return part, lax.ppermute(part, "tensor", [(0, 1), (1, 0)])
    return lax.psum(part, "tensor"), jnp.zeros_like(part)


def swap(blocks):
    return lax.all_to_all(blocks, "dp", 0, 0, tiled=True)


def on_device(
    block_input, output_grad, attn_gain, w_query, w_key, w_value, conv_query, conv_key, conv_value,
    w_beta, w_alpha, a_log, dt_bias, w_gate_out, out_gain, w_out, ffn_gain, w_gate, w_up, w_down,
):
    size, width = block_input.shape
    heads = a_log.shape[0]
    key_dim = w_query.shape[1] // heads
    value_dim = w_value.shape[1] // heads
    margin = conv_query.shape[0] - 1
    peers = lax.axis_size("dp")
    slices = peers // heads
    kc, vc, gc, ff = w_query.shape[1], w_value.shape[1], w_gate_out.shape[1], w_gate.shape[1]
    proj = 2 * kc + vc
    dims = (heads, key_dim, value_dim)
    rows = width // peers

    halo = shift_along(block_input[-HALO:], "dp", 1)
    rate, bias = a_log[None], dt_bias[None]
    again, fgain, ogain = attn_gain[None], ffn_gain[None], out_gain[None]

    normed, ext, gate_pre, small, cum, q, k, v, inv, p, w, u, wsm, send = call(
        functools.partial(front_body, *dims, margin, slices),
        [
            ((size + HALO, width), bf16), ((size + HALO, proj), bf16), ((size, gc), f32),
            ((size, LANES), f32), ((size, LANES), f32), ((size, kc), f32), ((size, kc), f32), ((size, vc), f32),
            ((size, heads * size), bf16), ((size, heads * size), bf16), ((size, kc), bf16),
            ((size, vc), f32), ((LANES, width), bf16),
            ((peers, key_dim + value_dim // slices, key_dim), bf16),
        ],
        block_input, halo, again, w_query, w_key, w_value, w_gate_out, w_beta.T, w_alpha.T,
        conv_query, conv_key, conv_value, rate, bias,
        scratch=[pltpu.VMEM((size + HALO, proj), f32)],
    )
    maps = swap(send)
    maps, late_input = lax.optimization_barrier((maps, block_input))
    paired = lax.axis_size("tensor") == 2
    if paired:
        half = width // 2
        late_input = lax.dynamic_slice_in_dim(late_input, lax.axis_index("tensor") * half, half, 1)
    everyone = lax.all_gather(late_input, "dp", axis=0, tiled=True)
    piece = (peers, value_dim // slices, key_dim)
    (entry,) = call(functools.partial(scan_fwd_body, key_dim), [(piece, bf16)], maps)
    st = swap(entry).reshape(heads, value_dim, key_dim)
    stored, mixed, gated, mix_part = call(
        functools.partial(mix_body, *dims),
        [((size, vc), bf16), ((size, vc), f32), ((size, vc), bf16), ((size, width), bf16)],
        st, u, w, p, q, cum, gate_pre, ogain, w_out,
    )
    mix_part, late_grad = lax.optimization_barrier((mix_part, output_grad))
    mix_pair = pair(mix_part)
    (grad_hidden,) = call(hidden_body, [((size, ff), bf16)], late_grad, w_down, near=True)
    ffn_input, hidden, gga, gua, back_part, down_part = call(
        ffn_body,
        [((size, width), bf16), ((size, ff), bf16), ((size, ff), bf16), ((size, ff), bf16),
         ((size, width), bf16), ((size, width), bf16)],
        block_input, *mix_pair, fgain, w_gate, w_up, w_down, grad_hidden, near=True, home=(4, 5),
    )
    back_pair = pair(back_part)
    step = -(-ff // LANES) * LANES
    total = 3 * step + gc
    (early,) = call(
        ffn_grads_body, [((width, total), bf16)], ffn_input, gga, gua, output_grad, hidden,
        scratch=[pltpu.VMEM((2, LANES, 3 * step), bf16), pltpu.SemaphoreType.DMA((2,))],
        raw=(("out", 0),), home=(0,), near=True,
    )
    back_pair, early = lax.optimization_barrier((back_pair, early))
    gres, dfg, dmix, pdo, dgate, dog, send_back, early = call(
        functools.partial(turn_body, *dims, slices),
        [((size, width), f32), ((1, width), f32), ((size, vc), bf16), ((size, vc), f32),
         ((size, gc), bf16), ((1, value_dim), f32),
         ((peers, 2 * piece[1], key_dim), bf16), ((width, total), bf16)],
        block_input, *mix_pair, *back_pair, output_grad, fgain, w_out, gated, mixed, gate_pre, ogain, p, w, q, cum,
        early,
        scratch=[pltpu.VMEM((width, gc), bf16), pltpu.SemaphoreType.DMA((1,))], raw=(16,), alias={16: 7}, near=True, home=range(7),
    )
    send_back, early, everyone = lax.optimization_barrier((send_back, early, everyone))
    dog_pair = pair(dog)
    dog_pair, everyone = lax.optimization_barrier((dog_pair, everyone))
    pieces = pair(everyone) if paired else (everyone,)
    first = lax.psum_scatter(early, "dp", scatter_dimension=0, tiled=True).astype(f32)
    local = swap(send_back)
    (exits,) = call(functools.partial(scan_bwd_body, key_dim), [(piece, bf16)], maps, local)
    dst = swap(exits).reshape(heads, value_dim, key_dim)
    down_pair = pair(down_part)

    qn, vn = kc // peers, vc // peers
    share = 2 * (qn + vn)
    send, part, wsmall = call(
        functools.partial(back_body, *dims, margin),
        [((peers, share - vn + 2 * HALO, size), bf16), ((size + HALO, width), bf16), ((2 * HALO, width), f32)],
        dst, st, block_input, halo, normed, ext, conv_query, conv_key, conv_value,
        q, k, v, inv, p, stored, dmix, pdo, dgate,
        small, cum, rate, bias, *dog_pair, w_query, w_key, w_value, w_gate_out, wsm,
        scratch=[
            pltpu.VMEM((size + HALO, proj), f32), pltpu.VMEM((size + 2 * HALO, proj), f32),
            pltpu.VMEM((peers * HALO, LANES), f32),
        ],
    )
    rim_pair = pair(shift_along(part[:HALO], "dp", -1))
    part_pair = pair(part)
    recv = swap(send)
    input_grad, tail = call(
        functools.partial(finish_body, heads),
        [((size, width), f32), ((2 * HALO, width), f32)],
        block_input, again, *part_pair, *rim_pair, gres, wsmall, dfg,
    )
    wide = 2 * qn + vn == LANES
    packed = rows + (rows // 2 if wide else 0) + 3 * HALO
    (send,) = call(
        functools.partial(gather_body, vn, len(pieces)), [((peers, packed, LANES), bf16)],
        recv, local, *pieces, again, tail, jnp.full((1, 1), lax.axis_index("tensor"), jnp.int32),
        scratch=[pltpu.VMEM((share, peers * size), bf16)],
    )
    recv = swap(send)
    side = jnp.full((1, 1), lax.axis_index("dp") % (LANES // rows), jnp.int32)
    gq, gk, gv, gg, gwb, gwa, gag, gfg, gcq, gck, gcv, grate, gbias, gog = call(
        functools.partial(scatter_body, heads, qn, vn, margin),
        [((rows, kc), f32), ((rows, kc), f32), ((rows, vc), f32), ((rows, gc), f32),
         ((heads, rows), f32), ((heads, rows), f32), ((1, rows), f32), ((1, rows), f32),
         ((margin + 1, kc), f32), ((margin + 1, kc), f32), ((margin + 1, vc), f32),
         ((1, heads), f32), ((1, heads), f32), ((1, value_dim), f32)],
        recv, side,
    )
    block_output = (
        block_input.astype(f32) + (mix_pair[0].astype(f32) + mix_pair[1].astype(f32))
        + (down_pair[0].astype(f32) + down_pair[1].astype(f32))
    )
    return (
        block_output, input_grad, gag[0], gq, gk, gv, gcq, gck, gcv, gwb.T, gwa.T,
        grate[0], gbias[0], gg, gog[0],
        first[:, 3 * step :].T, gfg[0], first[:, :ff], first[:, step : step + ff], first[:, 2 * step : 2 * step + ff].T,
    )


def solution(mesh):
    rows, cols, whole = P("dp", None), P(None, "tensor"), P()
    heads, high = P("tensor"), P("tensor", None)
    in_specs = (
        rows, rows, whole, cols, cols, cols, cols, cols, cols, cols, cols, heads, heads,
        cols, whole, high, whole, cols, cols, high,
    )
    both, crossed, dp = P("dp", "tensor"), P("tensor", "dp"), P("dp")
    out_specs = (
        rows, rows, dp, both, both, both, cols, cols, cols, both, both, heads, heads,
        both, whole, crossed, dp, both, both, crossed,
    )
    return jax.shard_map(
        on_device, mesh=mesh, in_specs=in_specs, out_specs=out_specs, check_vma=False
    )
```
